512 devices in a mesh: py: 16 (over x, z_lo, core), px: 32 (over y, z_hi).
Axes of the slice: x: 4, y: 8, z: 8 (z_hi: 4, z_lo: 2; z = z_hi * 2 + z_lo), core: 2. Of those that a mesh axis runs over, the one named last changes fastest.
Arguments:
- forcing: float32 [1024, 32, 1024], P('px', 'py')
- inv_density: float32 [1024, 32, 1024], P('px', 'py'), may hold values from 0.5 to 4
- stretch_x: float32 [1024], P('px'), may hold values from 0.5 to 2
- stretch_y: float32 [32], P('py'), may hold values from 0.5 to 2
- stretch_z: float32 [1024], replicated, may hold values from 0.5 to 2
- lines_z0: float32 [4, 256, 256], replicated
- lines_x0: float32 [4, 256, 256], replicated
- lines_z1: float32 [2, 256, 256], replicated
- lines_x1: float32 [2, 256, 256], replicated
- coarse_inverse: float32 [512, 512], P(('py', 'px')), as said below
Outputs:
- pressure_adjoint: float32 [1024, 32, 1024], P('px', 'py')
The draws below stay inside these ranges and needn't reach their ends.
Inputs may be any that keep to these rules, and one draw needn't show every extreme that they name: coarse_inverse is symmetric.
All inputs are finite; a program needn't handle non-finite values.
Results may differ from the reference program's by a relative error of at most 0.0001.
Values sent between devices are 32-bit elements; how exact they have to be, the bound alone decides.
No kernel may reach another device: no remote copies, remote signals or barrier semaphores. Data moves between devices by JAX's collectives and lax.ppermute only.
A program may use at most 64 MiB of HBM per device.

```python
import math
import jax
import jax.numpy as jnp
from jax import lax

NX = 1024
NZ = 1024
B = 256
CYCLES = 1
NY = 32
COARSE = 512
N_PY = 16
N_PX = 32


def block_lines(key, count):
    first_key, second_key = jax.random.split(key)
    diag_part = jax.random.uniform(first_key, (count, B, B), jnp.float32, 0.45, 0.65)
    off_part = 0.12 * jax.random.normal(second_key, (count, B, B), jnp.float32) / math.sqrt(B)
    unit = jnp.eye(B, dtype=jnp.float32)
    return unit * diag_part + (1.0 - unit) * off_part


def draw_lines_z0(key, part):
    return block_lines(jax.random.fold_in(key, 11), NZ // B)


def draw_lines_x0(key, part):
    return block_lines(jax.random.fold_in(key, 12), NX // B)


def draw_lines_z1(key, part):
    return block_lines(jax.random.fold_in(key, 13), NZ // 2 // B)


def draw_lines_x1(key, part):
    return block_lines(jax.random.fold_in(key, 14), NX // 2 // B)


def draw_coarse_inverse(key, part):
    first_key, second_key = jax.random.split(jax.random.fold_in(key, 21))
    diag_part = jax.random.uniform(first_key, (COARSE, COARSE), jnp.float32, 1.0, 2.0)
    noise = jax.random.normal(second_key, (COARSE, COARSE), jnp.float32)
    mirrored = (noise + noise.T) * (0.35 / math.sqrt(COARSE))
    unit = jnp.eye(COARSE, dtype=jnp.float32)
    return unit * diag_part + (1.0 - unit) * mirrored


def draw_forcing(key, part):
    first_key, second_key = jax.random.split(jax.random.fold_in(key, 31))
    phases = jax.random.uniform(second_key, (3,), jnp.float32, 0.0, 2.0 * math.pi)
    along_x = (jnp.arange(NX, dtype=jnp.float32) + 0.5) / NX
    along_y = (jnp.arange(NY, dtype=jnp.float32) + 0.5) / NY
    along_z = (jnp.arange(NZ, dtype=jnp.float32) + 0.5) / NZ
    smooth = 1.2 * jnp.sin(2.0 * math.pi * along_x + phases[0])[:, None, None] * jnp.cos(2.0 * math.pi * along_y + phases[1])[None, :, None] * jnp.cos(math.pi * along_z + phases[2])[None, None, :]
    rough = jax.random.normal(first_key, (NX, NY, NZ), jnp.float32)
    return rough + smooth


def block_scale(key, dims, cuts, low, largest):
    loudness = 1.0
    for axis_at, parts in cuts:
        steps = jax.random.uniform(jax.random.fold_in(jax.random.fold_in(key, 6), axis_at), (parts,), jnp.float32, low / len(cuts), largest / len(cuts))
        loudness = loudness * jnp.repeat(jnp.exp(steps), dims[axis_at] // parts).reshape((-1,) + (1,) * (len(dims) - 1 - axis_at))
    return loudness


def setup_inputs(seed: int = 0) -> dict:
    splits = jax.random.split(jax.random.key(seed), 11)
    return {
        "forcing": draw_forcing(jax.random.fold_in(splits[10], 71), 0),
        "inv_density": jnp.clip(jnp.exp(math.log(4.0) - 2.0794415 * jax.random.uniform(splits[1], (NX, NY, NZ), jnp.float32) ** block_scale(splits[1], (NX, NY, NZ), ((0, 32), (1, 16)), -0.2, 0.2)), 0.5, 4.0),
        "stretch_x": jnp.clip(jnp.exp(math.log(2.0) - 1.3862944 * jax.random.uniform(splits[2], (NX,), jnp.float32) ** block_scale(splits[2], (NX,), ((0, 32),), -0.2, 0.2)), 0.5, 2.0),
        "stretch_y": jnp.clip(jnp.exp(math.log(2.0) - 1.3862944 * jax.random.uniform(splits[3], (NY,), jnp.float32) ** block_scale(splits[3], (NY,), ((0, 16),), -0.2, 0.2)), 0.5, 2.0),
        "stretch_z": jnp.clip(jnp.exp(jax.random.uniform(splits[4], (NZ,), jnp.float32, math.log(0.5), math.log(2.0))), 0.5, 2.0),
        "lines_z0": draw_lines_z0(jax.random.fold_in(splits[10], 71), 0),
        "lines_x0": draw_lines_x0(jax.random.fold_in(splits[10], 71), 0),
        "lines_z1": draw_lines_z1(jax.random.fold_in(splits[10], 71), 0),
        "lines_x1": draw_lines_x1(jax.random.fold_in(splits[10], 71), 0),
        "coarse_inverse": draw_coarse_inverse(jax.random.fold_in(splits[10], 71), 0),
    }


shift_term = 0.1
highest = lax.Precision.HIGHEST


def pad_axis(field, axis):
    widths = [(0, 0), (0, 0), (0, 0)]
    widths[axis] = (1, 1)
    return jnp.pad(field, widths)


def beside_sum(padded, axis):
    length = padded.shape[axis] - 2
    return lax.slice_in_dim(padded, 2, length + 2, axis=axis) + lax.slice_in_dim(padded, 0, length, axis=axis)


def operate(field, level):
    density, coef_x, coef_y, coef_z = level[0], level[1], level[2], level[3]
    twice = 2.0 * field
    near_x = beside_sum(pad_axis(field, 0), 0)
    near_y = beside_sum(pad_axis(field, 1), 1)
    near_z = beside_sum(pad_axis(field, 2), 2)
    stencil = coef_x[:, None, None] * (twice - near_x) + coef_y[None, :, None] * (twice - near_y) + coef_z[None, None, :] * (twice - near_z)
    return shift_term * field + density * stencil


def diagonal(density, coef_x, coef_y, coef_z):
    return shift_term + 2.0 * density * (coef_x[:, None, None] + coef_y[None, :, None] + coef_z[None, None, :])


def lines_along_z(field, blocks):
    first, second, third = field.shape
    count = blocks.shape[0]
    grouped = field.reshape(first * second, count, third // count)
    return jnp.einsum('nkb,kcb->nkc', grouped, blocks, precision=highest).reshape(first, second, third)


def lines_along_x(field, blocks):
    first, second, third = field.shape
    count = blocks.shape[0]
    grouped = field.reshape(count, first // count, second * third)
    return jnp.einsum('kcb,kbn->kcn', blocks, grouped, precision=highest).reshape(first, second, third)


def sweep(iterate, rhs, level):
    residual = rhs - operate(iterate, level)
    iterate = iterate + lines_along_z(residual / level[4], level[5])
    residual = rhs - operate(iterate, level)
    return iterate + lines_along_x(residual / level[4], level[6])


def restrict_padded(padded, axis):
    length = padded.shape[axis] - 2

    def take(start):
        return lax.slice_in_dim(padded, start, start + length - 1, stride=2, axis=axis)

    return (take(0) + 3.0 * take(1) + 3.0 * take(2) + take(3)) * 0.125


def prolong_padded(padded, axis):
    length = padded.shape[axis] - 2
    lower = lax.slice_in_dim(padded, 0, length, axis=axis)
    middle = lax.slice_in_dim(padded, 1, length + 1, axis=axis)
    upper = lax.slice_in_dim(padded, 2, length + 2, axis=axis)
    even = (3.0 * middle + lower) * 0.25
    odd = (3.0 * middle + upper) * 0.25
    stacked = jnp.stack([even, odd], axis=axis + 1)
    shape = list(even.shape)
    shape[axis] = 2 * length
    return stacked.reshape(shape)


def halve(vector):
    return vector.reshape(-1, 2).sum(axis=1) * 0.125


def coarsen(density, coef_x, coef_y, coef_z):
    first, second, third = density.shape
    dense_one = density.reshape(first // 2, 2, second // 2, 2, third // 2, 2).mean(axis=(1, 3, 5))
    return dense_one, halve(coef_x), halve(coef_y), halve(coef_z)


def reference(forcing, inv_density, stretch_x, stretch_y, stretch_z, lines_z0, lines_x0, lines_z1, lines_x1, coarse_inverse):
    fine = (inv_density, stretch_x, stretch_y, stretch_z, diagonal(inv_density, stretch_x, stretch_y, stretch_z), lines_z0, lines_x0)
    dense_one, coef_x1, coef_y1, coef_z1 = coarsen(inv_density, stretch_x, stretch_y, stretch_z)
    middle = (dense_one, coef_x1, coef_y1, coef_z1, diagonal(dense_one, coef_x1, coef_y1, coef_z1), lines_z1, lines_x1)
    iterate = jnp.zeros_like(forcing)
    for cycle in range(CYCLES):
        iterate = sweep(iterate, forcing, fine)
        residual = forcing - operate(iterate, fine)
        right_one = restrict_padded(pad_axis(residual, 0), 0)
        right_one = restrict_padded(pad_axis(right_one, 1), 1)
        right_one = restrict_padded(pad_axis(right_one, 2), 2)
        level_one = sweep(jnp.zeros_like(right_one), right_one, middle)
        residual_one = right_one - operate(level_one, middle)
        size_x, size_y, size_z = residual_one.shape
        means = residual_one.reshape(N_PX, size_x // N_PX, N_PY, size_y // N_PY, size_z).mean(axis=(1, 3, 4))
        values = means.T.reshape(-1)
        correction = jnp.dot(coarse_inverse, values, precision=highest)
        spread = correction.reshape(N_PY, N_PX).T
        spread = jnp.repeat(jnp.repeat(spread, size_x // N_PX, axis=0), size_y // N_PY, axis=1)
        level_one = level_one + spread[:, :, None]
        level_one = sweep(level_one, right_one, middle)
        raised = prolong_padded(pad_axis(level_one, 0), 0)
        raised = prolong_padded(pad_axis(raised, 1), 1)
        raised = prolong_padded(pad_axis(raised, 2), 2)
        iterate = iterate + raised
        iterate = sweep(iterate, forcing, fine)
    return iterate
```

```python
import functools

import jax
import jax.numpy as jnp
from jax import lax
from jax.experimental import pallas as pl
from jax.experimental.pallas import tpu as pltpu
from jax.sharding import PartitionSpec as P

shift_term = 0.1
highest = lax.Precision.HIGHEST
f32 = jnp.float32

N_PY, N_PX = 16, 32
FX, FZ = 32, 1024
MX, MZ = 16, 512
FH, MH = 8, 4
FE, ME = FX + 2 * FH, MX + 2 * MH


def roll(v, shift, axis):
    return pltpu.roll(v, shift % v.shape[axis], axis)


def dyn(ref, start, size):
    return ref[pl.ds(pl.multiple_of(start, 8), size), :]


def dot(a, b):
    return jnp.dot(a, b, precision=highest, preferred_element_type=f32)


def dot_nt(a, b):
    return lax.dot_general(
        a, b, (((1,), (1,)), ((), ())), precision=highest, preferred_element_type=f32
    )


def iota(shape, axis):
    return lax.broadcasted_iota(jnp.int32, shape, axis)


def near_z(v):
    lane = iota(v.shape, 1)
    last = v.shape[1] - 1
    below = jnp.where(lane == 0, 0.0, roll(v, 1, 1))
    above = jnp.where(lane == last, 0.0, roll(v, -1, 1))
    return below + above


def near_x(v):
    return roll(v, 1, 0) + roll(v, -1, 0)


def operate(v, v_near_x, v_near_y, rho, cx, cy, cz):
    twice = 2.0 * v
    stencil = cx * (twice - v_near_x) + cy * (twice - v_near_y) + cz * (twice - near_z(v))
    return shift_term * v + rho * stencil


def diagonal(rho, cx, cy, cz):
    return shift_term + 2.0 * rho * (cx + cy + cz)


def solve_z(w, blocks):
    count = blocks.shape[0]
    size = blocks.shape[1]
    parts = [dot_nt(w[:, k * size : (k + 1) * size], blocks[k]) for k in range(count)]
    return jnp.concatenate(parts, axis=1)


def pair_columns(v, scale):
    fine, coarse = iota((256, 128), 0), iota((256, 128), 1)
    pick = jnp.where(fine // 2 == coarse, scale, 0.0).astype(f32)
    return jnp.concatenate(
        [dot(v[:, 256 * k : 256 * (k + 1)], pick) for k in range(v.shape[1] // 256)], axis=1
    )


def even_columns(v, scale):
    fine, coarse = iota((256, 128), 0), iota((256, 128), 1)
    pick = jnp.where(fine == 2 * coarse, scale, 0.0).astype(f32)
    return jnp.concatenate(
        [dot(v[:, 256 * k : 256 * (k + 1)], pick) for k in range(v.shape[1] // 256)], axis=1
    )


def restrict_columns(v):
    lane = iota(v.shape, 1)
    last = v.shape[1] - 1
    one = jnp.where(lane == last, 0.0, roll(v, -1, 1))
    two = jnp.where(lane >= last - 1, 0.0, roll(v, -2, 1))
    below = jnp.where(lane == 0, 0.0, roll(v, 1, 1))
    return even_columns(below + 3.0 * v + 3.0 * one + two, 0.125)


def raise_columns(v):
    lane = iota(v.shape, 1)
    last = v.shape[1] - 1
    below = jnp.where(lane == 0, 0.0, roll(v, 1, 1))
    above = jnp.where(lane == last, 0.0, roll(v, -1, 1))
    even = 3.0 * v + below
    odd = 3.0 * v + above
    coarse, fine = iota((128, 256), 0), iota((128, 256), 1)
    at_even = jnp.where(fine == 2 * coarse, 0.25, 0.0).astype(f32)
    at_odd = jnp.where(fine == 2 * coarse + 1, 0.25, 0.0).astype(f32)
    parts = []
    for k in range(v.shape[1] // 128):
        cut = slice(128 * k, 128 * (k + 1))
        parts.append(dot(even[:, cut], at_even) + dot(odd[:, cut], at_odd))
    return jnp.concatenate(parts, axis=1)


def restrict_rows(v):
    coarse, fine = iota((ME, FE), 0), iota((ME, FE), 1)
    away = fine - 2 * coarse
    weight = jnp.where((away == 0) | (away == 1), 0.375, 0.0)
    weight = weight + jnp.where((away == -1) | (away == 2), 0.125, 0.0)
    return dot(weight.astype(f32), v)


def pair_rows(v):
    coarse, fine = iota((ME, FE), 0), iota((ME, FE), 1)
    return dot(jnp.where(fine // 2 == coarse, 1.0, 0.0).astype(f32), v)


def raise_rows(v):
    fine, coarse = iota((FE, ME), 0), iota((FE, ME), 1)
    away = fine - 2 * coarse
    weight = jnp.where((away == 0) | (away == 1), 0.75, 0.0)
    weight = weight + jnp.where((away == 2) | (away == -1), 0.25, 0.0)
    return dot(weight.astype(f32), v)


def inside_middle(px):
    row = iota((ME, MZ), 0) + MX * px - MH
    return (row >= 0) & (row < MX * N_PX)


def inside_fine(px):
    row = iota((FE, FZ), 0) + FX * px - FH
    return (row >= 0) & (row < FX * N_PX)


def to_slabs(plane, out, at):
    for m in range(8):
        out[m, at] = plane[:, 128 * m : 128 * (m + 1)]


def from_slabs(ref, at):
    return jnp.concatenate([ref[m, at] for m in range(8)], axis=1)


def pack_y(px, py, force, rho, cy, lower, upper):
    for at, out in ((0, lower), (1, upper)):
        out[0:32] = force[at]
        out[32:64] = rho[at]
        out[64:72] = cy[8 * at : 8 * at + 8]


def pack_x(px, py, force, rho, cx, below, above, low, high):
    for rows, out in ((slice(0, 8), low), (slice(24, 32), high)):
        shifted = slice(32 + rows.start, 32 + rows.stop)
        out[0:8] = below[rows]
        out[8:16] = force[0, rows]
        out[16:24] = force[1, rows]
        out[24:32] = above[rows]
        out[32:40] = below[shifted]
        out[40:48] = rho[0, rows]
        out[48:56] = rho[1, rows]
        out[56:64] = above[shifted]
        out[64:72] = jnp.concatenate([cx[rows]] * 8, axis=1)


def first_half(px, py, force, rho, cx, cy, cz, below, above, left, right, lines, f_ext, r_ext, cx_ext, cy_ext, u_own, slabs):
    columns = jnp.concatenate([left[64:72, 0:128], cx[...], right[64:72, 0:128]], axis=0)
    cx_ext[...] = columns
    cx_col = columns[:, 0:1]
    cy_rows = [below[64:65, :], None, None, above[64:65, :]]
    cy_rows[1] = jnp.concatenate([cy[0:1]] * 1, axis=1)
    cy_rows[2] = cy[8:9]
    cy_ext[...] = jnp.concatenate(cy_rows + [cy_rows[3]] * 4, axis=0)
    cz_row = cz[0:1]
    mids_f = [below[0:32], force[0], force[1], above[0:32]]
    mids_r = [below[32:64], rho[0], rho[1], above[32:64]]
    us = []
    fs = []
    rs = []
    for j in range(4):
        cut = slice(8 * j, 8 * j + 8)
        deep = slice(32 + 8 * j, 40 + 8 * j)
        f_full = jnp.concatenate([left[cut], mids_f[j], right[cut]], axis=0)
        r_full = jnp.concatenate([left[deep], mids_r[j], right[deep]], axis=0)
        f_ext[j] = f_full
        r_ext[j] = r_full
        fs.append(f_full)
        rs.append(r_full)
        us.append(solve_z(f_full / diagonal(r_full, cx_col, cy_rows[j], cz_row), lines))
    for j in (1, 2):
        own = us[j]
        applied = operate(own, near_x(own), us[j - 1] + us[j + 1], rs[j], cx_col, cy_rows[j], cz_row)
        scaled = (fs[j] - applied) / diagonal(rs[j], cx_col, cy_rows[j], cz_row)
        u_own[j - 1] = own[FH : FH + FX]
        to_slabs(scaled[FH : FH + FX], slabs, j - 1)


def solve_x_fine(px, py, slabs, lines, out):
    block = lines[0]
    for at in range(2):
        column = jnp.concatenate([slabs[m, at] for m in range(8)], axis=0)
        solved = dot(block, column)
        for m in range(8):
            out[m, at] = solved[32 * m : 32 * (m + 1)]


def add_slabs(px, py, u, slabs, out):
    for at in range(2):
        out[at] = u[at] + from_slabs(slabs, at)


def pack_u(px, py, u, below, above, low, high):
    for rows, out in ((slice(0, 8), low), (slice(24, 32), high)):
        for j, part in enumerate((below[0, rows], below[1, rows], u[0, rows], u[1, rows], above[0, rows], above[1, rows])):
            out[8 * j : 8 * j + 8] = part


def to_middle(px, py, u, below, above, left, right, f_ext, r_ext, cx_ext, cy_ext, cz, lines, u_ext, f_mid, v_out, r_mid, cx_mid, cyz_mid):
    mids = [below[0], below[1], u[0], u[1], above[0], above[1]]
    planes = []
    for j in range(6):
        cut = slice(8 * j, 8 * j + 8)
        planes.append(jnp.concatenate([left[cut], mids[j], right[cut]], axis=0))
    cx_col = cx_ext[:, 0:1]
    cz_row = cz[0:1]
    total = None
    for j in range(4):
        own = planes[j + 1]
        u_ext[j] = own
        applied = operate(own, near_x(own), planes[j] + planes[j + 2], r_ext[j], cx_col, cy_ext[j : j + 1], cz_row)
        left_over = f_ext[j] - applied
        if j in (1, 2):
            left_over = 3.0 * left_over
        total = left_over if total is None else total + left_over
    rhs = restrict_columns(restrict_rows(total * 0.125))
    rhs = jnp.where(inside_middle(px), rhs, 0.0)
    dense = pair_columns(pair_rows(r_ext[1] + r_ext[2]), 0.125)
    cxm = pair_rows(cx_ext[...]) * 0.125
    czm = pair_columns(cz[...], 0.125)
    cym = ((cy_ext[1:2] + cy_ext[2:3]) * 0.125)[:, 0:MZ]
    f_mid[...] = rhs
    r_mid[...] = dense
    cx_mid[...] = cxm
    cyz_mid[...] = jnp.concatenate([czm[0:1], cym, czm[2:8]], axis=0)
    diag = diagonal(dense, cxm[:, 0:1], cym, czm[0:1])
    v_out[...] = solve_z(rhs / diag, lines)


def middle_parts(r_mid, cx_mid, cyz_mid):
    return r_mid[...], cx_mid[:, 0:1], cyz_mid[1:2], cyz_mid[0:1]


def middle_scaled(px, py, v, below, above, f_mid, r_mid, cx_mid, cyz_mid, out):
    rho, cx, cy, cz = middle_parts(r_mid, cx_mid, cyz_mid)
    own = v[...]
    applied = operate(own, near_x(own), below[...] + above[...], rho, cx, cy, cz)
    scaled = (f_mid[...] - applied) / diagonal(rho, cx, cy, cz)
    part = roll(scaled, -MH, 0)[0:MX]
    for i in range(N_PX):
        out[i] = part


def solve_x_middle(px, py, gathered, lines, v, out):
    total = MX * N_PX
    pieces = []
    starts = (
        (jnp.maximum(MX * px - 8, 0), 8),
        (MX * px, MX),
        (jnp.minimum(MX * px + MX, total - 8), 8),
    )
    for start, size in starts:
        rows = dyn(lines, start, size)
        block = (start // 256) * 256
        pieces.append(dot(rows, dyn(gathered, block, 256)))
    full = jnp.concatenate(pieces, axis=0)
    part = roll(full, MH - 8, 0)[0:ME]
    out[...] = v[...] + jnp.where(inside_middle(px), part, 0.0)


def block_mean(px, py, v, below, above, f_mid, r_mid, cx_mid, cyz_mid, column, out):
    rho, cx, cy, cz = middle_parts(r_mid, cx_mid, cyz_mid)
    own = v[...]
    applied = operate(own, near_x(own), below[...] + above[...], rho, cx, cy, cz)
    row = iota((ME, MZ), 0)
    kept = jnp.where((row >= MH) & (row < MH + MX), f_mid[...] - applied, 0.0)
    mean = jnp.sum(jnp.sum(kept, axis=0, keepdims=True), axis=1, keepdims=True) * (1.0 / (MX * MZ))
    sent = column[...] * mean
    for i in range(N_PX):
        out[i] = jnp.broadcast_to(sent[i : i + 1], (8, 128))


def sum_x(px, py, parts, out):
    total = parts[0]
    for i in range(1, N_PX):
        total = total + parts[i]
    for j in range(N_PY):
        out[j] = total


def second_half(px, py, parts, v, below, above, f_mid, r_mid, cx_mid, cyz_mid, lines, out):
    total = parts[0]
    for j in range(1, N_PY):
        total = total + parts[j]
    lane = iota((8, 128), 1)
    row = iota((ME, MZ), 0)

    def raised(plane, dy):
        held = (py + dy >= 0) & (py + dy < N_PY)
        at = []
        for dx in range(3):
            wanted = (lane == dx * N_PY + py + dy) & held
            found = jnp.sum(jnp.where(wanted, total, 0.0), axis=1, keepdims=True)[0:1]
            at.append(found)
        return plane + jnp.where(row < MH, at[0], jnp.where(row < MH + MX, at[1], at[2]))

    own = raised(v[...], 0)
    beside = raised(below[...], -1) + raised(above[...], 1)
    rho, cx, cy, cz = middle_parts(r_mid, cx_mid, cyz_mid)
    applied = operate(own, near_x(own), beside, rho, cx, cy, cz)
    out[...] = own + solve_z((f_mid[...] - applied) / diagonal(rho, cx, cy, cz), lines)


def to_fine(px, py, v, below, above, u_ext, f_ext, r_ext, cx_ext, cy_ext, cz, lines, out, lower, upper):
    raised = [raise_columns(raise_rows(p[...])) * 0.25 for p in (below, v, above)]
    mids = [
        3.0 * raised[0] + raised[1],
        3.0 * raised[1] + raised[0],
        3.0 * raised[1] + raised[2],
        3.0 * raised[2] + raised[1],
    ]
    inside = inside_fine(px)
    us = []
    for j in range(4):
        held = inside
        if j == 0:
            held = inside & (py > 0)
        if j == 3:
            held = inside & (py < N_PY - 1)
        us.append(u_ext[j] + jnp.where(held, mids[j], 0.0))
    cx_col = cx_ext[:, 0:1]
    cz_row = cz[0:1]
    for j in (1, 2):
        own = us[j]
        cy_row = cy_ext[j : j + 1]
        rho = r_ext[j]
        applied = operate(own, near_x(own), us[j - 1] + us[j + 1], rho, cx_col, cy_row, cz_row)
        solved = own + solve_z((f_ext[j] - applied) / diagonal(rho, cx_col, cy_row, cz_row), lines)
        out[j - 1] = solved
        (lower if j == 1 else upper)[...] = solved[FH : FH + FX]


def last_scaled(px, py, u, below, above, f_ext, r_ext, cx_ext, cy_ext, cz, slabs):
    cx_col = cx_ext[FH : FH + FX, 0:1]
    cz_row = cz[0:1]
    inner = slice(FH, FH + FX)
    for at in range(2):
        full = u[at]
        beside_x = near_x(full)[inner]
        own = full[inner]
        beside_y = (below[...] if at == 0 else u[0, inner]) + (above[...] if at == 1 else u[1, inner])
        rho = r_ext[at + 1, inner]
        cy_row = cy_ext[at + 1 : at + 2]
        applied = operate(own, beside_x, beside_y, rho, cx_col, cy_row, cz_row)
        scaled = (f_ext[at + 1, inner] - applied) / diagonal(rho, cx_col, cy_row, cz_row)
        to_slabs(scaled, slabs, at)


def finish(px, py, u, slabs, out):
    for at in range(2):
        out[at] = u[at, FH : FH + FX] + from_slabs(slabs, at)


class Device:
    def run(self, stage, shapes, *args):
        def kernel(*refs):
            stage(lax.axis_index("px"), lax.axis_index("py"), *refs)

        whole = pl.BlockSpec(memory_space=pltpu.VMEM)
        outs = pl.pallas_call(
            kernel,
            out_shape=[jax.ShapeDtypeStruct(s, f32) for s in shapes],
            in_specs=[whole] * len(args),
            out_specs=[whole] * len(shapes),
            compiler_params=pltpu.CompilerParams(vmem_limit_bytes=56 * 1024 * 1024),
            name=stage.__name__,
        )(*args)
        return outs if len(shapes) > 1 else outs[0]

    def local(self, fn, *args):
        return fn(*args)

    def block_of(self, lines):
        at = lax.axis_index("px") // 8
        return lax.dynamic_slice_in_dim(lines, at, 1, axis=0)

    def beside(self, axis, low, high):
        n = lax.axis_size(axis)
        up = [(i, i + 1) for i in range(n - 1)]
        down = [(j, i) for i, j in up]
        return lax.ppermute(high, axis, up), lax.ppermute(low, axis, down)

    def swap(self, axis, array, group):
        n = lax.axis_size(axis)
        groups = None
        if group < n:
            groups = [list(range(k, k + group)) for k in range(0, n, group)]
        return lax.all_to_all(array, axis, 0, 0, axis_index_groups=groups, tiled=True)


def arrange_column(coarse):
    table = coarse.reshape(N_PY, N_PX).T
    none = jnp.zeros((1, N_PY), f32)
    before = jnp.concatenate([none, table[:-1]], axis=0)
    after = jnp.concatenate([table[1:], none], axis=0)
    return jnp.concatenate([before, table, after, jnp.zeros((N_PX, 128 - 3 * N_PY), f32)], axis=1)


def prepare(forcing, inv_density, stretch_x, stretch_y, stretch_z, coarse_inverse):
    force = forcing.transpose(1, 0, 2)
    rho = inv_density.transpose(1, 0, 2)
    cx = jnp.broadcast_to(stretch_x[:, None], (FX, 128))
    cy = jnp.repeat(jnp.broadcast_to(stretch_y[:, None], (2, FZ)), 8, axis=0)
    cz = jnp.broadcast_to(stretch_z[None], (8, FZ))
    return force, rho, cx, cy, cz, arrange_column(coarse_inverse)


def cycle(d, forcing, inv_density, stretch_x, stretch_y, stretch_z, lines_z0, lines_x0, lines_z1, lines_x1, coarse_inverse):
    force, rho, cx, cy, cz, column = d.local(
        prepare, forcing, inv_density, stretch_x, stretch_y, stretch_z, coarse_inverse
    )
    block = d.block_of(lines_x0)
    rows_x1 = d.local(lambda a: a.reshape(MX * N_PX, 256), lines_x1)
    plane, slab, wide = (72, FZ), (8, 2, FX, 128), (4, FE, FZ)

    lower, upper = d.run(pack_y, [plane] * 2, force, rho, cy)
    below, above = d.beside("py", lower, upper)
    low, high = d.run(pack_x, [plane] * 2, force, rho, cx, below, above)
    left, right = d.beside("px", low, high)
    f_ext, r_ext, cx_ext, cy_ext, u, slabs = d.run(
        first_half,
        [wide, wide, (FE, 128), (8, FZ), (2, FX, FZ), slab],
        force, rho, cx, cy, cz, below, above, left, right, lines_z0,
    )
    slabs = d.swap("px", slabs, 8)
    slabs = d.run(solve_x_fine, [slab], slabs, block)
    slabs = d.swap("px", slabs, 8)
    u = d.run(add_slabs, [(2, FX, FZ)], u, slabs)
    below, above = d.beside("py", u, u)
    low, high = d.run(pack_u, [(48, FZ)] * 2, u, below, above)
    left, right = d.beside("px", low, high)
    mid = (ME, MZ)
    u_ext, f_mid, v, r_mid, cx_mid, cyz_mid = d.run(
        to_middle,
        [wide, mid, mid, mid, (ME, 128), (8, MZ)],
        u, below, above, left, right, f_ext, r_ext, cx_ext, cy_ext, cz, lines_z1,
    )
    statics = (f_mid, r_mid, cx_mid, cyz_mid)

    below, above = d.beside("py", v, v)
    every = d.run(middle_scaled, [(N_PX, MX, MZ)], v, below, above, *statics)
    every = d.swap("px", every, N_PX)
    every = d.local(lambda a: a.reshape(MX * N_PX, MZ), every)
    v = d.run(solve_x_middle, [mid], every, rows_x1, v)
    below, above = d.beside("py", v, v)
    sent = d.run(block_mean, [(N_PX, 8, 128)], v, below, above, *statics, column)
    parts = d.swap("px", sent, N_PX)
    parts = d.run(sum_x, [(N_PY, 8, 128)], parts)
    parts = d.swap("py", parts, N_PY)
    v = d.run(second_half, [mid], parts, v, below, above, *statics, lines_z1)
    below, above = d.beside("py", v, v)
    every = d.run(middle_scaled, [(N_PX, MX, MZ)], v, below, above, *statics)
    every = d.swap("px", every, N_PX)
    every = d.local(lambda a: a.reshape(MX * N_PX, MZ), every)
    v = d.run(solve_x_middle, [mid], every, rows_x1, v)

    below, above = d.beside("py", v, v)
    u, lower, upper = d.run(
        to_fine,
        [(2, FE, FZ), (FX, FZ), (FX, FZ)],
        v, below, above, u_ext, f_ext, r_ext, cx_ext, cy_ext, cz, lines_z0,
    )
    below, above = d.beside("py", lower, upper)
    slabs = d.run(last_scaled, [slab], u, below, above, f_ext, r_ext, cx_ext, cy_ext, cz)
    slabs = d.swap("px", slabs, 8)
    slabs = d.run(solve_x_fine, [slab], slabs, block)
    slabs = d.swap("px", slabs, 8)
    u = d.run(finish, [(2, FX, FZ)], u, slabs)
    return d.local(lambda a: a.transpose(1, 0, 2), u)


def solution(mesh):
    placed = (
        P("px", "py", None),
        P("px", "py", None),
        P("px"),
        P("py"),
        P(),
        P(),
        P(),
        P(),
        P(),
        P(("py", "px"), None),
    )
    return jax.shard_map(
        functools.partial(cycle, Device()),
        mesh=mesh,
        in_specs=placed,
        out_specs=P("px", "py", None),
        check_vma=False,
    )
```

```python
import functools

import jax
import jax.numpy as jnp
from jax import lax
from jax.experimental import pallas as pl
from jax.experimental.pallas import tpu as pltpu
from jax.sharding import PartitionSpec as P

shift_term = 0.1
f32 = jnp.float32
bf16 = jnp.bfloat16

N_PY, N_PX = 16, 32
FX, FZ = 32, 1024
MX, MZ = 16, 512
FH, MH = 8, 4
FE, ME = FX + 2 * FH, MX + 2 * MH


def roll(v, shift, axis):
    return pltpu.roll(v, shift % v.shape[axis], axis)


def dyn(ref, start, size):
    return ref[pl.ds(pl.multiple_of(start, 8), size), :]


def halves(a):
    high = a.astype(bf16)
    return high, (a - high.astype(f32)).astype(bf16)


def thirds(a):
    high, rest = a.astype(bf16), None
    rest = a - high.astype(f32)
    middle = rest.astype(bf16)
    return high, middle, (rest - middle.astype(f32)).astype(bf16)


def product(a, b, dims):
    return lax.dot_general(a, b, (dims, ((), ())), preferred_element_type=f32)


def dot(a, b, dims=((1,), (0,))):
    a_high, a_low = halves(a)
    b_high, b_low = halves(b)
    return product(a_high, b_high, dims) + (product(a_high, b_low, dims) + product(a_low, b_high, dims))


def pick_right(a, weight):
    dims = ((1,), (0,))
    w = weight.astype(bf16)
    high, middle, low = thirds(a)
    return product(high, w, dims) + (product(middle, w, dims) + product(low, w, dims))


def pick_left(weight, a):
    dims = ((1,), (0,))
    w = weight.astype(bf16)
    high, middle, low = thirds(a)
    return product(w, high, dims) + (product(w, middle, dims) + product(w, low, dims))


def iota(shape, axis):
    return lax.broadcasted_iota(jnp.int32, shape, axis)


def near_z(v):
    lane = iota(v.shape, 1)
    last = v.shape[1] - 1
    below = jnp.where(lane == 0, 0.0, roll(v, 1, 1))
    above = jnp.where(lane == last, 0.0, roll(v, -1, 1))
    return below + above


def near_x(v):
    return roll(v, 1, 0) + roll(v, -1, 0)


def operate(v, v_near_x, v_near_y, rho, cx, cy, cz):
    twice = 2.0 * v
    stencil = cx * (twice - v_near_x) + cy * (twice - v_near_y) + cz * (twice - near_z(v))
    return shift_term * v + rho * stencil


def diagonal(rho, cx, cy, cz):
    return shift_term + 2.0 * rho * (cx + cy + cz)


def solve_z(w, lines):
    count, size = lines.shape[0], lines.shape[1]
    parts = []
    for k in range(count):
        parts.append(dot(w[:, k * size : (k + 1) * size], lines[k], ((1,), (1,))))
    return jnp.concatenate(parts, axis=1)


def columns_by(v, pick):
    cuts = [slice(256 * k, 256 * (k + 1)) for k in range(v.shape[1] // 256)]
    return jnp.concatenate([pick_right(v[:, cut], pick) for cut in cuts], axis=1)


def pair_columns(v, scale):
    fine, coarse = iota((256, 128), 0), iota((256, 128), 1)
    return columns_by(v, jnp.where(fine // 2 == coarse, scale, 0.0))


def even_columns(v, scale):
    fine, coarse = iota((256, 128), 0), iota((256, 128), 1)
    return columns_by(v, jnp.where(fine == 2 * coarse, scale, 0.0))


def restrict_columns(v):
    lane = iota(v.shape, 1)
    last = v.shape[1] - 1
    one = jnp.where(lane == last, 0.0, roll(v, -1, 1))
    two = jnp.where(lane >= last - 1, 0.0, roll(v, -2, 1))
    below = jnp.where(lane == 0, 0.0, roll(v, 1, 1))
    return even_columns(below + 3.0 * v + 3.0 * one + two, 0.125)


def raise_columns(v):
    lane = iota(v.shape, 1)
    last = v.shape[1] - 1
    below = jnp.where(lane == 0, 0.0, roll(v, 1, 1))
    above = jnp.where(lane == last, 0.0, roll(v, -1, 1))
    even = 3.0 * v + below
    odd = 3.0 * v + above
    coarse, fine = iota((128, 256), 0), iota((128, 256), 1)
    at_even = jnp.where(fine == 2 * coarse, 0.25, 0.0)
    at_odd = jnp.where(fine == 2 * coarse + 1, 0.25, 0.0)
    parts = []
    for k in range(v.shape[1] // 128):
        cut = slice(128 * k, 128 * (k + 1))
        parts.append(pick_right(even[:, cut], at_even) + pick_right(odd[:, cut], at_odd))
    return jnp.concatenate(parts, axis=1)


def restrict_rows(v):
    coarse, fine = iota((ME, FE), 0), iota((ME, FE), 1)
    away = fine - 2 * coarse
    weight = jnp.where((away == 0) | (away == 1), 0.375, 0.0)
    weight = weight + jnp.where((away == -1) | (away == 2), 0.125, 0.0)
    return pick_left(weight, v)


def pair_rows(v):
    coarse, fine = iota((ME, FE), 0), iota((ME, FE), 1)
    return pick_left(jnp.where(fine // 2 == coarse, 1.0, 0.0), v)


def raise_rows(v):
    fine, coarse = iota((FE, ME), 0), iota((FE, ME), 1)
    away = fine - 2 * coarse
    weight = jnp.where((away == 0) | (away == 1), 0.75, 0.0)
    weight = weight + jnp.where((away == 2) | (away == -1), 0.25, 0.0)
    return pick_left(weight, v)


def inside_middle(px):
    row = iota((ME, MZ), 0) + MX * px - MH
    return (row >= 0) & (row < MX * N_PX)


def inside_fine(px):
    row = iota((FE, FZ), 0) + FX * px - FH
    return (row >= 0) & (row < FX * N_PX)


def to_slabs(plane, out, at):
    for m in range(8):
        out[m, at] = plane[:, 128 * m : 128 * (m + 1)]


def from_slabs(ref, at):
    return jnp.concatenate([ref[m, at] for m in range(8)], axis=1)


def start(px, py, forcing, inv_density, sx, sy, force, rho, lower, upper, low, high, cx):
    square = iota((FX, FX), 0) == iota((FX, FX), 1)
    column = jnp.sum(jnp.where(square, sx[...], 0.0), axis=1, keepdims=True)
    cx[...] = jnp.broadcast_to(column, (FX, 128))
    wide = jnp.broadcast_to(column, (FX, FZ))
    for at, out in ((0, lower), (1, upper)):
        f_plane, r_plane = forcing[:, at, :], inv_density[:, at, :]
        force[at] = f_plane
        rho[at] = r_plane
        out[0:32] = f_plane
        out[32:64] = r_plane
        out[64:72] = jnp.broadcast_to(sy[0:1, at : at + 1], (8, FZ))
        for side, rows in ((low, slice(0, 8)), (high, slice(24, 32))):
            side[8 * at : 8 * at + 8] = f_plane[rows]
            side[16 + 8 * at : 24 + 8 * at] = r_plane[rows]
    low[32:40] = wide[0:8]
    high[32:40] = wide[24:32]


def own_lines(px, py, force, rho, cx, sy, cz, lines, u):
    parts = []
    for at in range(2):
        parts.append(force[at] / diagonal(rho[at], cx[:, 0:1], sy[0:1, at : at + 1], cz[...]))
    solved = solve_z(jnp.concatenate(parts, axis=0), lines)
    u[0] = solved[0:FX]
    u[1] = solved[FX : 2 * FX]


def first_half(px, py, force, rho, cx, sy, cz, u, below, above, left, right, lines, slabs):
    cx_col = cx[:, 0:1]
    cz_row = cz[...]
    parts = []
    for side in (below, above):
        parts.append(side[0:32] / diagonal(side[32:64], cx_col, side[64:65], cz_row))
    for side in (left, right):
        for at in range(2):
            cut, deep = slice(8 * at, 8 * at + 8), slice(16 + 8 * at, 24 + 8 * at)
            parts.append(side[cut] / diagonal(side[deep], side[32:40, 0:1], sy[0:1, at : at + 1], cz_row))
    solved = solve_z(jnp.concatenate(parts, axis=0), lines)
    planes = [solved[0:32], u[0], u[1], solved[32:64]]
    for at in range(2):
        own = u[at]
        before, after = solved[64 + 8 * at : 72 + 8 * at], solved[80 + 8 * at : 88 + 8 * at]
        beside_x = near_x(jnp.concatenate([before, own, after], axis=0))[FH : FH + FX]
        beside_y = planes[at] + planes[at + 2]
        cy = sy[0:1, at : at + 1]
        applied = operate(own, beside_x, beside_y, rho[at], cx_col, cy, cz_row)
        to_slabs((force[at] - applied) / diagonal(rho[at], cx_col, cy, cz_row), slabs, at)


def middle_statics(px, py, rho, cx, sy, cz, left, right, column, r_mid, cx_mid, cyz_mid, told):
    total = None
    for at in range(2):
        deep = slice(16 + 8 * at, 24 + 8 * at)
        plane = jnp.concatenate([left[deep], rho[at], right[deep]], axis=0)
        total = plane if total is None else total + plane
    dense = pair_columns(pair_rows(total), 0.125)
    columns = jnp.concatenate([left[32:40, 0:128], cx[...], right[32:40, 0:128]], axis=0)
    cym = jnp.broadcast_to((sy[0:1, 0:1] + sy[0:1, 1:2]) * 0.125, (8, MZ))
    czm = pair_columns(jnp.broadcast_to(cz[...], (16, FZ)), 0.125)
    r_mid[...] = dense
    cx_mid[...] = pair_rows(columns) * 0.125
    cyz_mid[...] = jnp.concatenate([czm[0:1], cym[0:7]], axis=0)
    own = roll(dense, -MH, 0)[0:MX]
    told[0:8, 0:MZ] = own[0:8]
    told[0:8, MZ:FZ] = own[8:16]
    for k in range(4):
        told[8:16, 128 * k : 128 * (k + 1)] = column[8 * k : 8 * (k + 1)]
    told[8:16, MZ:FZ] = cym


def solve_x_fine(px, py, slabs, lines, out):
    block = lines[0]
    for at in range(2):
        column = jnp.concatenate([slabs[m, at] for m in range(8)], axis=0)
        solved = dot(block, column)
        for m in range(8):
            out[m, at] = solved[32 * m : 32 * (m + 1)]


def add_slabs(px, py, u, slabs, told, out):
    for at in range(2):
        out[FX * at : FX * (at + 1)] = u[at] + from_slabs(slabs, at)
    out[64:80] = told[...]


def pack_u(px, py, u, below, above, y_below, y_above, low, high):
    for start_row, out in ((0, low), (24, high)):
        rows = slice(start_row, start_row + 8)
        next_rows = slice(32 + start_row, 40 + start_row)
        for j, side in enumerate((below, u, above)):
            out[16 * j : 16 * j + 8] = side[rows]
            out[16 * j + 8 : 16 * j + 16] = side[next_rows]
        for j, side in enumerate((y_below, y_above)):
            out[48 + 16 * j : 56 + 16 * j] = side[rows]
            out[56 + 16 * j : 64 + 16 * j] = side[next_rows]


def to_middle(px, py, u, below, above, left, right, force, rho, y_below, y_above, x_left, x_right, cx, sy, cz, r_mid, cx_mid, cyz_mid, lines, u_ext, f_ext, r_ext, cx_ext, f_mid, v_out, told):
    columns = jnp.concatenate([x_left[32:40, 0:128], cx[...], x_right[32:40, 0:128]], axis=0)
    cx_ext[...] = columns
    cx_col = columns[:, 0:1]
    cz_row = cz[...]
    told[0:16] = below[64:80]
    told[16:32] = above[64:80]
    planes = []
    for j in range(6):
        side = (below, u, above)[j // 2]
        own = side[FX * (j % 2) : FX * (j % 2) + FX]
        planes.append(jnp.concatenate([left[8 * j : 8 * j + 8], own, right[8 * j : 8 * j + 8]], axis=0))
    total = None
    for j in range(4):
        if j in (1, 2):
            at = j - 1
            cut, deep = slice(8 * at, 8 * at + 8), slice(16 + 8 * at, 24 + 8 * at)
            f_plane = jnp.concatenate([x_left[cut], force[at], x_right[cut]], axis=0)
            r_plane = jnp.concatenate([x_left[deep], rho[at], x_right[deep]], axis=0)
            f_ext[at] = f_plane
            r_ext[at] = r_plane
            cy = sy[0:1, at : at + 1]
        else:
            side, at = (y_below, 48) if j == 0 else (y_above, 64)
            cut, deep = slice(at, at + 8), slice(at + 8, at + 16)
            f_plane = jnp.concatenate([left[cut], side[0:32], right[cut]], axis=0)
            r_plane = jnp.concatenate([left[deep], side[32:64], right[deep]], axis=0)
            cy = side[64:65]
        own = planes[j + 1]
        u_ext[j] = own
        applied = operate(own, near_x(own), planes[j] + planes[j + 2], r_plane, cx_col, cy, cz_row)
        left_over = f_plane - applied
        if j in (1, 2):
            left_over = 3.0 * left_over
        total = left_over if total is None else total + left_over
    rhs = restrict_columns(restrict_rows(total * 0.125))
    rhs = jnp.where(inside_middle(px), rhs, 0.0)
    f_mid[...] = rhs
    diag = diagonal(*middle_parts(r_mid, cx_mid, cyz_mid))
    v_out[...] = solve_z(rhs / diag, lines)


def middle_parts(r_mid, cx_mid, cyz_mid):
    return r_mid[...], cx_mid[:, 0:1], cyz_mid[1:2], cyz_mid[0:1]


def middle_scaled(px, py, v, below, above, f_mid, r_mid, cx_mid, cyz_mid, out):
    rho, cx, cy, cz = middle_parts(r_mid, cx_mid, cyz_mid)
    own = v[...]
    applied = operate(own, near_x(own), below[...] + above[...], rho, cx, cy, cz)
    scaled = (f_mid[...] - applied) / diagonal(rho, cx, cy, cz)
    part = roll(scaled, -MH, 0)[0:MX]
    for i in range(N_PX):
        out[i] = part


def solve_x_middle(px, py, gathered, lines, v, out):
    total = MX * N_PX
    pieces = []
    starts = (
        (jnp.maximum(MX * px - 8, 0), 8),
        (MX * px, MX),
        (jnp.minimum(MX * px + MX, total - 8), 8),
    )
    for start, size in starts:
        rows = dyn(lines, start, size)
        block = (start // 256) * 256
        pieces.append(dot(rows, dyn(gathered, block, 256)))
    full = jnp.concatenate(pieces, axis=0)
    part = roll(full, MH - 8, 0)[0:ME]
    out[...] = v[...] + jnp.where(inside_middle(px), part, 0.0)


def block_mean(px, py, v, f_mid, r_mid, cx_mid, cyz_mid, told, column, out):
    rho, cx, cy, cz = middle_parts(r_mid, cx_mid, cyz_mid)
    own = v[...]
    applied = operate(own, near_x(own), 0.0, rho, cx, cy, cz)
    row = iota((ME, MZ), 0)
    kept = jnp.where((row >= MH) & (row < MH + MX), f_mid[...] - applied, 0.0)

    def mean(a):
        return jnp.sum(jnp.sum(a, axis=0, keepdims=True), axis=1, keepdims=True) * (1.0 / (MX * MZ))

    sent = column[...] * mean(kept)
    inner = roll(own, -MH, 0)[0:MX]
    for at in (0, 16):
        share = mean(told[at : at + 8, 0:MZ] * inner[0:8] + told[at : at + 8, MZ:FZ] * inner[8:16])
        share = share * told[at + 8 : at + 9, MZ : MZ + 1]
        theirs = [told[at + 8 : at + 16, 128 * k : 128 * (k + 1)] for k in range(4)]
        sent = sent + jnp.concatenate(theirs, axis=0) * share
    for i in range(N_PX):
        out[i] = jnp.broadcast_to(sent[i : i + 1], (8, 128))


def sum_x(px, py, parts, out):
    total = parts[0]
    for i in range(1, N_PX):
        total = total + parts[i]
    for j in range(N_PY):
        out[j] = total


def second_half(px, py, parts, v, below, above, f_mid, r_mid, cx_mid, cyz_mid, lines, out):
    total = parts[0]
    for j in range(1, N_PY):
        total = total + parts[j]
    lane = iota((8, 128), 1)
    row = iota((ME, MZ), 0)

    def raised(plane, dy):
        held = (py + dy >= 0) & (py + dy < N_PY)
        at = []
        for dx in range(3):
            wanted = (lane == dx * N_PY + py + dy) & held
            found = jnp.sum(jnp.where(wanted, total, 0.0), axis=1, keepdims=True)[0:1]
            at.append(found)
        return plane + jnp.where(row < MH, at[0], jnp.where(row < MH + MX, at[1], at[2]))

    own = raised(v[...], 0)
    beside = raised(below[...], -1) + raised(above[...], 1)
    rho, cx, cy, cz = middle_parts(r_mid, cx_mid, cyz_mid)
    applied = operate(own, near_x(own), beside, rho, cx, cy, cz)
    out[...] = own + solve_z((f_mid[...] - applied) / diagonal(rho, cx, cy, cz), lines)


def to_fine(px, py, v, below, above, u_ext, f_ext, r_ext, cx_ext, sy, cz, lines, out, lower, upper):
    rows = [raise_rows(p[...]) for p in (below, v, above)]
    columns = raise_columns(jnp.concatenate(rows, axis=0)) * 0.25
    raised = [columns[FE * i : FE * (i + 1)] for i in range(3)]
    mids = [
        3.0 * raised[0] + raised[1],
        3.0 * raised[1] + raised[0],
        3.0 * raised[1] + raised[2],
        3.0 * raised[2] + raised[1],
    ]
    inside = inside_fine(px)
    us = []
    for j in range(4):
        held = inside
        if j == 0:
            held = inside & (py > 0)
        if j == 3:
            held = inside & (py < N_PY - 1)
        us.append(u_ext[j] + jnp.where(held, mids[j], 0.0))
    cx_col = cx_ext[:, 0:1]
    cz_row = cz[...]
    parts = []
    for at in range(2):
        own = us[at + 1]
        cy = sy[0:1, at : at + 1]
        applied = operate(own, near_x(own), us[at] + us[at + 2], r_ext[at], cx_col, cy, cz_row)
        parts.append((f_ext[at] - applied) / diagonal(r_ext[at], cx_col, cy, cz_row))
    solved = solve_z(jnp.concatenate(parts, axis=0), lines)
    for at in range(2):
        new = us[at + 1] + solved[FE * at : FE * (at + 1)]
        out[at] = new
        (lower if at == 0 else upper)[...] = new[FH : FH + FX]


def last_scaled(px, py, u, below, above, f_ext, r_ext, cx_ext, sy, cz, slabs):
    cx_col = cx_ext[FH : FH + FX, 0:1]
    cz_row = cz[...]
    inner = slice(FH, FH + FX)
    for at in range(2):
        full = u[at]
        beside_x = near_x(full)[inner]
        own = full[inner]
        beside_y = (below[...] if at == 0 else u[0, inner]) + (above[...] if at == 1 else u[1, inner])
        rho = r_ext[at, inner]
        cy = sy[0:1, at : at + 1]
        applied = operate(own, beside_x, beside_y, rho, cx_col, cy, cz_row)
        scaled = (f_ext[at, inner] - applied) / diagonal(rho, cx_col, cy, cz_row)
        to_slabs(scaled, slabs, at)


def finish(px, py, u, slabs, out):
    for at in range(2):
        out[:, at, :] = u[at, FH : FH + FX] + from_slabs(slabs, at)


class Device:
    def run(self, stage, shapes, *args):
        def kernel(*refs):
            stage(lax.axis_index("px"), lax.axis_index("py"), *refs)

        whole = pl.BlockSpec(memory_space=pltpu.VMEM)
        outs = pl.pallas_call(
            kernel,
            out_shape=[jax.ShapeDtypeStruct(s, f32) for s in shapes],
            in_specs=[whole] * len(args),
            out_specs=[whole] * len(shapes),
            compiler_params=pltpu.CompilerParams(vmem_limit_bytes=24 * 1024 * 1024),
            name=stage.__name__,
        )(*args)
        return outs if len(shapes) > 1 else outs[0]

    def local(self, fn, *args):
        return fn(*args)

    def block_of(self, lines):
        at = lax.axis_index("px") // 8
        return lax.dynamic_slice_in_dim(lines, at, 1, axis=0)

    def beside(self, axis, low, high):
        n = lax.axis_size(axis)
        up = [(i, i + 1) for i in range(n - 1)]
        down = [(j, i) for i, j in up]
        return lax.ppermute(high, axis, up), lax.ppermute(low, axis, down)

    def swap(self, axis, array, group):
        n = lax.axis_size(axis)
        groups = None
        if group < n:
            groups = [list(range(k, k + group)) for k in range(0, n, group)]
        return lax.all_to_all(array, axis, 0, 0, axis_index_groups=groups, tiled=True)


def arrange_column(coarse):
    table = coarse.reshape(N_PY, N_PX).T
    none = jnp.zeros((1, N_PY), f32)
    before = jnp.concatenate([none, table[:-1]], axis=0)
    after = jnp.concatenate([table[1:], none], axis=0)
    return jnp.concatenate([before, table, after, jnp.zeros((N_PX, 128 - 3 * N_PY), f32)], axis=1)


def cycle(d, forcing, inv_density, stretch_x, stretch_y, stretch_z, lines_z0, lines_x0, lines_z1, lines_x1, coarse_inverse):
    sx = d.local(lambda a: a.reshape(1, FX), stretch_x)
    sy = d.local(lambda a: a.reshape(1, 2), stretch_y)
    cz = d.local(lambda a: a.reshape(1, FZ), stretch_z)
    rows_x1 = d.local(lambda a: a.reshape(MX * N_PX, 256), lines_x1)
    slab, own, mid = (8, 2, FX, 128), (2, FX, FZ), (ME, MZ)

    force, rho, lower, upper, low, high, cx = d.run(
        start,
        [own, own, (72, FZ), (72, FZ), (40, FZ), (40, FZ), (FX, 128)],
        forcing, inv_density, sx, sy,
    )
    y_below, y_above = d.beside("py", lower, upper)
    x_left, x_right = d.beside("px", low, high)
    column = d.local(arrange_column, coarse_inverse)
    block = d.block_of(lines_x0)
    u = d.run(own_lines, [own], force, rho, cx, sy, cz, lines_z0)
    slabs = d.run(
        first_half, [slab],
        force, rho, cx, sy, cz, u, y_below, y_above, x_left, x_right, lines_z0,
    )
    slabs = d.swap("px", slabs, 8)
    r_mid, cx_mid, cyz_mid, told = d.run(
        middle_statics,
        [mid, (ME, 128), (8, MZ), (16, FZ)],
        rho, cx, sy, cz, x_left, x_right, column,
    )
    slabs = d.run(solve_x_fine, [slab], slabs, block)
    slabs = d.swap("px", slabs, 8)
    u = d.run(add_slabs, [(80, FZ)], u, slabs, told)
    below, above = d.beside("py", u, u)
    low, high = d.run(pack_u, [(80, FZ)] * 2, u, below, above, y_below, y_above)
    left, right = d.beside("px", low, high)
    u_ext, f_ext, r_ext, cx_ext, f_mid, v, told = d.run(
        to_middle,
        [(4, FE, FZ), (2, FE, FZ), (2, FE, FZ), (FE, 128), mid, mid, (32, FZ)],
        u, below, above, left, right, force, rho, y_below, y_above, x_left, x_right,
        cx, sy, cz, r_mid, cx_mid, cyz_mid, lines_z1,
    )
    statics = (f_mid, r_mid, cx_mid, cyz_mid)

    below, above = d.beside("py", v, v)
    every = d.run(middle_scaled, [(N_PX, MX, MZ)], v, below, above, *statics)
    every = d.swap("px", every, N_PX)
    every = d.local(lambda a: a.reshape(MX * N_PX, MZ), every)
    v = d.run(solve_x_middle, [mid], every, rows_x1, v)
    below, above = d.beside("py", v, v)
    sent = d.run(block_mean, [(N_PX, 8, 128)], v, *statics, told, column)
    parts = d.swap("px", sent, N_PX)
    parts = d.run(sum_x, [(N_PY, 8, 128)], parts)
    parts = d.swap("py", parts, N_PY)
    v = d.run(second_half, [mid], parts, v, below, above, *statics, lines_z1)
    below, above = d.beside("py", v, v)
    every = d.run(middle_scaled, [(N_PX, MX, MZ)], v, below, above, *statics)
    every = d.swap("px", every, N_PX)
    every = d.local(lambda a: a.reshape(MX * N_PX, MZ), every)
    v = d.run(solve_x_middle, [mid], every, rows_x1, v)

    below, above = d.beside("py", v, v)
    u, lower, upper = d.run(
        to_fine,
        [(2, FE, FZ), (FX, FZ), (FX, FZ)],
        v, below, above, u_ext, f_ext, r_ext, cx_ext, sy, cz, lines_z0,
    )
    below, above = d.beside("py", lower, upper)
    slabs = d.run(last_scaled, [slab], u, below, above, f_ext, r_ext, cx_ext, sy, cz)
    slabs = d.swap("px", slabs, 8)
    slabs = d.run(solve_x_fine, [slab], slabs, block)
    slabs = d.swap("px", slabs, 8)
    return d.run(finish, [(FX, 2, FZ)], u, slabs)


def solution(mesh):
    placed = (
        P("px", "py", None),
        P("px", "py", None),
        P("px"),
        P("py"),
        P(),
        P(),
        P(),
        P(),
        P(),
        P(("py", "px"), None),
    )
    return jax.shard_map(
        functools.partial(cycle, Device()),
        mesh=mesh,
        in_specs=placed,
        out_specs=P("px", "py", None),
        check_vma=False,
    )
```

```python
import jax
import jax.numpy as jnp
from jax import lax
from jax.experimental import pallas as pl
from jax.experimental.pallas import tpu as pltpu
from jax.sharding import PartitionSpec as P


shift_term = 0.1
f32 = jnp.float32
bf16 = jnp.bfloat16

N_PY, N_PX = 16, 32
FX, FZ = 32, 1024
MX, MZ = 16, 512
FH, MH = 8, 4
FE, ME = FX + 2 * FH, MX + 2 * MH


def roll(v, shift, axis):
    return pltpu.roll(v, shift % v.shape[axis], axis)


def dyn(ref, start, size):
    return ref[pl.ds(pl.multiple_of(start, 8), size), :]


def halves(a):
    high = a.astype(bf16)
    return high, (a - high.astype(f32)).astype(bf16)


def thirds(a):
    high, rest = a.astype(bf16), None
    rest = a - high.astype(f32)
    middle = rest.astype(bf16)
    return high, middle, (rest - middle.astype(f32)).astype(bf16)


def product(a, b, dims):
    return lax.dot_general(a, b, (dims, ((), ())), preferred_element_type=f32)


def dot(a, b, dims=((1,), (0,))):
    a_high, a_low = halves(a)
    b_high, b_low = halves(b)
    return product(a_high, b_high, dims) + (product(a_high, b_low, dims) + product(a_low, b_high, dims))


def pick_right(a, weight):
    dims = ((1,), (0,))
    w = weight.astype(bf16)
    high, middle, low = thirds(a)
    return product(high, w, dims) + (product(middle, w, dims) + product(low, w, dims))


def pick_left(weight, a):
    dims = ((1,), (0,))
    w = weight.astype(bf16)
    high, middle, low = thirds(a)
    return product(w, high, dims) + (product(w, middle, dims) + product(w, low, dims))


def iota(shape, axis):
    return lax.broadcasted_iota(jnp.int32, shape, axis)


def near_z(v):
    lane = iota(v.shape, 1)
    last = v.shape[1] - 1
    below = jnp.where(lane == 0, 0.0, roll(v, 1, 1))
    above = jnp.where(lane == last, 0.0, roll(v, -1, 1))
    return below + above


def near_x(v):
    return roll(v, 1, 0) + roll(v, -1, 0)


def operate(v, v_near_x, v_near_y, rho, cx, cy, cz):
    twice = 2.0 * v
    stencil = cx * (twice - v_near_x) + cy * (twice - v_near_y) + cz * (twice - near_z(v))
    return shift_term * v + rho * stencil


def diagonal(rho, cx, cy, cz):
    return shift_term + 2.0 * rho * (cx + cy + cz)


def solve_z(w, lines):
    count, size = lines.shape[0], lines.shape[1]
    parts = []
    for k in range(count):
        parts.append(dot(w[:, k * size : (k + 1) * size], lines[k], ((1,), (1,))))
    return jnp.concatenate(parts, axis=1)


def columns_by(v, pick):
    cuts = [slice(256 * k, 256 * (k + 1)) for k in range(v.shape[1] // 256)]
    return jnp.concatenate([pick_right(v[:, cut], pick) for cut in cuts], axis=1)


def pair_columns(v, scale):
    fine, coarse = iota((256, 128), 0), iota((256, 128), 1)
    return columns_by(v, jnp.where(fine // 2 == coarse, scale, 0.0))


def even_columns(v, scale):
    fine, coarse = iota((256, 128), 0), iota((256, 128), 1)
    return columns_by(v, jnp.where(fine == 2 * coarse, scale, 0.0))


def restrict_columns(v):
    lane = iota(v.shape, 1)
    last = v.shape[1] - 1
    one = jnp.where(lane == last, 0.0, roll(v, -1, 1))
    two = jnp.where(lane >= last - 1, 0.0, roll(v, -2, 1))
    below = jnp.where(lane == 0, 0.0, roll(v, 1, 1))
    return even_columns(below + 3.0 * v + 3.0 * one + two, 0.125)


def raise_columns(v):
    lane = iota(v.shape, 1)
    last = v.shape[1] - 1
    below = jnp.where(lane == 0, 0.0, roll(v, 1, 1))
    above = jnp.where(lane == last, 0.0, roll(v, -1, 1))
    even = 3.0 * v + below
    odd = 3.0 * v + above
    coarse, fine = iota((128, 256), 0), iota((128, 256), 1)
    at_even = jnp.where(fine == 2 * coarse, 0.25, 0.0)
    at_odd = jnp.where(fine == 2 * coarse + 1, 0.25, 0.0)
    parts = []
    for k in range(v.shape[1] // 128):
        cut = slice(128 * k, 128 * (k + 1))
        parts.append(pick_right(even[:, cut], at_even) + pick_right(odd[:, cut], at_odd))
    return jnp.concatenate(parts, axis=1)


def restrict_rows(v):
    coarse, fine = iota((ME, FE), 0), iota((ME, FE), 1)
    away = fine - 2 * coarse
    weight = jnp.where((away == 0) | (away == 1), 0.375, 0.0)
    weight = weight + jnp.where((away == -1) | (away == 2), 0.125, 0.0)
    return pick_left(weight, v)


def pair_rows(v):
    coarse, fine = iota((ME, FE), 0), iota((ME, FE), 1)
    return pick_left(jnp.where(fine // 2 == coarse, 1.0, 0.0), v)


def raise_rows(v):
    fine, coarse = iota((FE, ME), 0), iota((FE, ME), 1)
    away = fine - 2 * coarse
    weight = jnp.where((away == 0) | (away == 1), 0.75, 0.0)
    weight = weight + jnp.where((away == 2) | (away == -1), 0.25, 0.0)
    return pick_left(weight, v)


def inside_middle(px):
    row = iota((ME, MZ), 0) + MX * px - MH
    return (row >= 0) & (row < MX * N_PX)


def inside_fine(px):
    row = iota((FE, FZ), 0) + FX * px - FH
    return (row >= 0) & (row < FX * N_PX)


def to_slabs(plane, out, at):
    for m in range(8):
        out[m, at] = plane[:, 128 * m : 128 * (m + 1)]


def from_slabs(ref, at):
    return jnp.concatenate([ref[m, at] for m in range(8)], axis=1)


def start(px, py, forcing, inv_density, sx, sy, force, rho, lower, upper, low, high, cx):
    square = iota((FX, FX), 0) == iota((FX, FX), 1)
    column = jnp.sum(jnp.where(square, sx[...], 0.0), axis=1, keepdims=True)
    cx[...] = jnp.broadcast_to(column, (FX, 128))
    wide = jnp.broadcast_to(column, (FX, FZ))
    for at, out in ((0, lower), (1, upper)):
        f_plane, r_plane = forcing[:, at, :], inv_density[:, at, :]
        force[at] = f_plane
        rho[at] = r_plane
        out[0:32] = f_plane
        out[32:64] = r_plane
        out[64:72] = jnp.broadcast_to(sy[0:1, at : at + 1], (8, FZ))
        for side, rows in ((low, slice(0, 8)), (high, slice(24, 32))):
            side[8 * at : 8 * at + 8] = f_plane[rows]
            side[16 + 8 * at : 24 + 8 * at] = r_plane[rows]
    low[32:40] = wide[0:8]
    high[32:40] = wide[24:32]


def own_lines(px, py, force, rho, cx, sy, cz, lines, u):
    parts = []
    for at in range(2):
        parts.append(force[at] / diagonal(rho[at], cx[:, 0:1], sy[0:1, at : at + 1], cz[...]))
    solved = solve_z(jnp.concatenate(parts, axis=0), lines)
    u[0] = solved[0:FX]
    u[1] = solved[FX : 2 * FX]


def first_half(px, py, force, rho, cx, sy, cz, u, below, above, left, right, lines, slabs):
    cx_col = cx[:, 0:1]
    cz_row = cz[...]
    parts = []
    for side in (below, above):
        parts.append(side[0:32] / diagonal(side[32:64], cx_col, side[64:65], cz_row))
    for side in (left, right):
        for at in range(2):
            cut, deep = slice(8 * at, 8 * at + 8), slice(16 + 8 * at, 24 + 8 * at)
            parts.append(side[cut] / diagonal(side[deep], side[32:40, 0:1], sy[0:1, at : at + 1], cz_row))
    solved = solve_z(jnp.concatenate(parts, axis=0), lines)
    planes = [solved[0:32], u[0], u[1], solved[32:64]]
    for at in range(2):
        own = u[at]
        before, after = solved[64 + 8 * at : 72 + 8 * at], solved[80 + 8 * at : 88 + 8 * at]
        beside_x = near_x(jnp.concatenate([before, own, after], axis=0))[FH : FH + FX]
        beside_y = planes[at] + planes[at + 2]
        cy = sy[0:1, at : at + 1]
        applied = operate(own, beside_x, beside_y, rho[at], cx_col, cy, cz_row)
        to_slabs((force[at] - applied) / diagonal(rho[at], cx_col, cy, cz_row), slabs, at)


def middle_statics(px, py, rho, cx, sy, cz, left, right, column, r_mid, cx_mid, cyz_mid, told):
    total = None
    for at in range(2):
        deep = slice(16 + 8 * at, 24 + 8 * at)
        plane = jnp.concatenate([left[deep], rho[at], right[deep]], axis=0)
        total = plane if total is None else total + plane
    dense = pair_columns(pair_rows(total), 0.125)
    columns = jnp.concatenate([left[32:40, 0:128], cx[...], right[32:40, 0:128]], axis=0)
    cym = jnp.broadcast_to((sy[0:1, 0:1] + sy[0:1, 1:2]) * 0.125, (8, MZ))
    czm = pair_columns(jnp.broadcast_to(cz[...], (16, FZ)), 0.125)
    r_mid[...] = dense
    cx_mid[...] = pair_rows(columns) * 0.125
    cyz_mid[...] = jnp.concatenate([czm[0:1], cym[0:7]], axis=0)
    own = roll(dense, -MH, 0)[0:MX]
    told[0:8, 0:MZ] = own[0:8]
    told[0:8, MZ:FZ] = own[8:16]
    for k in range(4):
        told[8:16, 128 * k : 128 * (k + 1)] = column[8 * k : 8 * (k + 1)]
    told[8:16, MZ:FZ] = cym


def solve_x_fine(px, py, slabs, lines, out):
    block = lines[0]
    for at in range(2):
        column = jnp.concatenate([slabs[m, at] for m in range(8)], axis=0)
        solved = dot(block, column)
        for m in range(8):
            out[m, at] = solved[32 * m : 32 * (m + 1)]


def add_slabs(px, py, u, slabs, told, out):
    for at in range(2):
        out[FX * at : FX * (at + 1)] = u[at] + from_slabs(slabs, at)
    out[64:80] = told[...]


def pack_u(px, py, u, below, above, y_below, y_above, low, high):
    for start_row, out in ((0, low), (24, high)):
        rows = slice(start_row, start_row + 8)
        next_rows = slice(32 + start_row, 40 + start_row)
        for j, side in enumerate((below, u, above)):
            out[16 * j : 16 * j + 8] = side[rows]
            out[16 * j + 8 : 16 * j + 16] = side[next_rows]
        for j, side in enumerate((y_below, y_above)):
            out[48 + 16 * j : 56 + 16 * j] = side[rows]
            out[56 + 16 * j : 64 + 16 * j] = side[next_rows]
        out[80:88] = u[72:80]


def to_middle(px, py, u, below, above, left, right, force, rho, y_below, y_above, x_left, x_right, cx, sy, cz, r_mid, cx_mid, cyz_mid, lines, u_ext, f_ext, r_ext, cx_ext, f_mid, v_out, told):
    columns = jnp.concatenate([x_left[32:40, 0:128], cx[...], x_right[32:40, 0:128]], axis=0)
    cx_ext[...] = columns
    cx_col = columns[:, 0:1]
    cz_row = cz[...]
    told[0:16] = below[64:80]
    told[16:32] = above[64:80]
    told[32:40] = right[80:88]
    told[40:48] = left[80:88]
    planes = []
    for j in range(6):
        side = (below, u, above)[j // 2]
        own = side[FX * (j % 2) : FX * (j % 2) + FX]
        planes.append(jnp.concatenate([left[8 * j : 8 * j + 8], own, right[8 * j : 8 * j + 8]], axis=0))
    total = None
    for j in range(4):
        if j in (1, 2):
            at = j - 1
            cut, deep = slice(8 * at, 8 * at + 8), slice(16 + 8 * at, 24 + 8 * at)
            f_plane = jnp.concatenate([x_left[cut], force[at], x_right[cut]], axis=0)
            r_plane = jnp.concatenate([x_left[deep], rho[at], x_right[deep]], axis=0)
            f_ext[at] = f_plane
            r_ext[at] = r_plane
            cy = sy[0:1, at : at + 1]
        else:
            side, at = (y_below, 48) if j == 0 else (y_above, 64)
            cut, deep = slice(at, at + 8), slice(at + 8, at + 16)
            f_plane = jnp.concatenate([left[cut], side[0:32], right[cut]], axis=0)
            r_plane = jnp.concatenate([left[deep], side[32:64], right[deep]], axis=0)
            cy = side[64:65]
        own = planes[j + 1]
        u_ext[j] = own
        applied = operate(own, near_x(own), planes[j] + planes[j + 2], r_plane, cx_col, cy, cz_row)
        left_over = f_plane - applied
        if j in (1, 2):
            left_over = 3.0 * left_over
        total = left_over if total is None else total + left_over
    rhs = restrict_columns(restrict_rows(total * 0.125))
    rhs = jnp.where(inside_middle(px), rhs, 0.0)
    f_mid[...] = rhs
    diag = diagonal(*middle_parts(r_mid, cx_mid, cyz_mid))
    v_out[...] = solve_z(rhs / diag, lines)


def middle_parts(r_mid, cx_mid, cyz_mid):
    return r_mid[...], cx_mid[:, 0:1], cyz_mid[1:2], cyz_mid[0:1]


def middle_scaled(px, py, v, below, above, f_mid, r_mid, cx_mid, cyz_mid, out):
    rho, cx, cy, cz = middle_parts(r_mid, cx_mid, cyz_mid)
    own = v[...]
    applied = operate(own, near_x(own), below[...] + above[...], rho, cx, cy, cz)
    scaled = (f_mid[...] - applied) / diagonal(rho, cx, cy, cz)
    part = roll(scaled, -MH, 0)[0:MX]
    for i in range(out.shape[0]):
        out[i] = part


def solve_x_middle(px, py, gathered, lines, v, out):
    total = MX * N_PX
    pieces = []
    starts = (
        (jnp.maximum(MX * px - 8, 0), 8),
        (MX * px, MX),
        (jnp.minimum(MX * px + MX, total - 8), 8),
    )
    for start, size in starts:
        rows = dyn(lines, start, size)
        block = (start // 256) * 256
        pieces.append(dot(rows, dyn(gathered, block, 256)))
    full = jnp.concatenate(pieces, axis=0)
    part = roll(full, MH - 8, 0)[0:ME]
    out[...] = v[...] + jnp.where(inside_middle(px), part, 0.0)


def solve_x_block(px, py, gathered, lines, v, out):
    total = MX * N_PX
    pieces = []
    starts = (
        (jnp.maximum(MX * px - 8, 0), 8),
        (MX * px, MX),
        (jnp.minimum(MX * px + MX, total - 8), 8),
    )
    for start, size in starts:
        pieces.append(dyn(lines, start, size))
    full = dot(jnp.concatenate(pieces, axis=0), gathered[...])
    part = roll(full, MH - 8, 0)[0:ME]
    row = iota((ME, MZ), 0) + MX * px - MH
    first = 256 * (px // 16)
    held = (row >= first) & (row < first + 256)
    out[...] = jnp.where(held, v[...] + part, 0.0)


def mend(px, py, v, other, out):
    row = iota((ME, MZ), 0)
    theirs = other[...]
    up = jnp.where((row >= MH + MX) & (px == 15), roll(theirs, MX, 0), 0.0)
    down = jnp.where((row < MH) & (px == 16), roll(theirs, -MX, 0), 0.0)
    out[...] = v[...] + (up + down)


def block_mean(px, py, v, f_mid, r_mid, cx_mid, cyz_mid, told, column, out):
    rho, cx, cy, cz = middle_parts(r_mid, cx_mid, cyz_mid)
    own = v[...]
    applied = operate(own, near_x(own), 0.0, rho, cx, cy, cz)
    row = iota((ME, MZ), 0)
    kept = jnp.where((row >= MH) & (row < MH + MX), f_mid[...] - applied, 0.0)

    def mean(a):
        return jnp.sum(jnp.sum(a, axis=0, keepdims=True), axis=1, keepdims=True) * (1.0 / (MX * MZ))

    sent = column[...] * mean(kept)
    inner = roll(own, -MH, 0)[0:MX]
    for at in (0, 16):
        share = mean(told[at : at + 8, 0:MZ] * inner[0:8] + told[at : at + 8, MZ:FZ] * inner[8:16])
        share = share * told[at + 8 : at + 9, MZ : MZ + 1]
        theirs = [told[at + 8 : at + 16, 128 * k : 128 * (k + 1)] for k in range(4)]
        sent = sent + jnp.concatenate(theirs, axis=0) * share
    for at, edge, inner_row, mine in ((32, MH + MX, MH + MX - 1, px == 15), (40, MH - 1, MH, px == 16)):
        line = r_mid[edge : edge + 1] * cx_mid[edge : edge + 1, 0:1] * v[inner_row : inner_row + 1]
        share = jnp.where(mine, mean(line), 0.0)
        theirs = [told[at : at + 8, 128 * k : 128 * (k + 1)] for k in range(4)]
        sent = sent + jnp.concatenate(theirs, axis=0) * share
    for i in range(N_PX):
        out[i] = jnp.broadcast_to(sent[i : i + 1], (8, 128))


def sum_x(px, py, parts, out):
    total = parts[0]
    for i in range(1, N_PX):
        total = total + parts[i]
    for j in range(N_PY):
        out[j] = total


def second_half(px, py, parts, v, below, above, f_mid, r_mid, cx_mid, cyz_mid, lines, out):
    total = parts[0]
    for j in range(1, N_PY):
        total = total + parts[j]
    lane = iota((8, 128), 1)
    row = iota((ME, MZ), 0)

    def raised(plane, dy):
        held = (py + dy >= 0) & (py + dy < N_PY)
        at = []
        for dx in range(3):
            wanted = (lane == dx * N_PY + py + dy) & held
            found = jnp.sum(jnp.where(wanted, total, 0.0), axis=1, keepdims=True)[0:1]
            at.append(found)
        return plane + jnp.where(row < MH, at[0], jnp.where(row < MH + MX, at[1], at[2]))

    own = raised(v[...], 0)
    beside = raised(below[...], -1) + raised(above[...], 1)
    rho, cx, cy, cz = middle_parts(r_mid, cx_mid, cyz_mid)
    applied = operate(own, near_x(own), beside, rho, cx, cy, cz)
    out[...] = own + solve_z((f_mid[...] - applied) / diagonal(rho, cx, cy, cz), lines)


def to_fine(px, py, v, below, above, u_ext, f_ext, r_ext, cx_ext, sy, cz, lines, out, lower, upper):
    rows = [raise_rows(p[...]) for p in (below, v, above)]
    columns = raise_columns(jnp.concatenate(rows, axis=0)) * 0.25
    raised = [columns[FE * i : FE * (i + 1)] for i in range(3)]
    mids = [
        3.0 * raised[0] + raised[1],
        3.0 * raised[1] + raised[0],
        3.0 * raised[1] + raised[2],
        3.0 * raised[2] + raised[1],
    ]
    inside = inside_fine(px)
    us = []
    for j in range(4):
        held = inside
        if j == 0:
            held = inside & (py > 0)
        if j == 3:
            held = inside & (py < N_PY - 1)
        us.append(u_ext[j] + jnp.where(held, mids[j], 0.0))
    cx_col = cx_ext[:, 0:1]
    cz_row = cz[...]
    parts = []
    for at in range(2):
        own = us[at + 1]
        cy = sy[0:1, at : at + 1]
        applied = operate(own, near_x(own), us[at] + us[at + 2], r_ext[at], cx_col, cy, cz_row)
        parts.append((f_ext[at] - applied) / diagonal(r_ext[at], cx_col, cy, cz_row))
    solved = solve_z(jnp.concatenate(parts, axis=0), lines)
    for at in range(2):
        new = us[at + 1] + solved[FE * at : FE * (at + 1)]
        out[at] = new
        (lower if at == 0 else upper)[...] = new[FH : FH + FX]


def last_scaled(px, py, u, below, above, f_ext, r_ext, cx_ext, sy, cz, slabs):
    cx_col = cx_ext[FH : FH + FX, 0:1]
    cz_row = cz[...]
    inner = slice(FH, FH + FX)
    for at in range(2):
        full = u[at]
        beside_x = near_x(full)[inner]
        own = full[inner]
        beside_y = (below[...] if at == 0 else u[0, inner]) + (above[...] if at == 1 else u[1, inner])
        rho = r_ext[at, inner]
        cy = sy[0:1, at : at + 1]
        applied = operate(own, beside_x, beside_y, rho, cx_col, cy, cz_row)
        scaled = (f_ext[at, inner] - applied) / diagonal(rho, cx_col, cy, cz_row)
        to_slabs(scaled, slabs, at)


def finish(px, py, u, slabs, out):
    for at in range(2):
        out[:, at, :] = u[at, FH : FH + FX] + from_slabs(slabs, at)


class Device:
    def run(self, stage, shapes, *args):
        def kernel(*refs):
            stage(lax.axis_index("px"), lax.axis_index("py"), *refs)

        whole = pl.BlockSpec(memory_space=pltpu.VMEM)
        outs = pl.pallas_call(
            kernel,
            out_shape=[jax.ShapeDtypeStruct(s, f32) for s in shapes],
            in_specs=[whole] * len(args),
            out_specs=[whole] * len(shapes),
            compiler_params=pltpu.CompilerParams(vmem_limit_bytes=24 * 1024 * 1024),
        )(*args)
        return outs if len(shapes) > 1 else outs[0]

    def local(self, fn, *args):
        return fn(*args)

    def block_of(self, lines):
        at = lax.axis_index("px") // 8
        return lax.dynamic_slice_in_dim(lines, at, 1, axis=0)

    def beside(self, axis, low, high):
        n = lax.axis_size(axis)
        up = [(i, i + 1) for i in range(n - 1)]
        down = [(j, i) for i, j in up]
        return lax.ppermute(high, axis, up), lax.ppermute(low, axis, down)

    def across(self, array):
        return lax.ppermute(array, "px", [(15, 16), (16, 15)])

    def swap(self, axis, array, group):
        n = lax.axis_size(axis)
        groups = None
        if group < n:
            groups = [list(range(k, k + group)) for k in range(0, n, group)]
        return lax.all_to_all(array, axis, 0, 0, axis_index_groups=groups, tiled=True)


def arrange_column(coarse):
    table = coarse.reshape(N_PY, N_PX).T
    none = jnp.zeros((1, N_PY), f32)
    before = jnp.concatenate([none, table[:-1]], axis=0)
    after = jnp.concatenate([table[1:], none], axis=0)
    return jnp.concatenate([before, table, after, jnp.zeros((N_PX, 128 - 3 * N_PY), f32)], axis=1)


def cycle(d, forcing, inv_density, stretch_x, stretch_y, stretch_z, lines_z0, lines_x0, lines_z1, lines_x1, coarse_inverse):
    sx = d.local(lambda a: a.reshape(1, FX), stretch_x)
    sy = d.local(lambda a: a.reshape(1, 2), stretch_y)
    cz = d.local(lambda a: a.reshape(1, FZ), stretch_z)
    rows_x1 = d.local(lambda a: a.reshape(MX * N_PX, 256), lines_x1)
    slab, own, mid = (8, 2, FX, 128), (2, FX, FZ), (ME, MZ)

    force, rho, lower, upper, low, high, cx = d.run(
        start,
        [own, own, (72, FZ), (72, FZ), (40, FZ), (40, FZ), (FX, 128)],
        forcing, inv_density, sx, sy,
    )
    y_below, y_above = d.beside("py", lower, upper)
    x_left, x_right = d.beside("px", low, high)
    column = d.local(arrange_column, coarse_inverse)
    block = d.block_of(lines_x0)
    u = d.run(own_lines, [own], force, rho, cx, sy, cz, lines_z0)
    slabs = d.run(
        first_half, [slab],
        force, rho, cx, sy, cz, u, y_below, y_above, x_left, x_right, lines_z0,
    )
    slabs = d.swap("px", slabs, 8)
    r_mid, cx_mid, cyz_mid, told = d.run(
        middle_statics,
        [mid, (ME, 128), (8, MZ), (16, FZ)],
        rho, cx, sy, cz, x_left, x_right, column,
    )
    slabs = d.run(solve_x_fine, [slab], slabs, block)
    slabs = d.swap("px", slabs, 8)
    u = d.run(add_slabs, [(80, FZ)], u, slabs, told)
    below, above = d.beside("py", u, u)
    low, high = d.run(pack_u, [(88, FZ)] * 2, u, below, above, y_below, y_above)
    left, right = d.beside("px", low, high)
    u_ext, f_ext, r_ext, cx_ext, f_mid, v, told = d.run(
        to_middle,
        [(4, FE, FZ), (2, FE, FZ), (2, FE, FZ), (FE, 128), mid, mid, (48, FZ)],
        u, below, above, left, right, force, rho, y_below, y_above, x_left, x_right,
        cx, sy, cz, r_mid, cx_mid, cyz_mid, lines_z1,
    )
    statics = (f_mid, r_mid, cx_mid, cyz_mid)

    below, above = d.beside("py", v, v)
    every = d.run(middle_scaled, [(16, MX, MZ)], v, below, above, *statics)
    every = d.swap("px", every, 16)
    every = d.local(lambda a: a.reshape(256, MZ), every)
    v = d.run(solve_x_block, [mid], every, rows_x1, v)
    other = d.across(v)
    sent = d.run(block_mean, [(N_PX, 8, 128)], v, *statics, told, column)
    parts = d.swap("px", sent, N_PX)
    v = d.run(mend, [mid], v, other)
    below, above = d.beside("py", v, v)
    parts = d.run(sum_x, [(N_PY, 8, 128)], parts)
    parts = d.swap("py", parts, N_PY)
    v = d.run(second_half, [mid], parts, v, below, above, *statics, lines_z1)
    below, above = d.beside("py", v, v)
    every = d.run(middle_scaled, [(N_PX, MX, MZ)], v, below, above, *statics)
    every = d.swap("px", every, N_PX)
    every = d.local(lambda a: a.reshape(MX * N_PX, MZ), every)
    v = d.run(solve_x_middle, [mid], every, rows_x1, v)

    below, above = d.beside("py", v, v)
    u, lower, upper = d.run(
        to_fine,
        [(2, FE, FZ), (FX, FZ), (FX, FZ)],
        v, below, above, u_ext, f_ext, r_ext, cx_ext, sy, cz, lines_z0,
    )
    below, above = d.beside("py", lower, upper)
    slabs = d.run(last_scaled, [slab], u, below, above, f_ext, r_ext, cx_ext, sy, cz)
    slabs = d.swap("px", slabs, 8)
    slabs = d.run(solve_x_fine, [slab], slabs, block)
    slabs = d.swap("px", slabs, 8)
    return d.run(finish, [(FX, 2, FZ)], u, slabs)


def solution(mesh):
    placed = (
        P("px", "py", None),
        P("px", "py", None),
        P("px"),
        P("py"),
        P(),
        P(),
        P(),
        P(),
        P(),
        P(("py", "px"), None),
    )

    def step(*args):
        return cycle(Device(), *args)

    return jax.shard_map(
        step, mesh=mesh, in_specs=placed, out_specs=P("px", "py", None), check_vma=False
    )
```

```python
import jax
import jax.numpy as jnp
from jax import lax
from jax.experimental import pallas as pl
from jax.experimental.pallas import tpu as pltpu
from jax.sharding import PartitionSpec as P


shift_term = 0.1
f32 = jnp.float32
bf16 = jnp.bfloat16

N_PY, N_PX = 16, 32
FX, FZ = 32, 1024
MX, MZ = 16, 512
FH, MH = 8, 4
FE, ME = FX + 2 * FH, MX + 2 * MH


def roll(v, shift, axis):
    return pltpu.roll(v, shift % v.shape[axis], axis)


def dyn(ref, start, size):
    return ref[pl.ds(pl.multiple_of(start, 8), size), :]


def halves(a):
    high = a.astype(bf16)
    return high, (a - high.astype(f32)).astype(bf16)


def thirds(a):
    high, rest = a.astype(bf16), None
    rest = a - high.astype(f32)
    middle = rest.astype(bf16)
    return high, middle, (rest - middle.astype(f32)).astype(bf16)


def product(a, b, dims):
    return lax.dot_general(a, b, (dims, ((), ())), preferred_element_type=f32)


def dot(a, b, dims=((1,), (0,))):
    a_high, a_low = halves(a)
    b_high, b_low = halves(b)
    return product(a_high, b_high, dims) + (product(a_high, b_low, dims) + product(a_low, b_high, dims))


def pick_right(a, weight):
    dims = ((1,), (0,))
    w = weight.astype(bf16)
    high, middle, low = thirds(a)
    return product(high, w, dims) + (product(middle, w, dims) + product(low, w, dims))


def pick_left(weight, a):
    dims = ((1,), (0,))
    w = weight.astype(bf16)
    high, middle, low = thirds(a)
    return product(w, high, dims) + (product(w, middle, dims) + product(w, low, dims))


def iota(shape, axis):
    return lax.broadcasted_iota(jnp.int32, shape, axis)


def rows_of(rows):
    at = iota((8, rows[0].shape[1]), 0)
    total = jnp.zeros((8, rows[0].shape[1]), f32)
    for i, row in enumerate(rows):
        total = jnp.where(at == i, row, total)
    return total


def rows_at(pairs):
    at = iota((8, pairs[0][1].shape[1]), 0)
    total = jnp.zeros((8, pairs[0][1].shape[1]), f32)
    for i, row in pairs:
        total = jnp.where(at == i, row, total)
    return total


def near_z(v):
    lane = iota(v.shape, 1)
    last = v.shape[1] - 1
    below = jnp.where(lane == 0, 0.0, roll(v, 1, 1))
    above = jnp.where(lane == last, 0.0, roll(v, -1, 1))
    return below + above


def near_x(v):
    return roll(v, 1, 0) + roll(v, -1, 0)


def operate(v, v_near_x, v_near_y, rho, cx, cy, cz):
    twice = 2.0 * v
    stencil = cx * (twice - v_near_x) + cy * (twice - v_near_y) + cz * (twice - near_z(v))
    return shift_term * v + rho * stencil


def diagonal(rho, cx, cy, cz):
    return shift_term + 2.0 * rho * (cx + cy + cz)


def solve_z(w, lines):
    count, size = lines.shape[0], lines.shape[1]
    parts = []
    for k in range(count):
        parts.append(dot(w[:, k * size : (k + 1) * size], lines[k], ((1,), (1,))))
    return jnp.concatenate(parts, axis=1)


def columns_by(v, pick):
    cuts = [slice(256 * k, 256 * (k + 1)) for k in range(v.shape[1] // 256)]
    return jnp.concatenate([pick_right(v[:, cut], pick) for cut in cuts], axis=1)


def pair_columns(v, scale):
    fine, coarse = iota((256, 128), 0), iota((256, 128), 1)
    return columns_by(v, jnp.where(fine // 2 == coarse, scale, 0.0))


def even_columns(v, scale):
    fine, coarse = iota((256, 128), 0), iota((256, 128), 1)
    return columns_by(v, jnp.where(fine == 2 * coarse, scale, 0.0))


def restrict_columns(v):
    lane = iota(v.shape, 1)
    last = v.shape[1] - 1
    one = jnp.where(lane == last, 0.0, roll(v, -1, 1))
    two = jnp.where(lane >= last - 1, 0.0, roll(v, -2, 1))
    below = jnp.where(lane == 0, 0.0, roll(v, 1, 1))
    return even_columns(below + 3.0 * v + 3.0 * one + two, 0.125)


def raise_columns(v):
    lane = iota(v.shape, 1)
    last = v.shape[1] - 1
    below = jnp.where(lane == 0, 0.0, roll(v, 1, 1))
    above = jnp.where(lane == last, 0.0, roll(v, -1, 1))
    even = 3.0 * v + below
    odd = 3.0 * v + above
    coarse, fine = iota((128, 256), 0), iota((128, 256), 1)
    at_even = jnp.where(fine == 2 * coarse, 0.25, 0.0)
    at_odd = jnp.where(fine == 2 * coarse + 1, 0.25, 0.0)
    parts = []
    for k in range(v.shape[1] // 128):
        cut = slice(128 * k, 128 * (k + 1))
        parts.append(pick_right(even[:, cut], at_even) + pick_right(odd[:, cut], at_odd))
    return jnp.concatenate(parts, axis=1)


def restrict_rows(v):
    coarse, fine = iota((ME, FE), 0), iota((ME, FE), 1)
    away = fine - 2 * coarse
    weight = jnp.where((away == 0) | (away == 1), 0.375, 0.0)
    weight = weight + jnp.where((away == -1) | (away == 2), 0.125, 0.0)
    return pick_left(weight, v)


def pair_rows(v):
    coarse, fine = iota((ME, FE), 0), iota((ME, FE), 1)
    return pick_left(jnp.where(fine // 2 == coarse, 1.0, 0.0), v)


def raise_rows(v):
    fine, coarse = iota((FE, ME), 0), iota((FE, ME), 1)
    away = fine - 2 * coarse
    weight = jnp.where((away == 0) | (away == 1), 0.75, 0.0)
    weight = weight + jnp.where((away == 2) | (away == -1), 0.25, 0.0)
    return pick_left(weight, v)


def inside_middle(px):
    row = iota((ME, MZ), 0) + MX * px - MH
    return (row >= 0) & (row < MX * N_PX)


def inside_fine(px):
    row = iota((FE, FZ), 0) + FX * px - FH
    return (row >= 0) & (row < FX * N_PX)


def to_slabs(plane, out, at):
    for m in range(8):
        out[m, at] = plane[:, 128 * m : 128 * (m + 1)]


def from_slabs(ref, at):
    return jnp.concatenate([ref[m, at] for m in range(8)], axis=1)


def start(px, py, forcing, inv_density, sx, sy, force, rho, lower, upper, low, high, cx):
    square = iota((FX, FX), 0) == iota((FX, FX), 1)
    column = jnp.sum(jnp.where(square, sx[...], 0.0), axis=1, keepdims=True)
    cx[...] = jnp.broadcast_to(column, (FX, 128))
    wide = jnp.broadcast_to(column, (FX, FZ))
    edges = {}
    for at, out in ((0, lower), (1, upper)):
        f_plane, r_plane = forcing[:, at, :], inv_density[:, at, :]
        force[at] = f_plane
        rho[at] = r_plane
        out[0:32] = f_plane
        out[32:64] = r_plane
        out[64:72] = jnp.broadcast_to(sy[0:1, at : at + 1], (8, FZ))
        for row in (0, FX - 1):
            edges[at, row] = (f_plane[row : row + 1], r_plane[row : row + 1])
    for side, row, cut in ((low, 0, slice(0, 8)), (high, FX - 1, slice(24, 32))):
        for k in range(2):
            side[8 * k : 8 * k + 8] = rows_of([edges[0, row][k], edges[1, row][k]])
        side[16:24] = wide[cut]


def own_lines(px, py, force, rho, cx, sy, cz, lines, u):
    parts = []
    for at in range(2):
        parts.append(force[at] / diagonal(rho[at], cx[:, 0:1], sy[0:1, at : at + 1], cz[...]))
    solved = solve_z(jnp.concatenate(parts, axis=0), lines)
    u[0] = solved[0:FX]
    u[1] = solved[FX : 2 * FX]


def first_half(px, py, force, rho, cx, sy, cz, u, below, above, left, right, lines, slabs):
    cx_col = cx[:, 0:1]
    cz_row = cz[...]
    parts = []
    for side in (below, above):
        parts.append(side[0:32] / diagonal(side[32:64], cx_col, side[64:65], cz_row))
    cy_edge = jnp.where(iota((8, 1), 0) == 0, sy[0:1, 0:1], sy[0:1, 1:2])
    for side, row in ((left, 23), (right, 16)):
        parts.append(side[0:8] / diagonal(side[8:16], side[row : row + 1, 0:1], cy_edge, cz_row))
    solved = solve_z(jnp.concatenate(parts, axis=0), lines)
    planes = [solved[0:32], u[0], u[1], solved[32:64]]
    for at in range(2):
        own = u[at]
        before = rows_at([(7, solved[64 + at : 65 + at])])
        after = rows_at([(0, solved[72 + at : 73 + at])])
        beside_x = near_x(jnp.concatenate([before, own, after], axis=0))[FH : FH + FX]
        beside_y = planes[at] + planes[at + 2]
        cy = sy[0:1, at : at + 1]
        applied = operate(own, beside_x, beside_y, rho[at], cx_col, cy, cz_row)
        to_slabs((force[at] - applied) / diagonal(rho[at], cx_col, cy, cz_row), slabs, at)


def middle_statics(px, py, rho, cx, sy, cz, left, right, column, cx_mid, cyz_mid, told):
    coarse, fine = iota((MX, FX), 0), iota((MX, FX), 1)
    pairs = pick_left(jnp.where(fine // 2 == coarse, 1.0, 0.0), rho[0] + rho[1])
    own = pair_columns(pairs, 0.125)
    columns = jnp.concatenate([left[16:24, 0:128], cx[...], right[16:24, 0:128]], axis=0)
    cym = jnp.broadcast_to((sy[0:1, 0:1] + sy[0:1, 1:2]) * 0.125, (8, MZ))
    czm = pair_columns(jnp.broadcast_to(cz[...], (16, FZ)), 0.125)
    cx_mid[...] = pair_rows(columns) * 0.125
    cyz_mid[...] = jnp.concatenate([czm[0:1], cym[0:7]], axis=0)
    told[0:8, 0:MZ] = own[0:8]
    told[0:8, MZ:FZ] = own[8:16]
    for k in range(4):
        told[8:16, 128 * k : 128 * (k + 1)] = column[8 * k : 8 * (k + 1)]
    told[8:16, MZ:FZ] = cym


def solve_x_fine(px, py, slabs, lines, out):
    block = lines[0]
    for at in range(2):
        column = jnp.concatenate([slabs[m, at] for m in range(8)], axis=0)
        solved = dot(block, column)
        for m in range(8):
            out[m, at] = solved[32 * m : 32 * (m + 1)]


def add_slabs(px, py, u, slabs, told, out):
    for at in range(2):
        out[FX * at : FX * (at + 1)] = u[at] + from_slabs(slabs, at)
    out[64:80] = told[...]


def half_residual(px, py, u, below, above, force, rho, y_below, y_above, cx, sy, cz, q, low, high):
    cx_col = cx[...][:, 0:1]
    cz_row = cz[...]
    us = [below[0:32], below[32:64], u[0:32], u[32:64], above[0:32], above[32:64]]
    fs = [y_below[0:32], force[0], force[1], y_above[0:32]]
    rs = [y_below[32:64], rho[0], rho[1], y_above[32:64]]
    cys = [y_below[64:65], sy[0:1, 0:1], sy[0:1, 1:2], y_above[64:65]]
    row = iota((FX, FZ), 0)
    total = None
    for j in range(4):
        own = us[j + 1]
        beside_x = jnp.where(row == 0, 0.0, roll(own, 1, 0)) + jnp.where(row == FX - 1, 0.0, roll(own, -1, 0))
        left_over = fs[j] - operate(own, beside_x, us[j] + us[j + 2], rs[j], cx_col, cys[j], cz_row)
        if j in (1, 2):
            left_over = 3.0 * left_over
        total = left_over if total is None else total + left_over
    total = total * 0.125
    q[...] = total
    for out, edge, step, cut in ((low, 0, 1, slice(0, 8)), (high, FX - 1, -1, slice(24, 32))):
        out[0:8] = total[cut]
        next_row = edge + step
        picked = [us[j + 1][edge : edge + 1] for j in range(4)]
        out[8:16] = rows_of(picked + [us[j + 1][next_row : next_row + 1] for j in range(4)])
        out[16:24] = rows_of([rs[j][edge : edge + 1] for j in range(4)])
        out[24:32, 0:MZ] = u[72:80, 0:MZ]
        out[24:32, MZ:FZ] = u[64:72, 0:MZ] if edge == 0 else u[64:72, MZ:FZ]


def to_middle(px, py, q, u, below, above, left, right, force, rho, y_below, y_above, x_left, x_right, cx, cx_mid, cyz_mid, lines, u_ext, f_ext, r_ext, cx_ext, r_mid, f_mid, v_out, told):
    columns = jnp.concatenate([x_left[16:24, 0:128], cx[...], x_right[16:24, 0:128]], axis=0)
    cx_ext[...] = columns
    told[0:16] = below[64:80]
    told[16:32] = above[64:80]
    told[32:40] = right[24:32]
    told[40:48] = left[24:32]
    us = [below[32:64], u[0:32], u[32:64], above[0:32]]
    rs = [y_below[32:64], rho[0], rho[1], y_above[32:64]]
    cross = []
    for side, row in ((left, 0), (right, FX - 1)):
        inward = outward = None
        for j in range(4):
            weight = 0.375 if j in (1, 2) else 0.125
            here = weight * rs[j][row : row + 1] * side[8 + j : 9 + j]
            there = weight * side[16 + j : 17 + j] * us[j][row : row + 1]
            inward = here if inward is None else inward + here
            outward = there if outward is None else outward + there
        at = FH + row
        beyond = at - 1 if row == 0 else at + 1
        cross.append((at, inward * columns[at : at + 1, 0:1]))
        cross.append((beyond, outward * columns[beyond : beyond + 1, 0:1]))
    total = jnp.concatenate([left[0:8], q[...], right[0:8]], axis=0)
    line = iota((FE, FZ), 0)
    for at, term in cross:
        total = total + jnp.where(line == at, term, 0.0)
    for j in range(4):
        before = rows_at([(7, left[8 + j : 9 + j]), (6, left[12 + j : 13 + j])])
        after = rows_at([(0, right[8 + j : 9 + j]), (1, right[12 + j : 13 + j])])
        u_ext[j] = jnp.concatenate([before, us[j], after], axis=0)
    for at in range(2):
        for k, own, out in ((0, force, f_ext), (8, rho, r_ext)):
            before = rows_at([(7, x_left[k + at : k + at + 1])])
            after = rows_at([(0, x_right[k + at : k + at + 1])])
            out[at] = jnp.concatenate([before, own[at], after], axis=0)
    dense = [left[24:32, MZ:FZ], u[64:72, 0:MZ], u[64:72, MZ:FZ], right[24:32, MZ:FZ]]
    r_mid[...] = roll(jnp.concatenate(dense, axis=0), MH - 8, 0)[0:ME]
    rhs = restrict_columns(restrict_rows(total))
    rhs = jnp.where(inside_middle(px), rhs, 0.0)
    f_mid[...] = rhs
    diag = diagonal(*middle_parts(r_mid, cx_mid, cyz_mid))
    v_out[...] = solve_z(rhs / diag, lines)


def middle_parts(r_mid, cx_mid, cyz_mid):
    return r_mid[...], cx_mid[:, 0:1], cyz_mid[1:2], cyz_mid[0:1]


def middle_scaled(px, py, v, below, above, f_mid, r_mid, cx_mid, cyz_mid, out):
    rho, cx, cy, cz = middle_parts(r_mid, cx_mid, cyz_mid)
    own = v[...]
    applied = operate(own, near_x(own), below[...] + above[...], rho, cx, cy, cz)
    scaled = (f_mid[...] - applied) / diagonal(rho, cx, cy, cz)
    part = roll(scaled, -MH, 0)[0:MX]
    for i in range(out.shape[0]):
        out[i] = part


def solve_x_middle(px, py, gathered, lines, v, out):
    total = MX * N_PX
    pieces = []
    starts = (
        (jnp.maximum(MX * px - 8, 0), 8),
        (MX * px, MX),
        (jnp.minimum(MX * px + MX, total - 8), 8),
    )
    for start, size in starts:
        rows = dyn(lines, start, size)
        block = (start // 256) * 256
        pieces.append(dot(rows, dyn(gathered, block, 256)))
    full = jnp.concatenate(pieces, axis=0)
    part = roll(full, MH - 8, 0)[0:ME]
    out[...] = v[...] + jnp.where(inside_middle(px), part, 0.0)


def solve_x_block(px, py, gathered, lines, v, out):
    total = MX * N_PX
    pieces = []
    starts = (
        (jnp.maximum(MX * px - 8, 0), 8),
        (MX * px, MX),
        (jnp.minimum(MX * px + MX, total - 8), 8),
    )
    for start, size in starts:
        pieces.append(dyn(lines, start, size))
    full = dot(jnp.concatenate(pieces, axis=0), gathered[...])
    part = roll(full, MH - 8, 0)[0:ME]
    row = iota((ME, MZ), 0) + MX * px - MH
    first = 256 * (px // 16)
    held = (row >= first) & (row < first + 256)
    out[...] = jnp.where(held, v[...] + part, 0.0)


def mend(px, py, v, other, out):
    row = iota((ME, MZ), 0)
    theirs = other[...]
    up = jnp.where((row >= MH + MX) & (px == 15), roll(theirs, MX, 0), 0.0)
    down = jnp.where((row < MH) & (px == 16), roll(theirs, -MX, 0), 0.0)
    out[...] = v[...] + (up + down)


def block_mean(px, py, v, f_mid, r_mid, cx_mid, cyz_mid, told, column, out):
    rho, cx, cy, cz = middle_parts(r_mid, cx_mid, cyz_mid)
    own = v[...]
    applied = operate(own, near_x(own), 0.0, rho, cx, cy, cz)
    row = iota((ME, MZ), 0)
    kept = jnp.where((row >= MH) & (row < MH + MX), f_mid[...] - applied, 0.0)

    def mean(a):
        return jnp.sum(jnp.sum(a, axis=0, keepdims=True), axis=1, keepdims=True) * (1.0 / (MX * MZ))

    sent = column[...] * mean(kept)
    inner = roll(own, -MH, 0)[0:MX]
    for at in (0, 16):
        share = mean(told[at : at + 8, 0:MZ] * inner[0:8] + told[at : at + 8, MZ:FZ] * inner[8:16])
        share = share * told[at + 8 : at + 9, MZ : MZ + 1]
        theirs = [told[at + 8 : at + 16, 128 * k : 128 * (k + 1)] for k in range(4)]
        sent = sent + jnp.concatenate(theirs, axis=0) * share
    for at, edge, inner_row, mine in ((32, MH + MX, MH + MX - 1, px == 15), (40, MH - 1, MH, px == 16)):
        line = r_mid[edge : edge + 1] * cx_mid[edge : edge + 1, 0:1] * v[inner_row : inner_row + 1]
        share = jnp.where(mine, mean(line), 0.0)
        theirs = [told[at : at + 8, 128 * k : 128 * (k + 1)] for k in range(4)]
        sent = sent + jnp.concatenate(theirs, axis=0) * share
    for i in range(N_PX):
        out[i] = jnp.broadcast_to(sent[i : i + 1], (8, 128))


def sum_x(px, py, parts, out):
    total = parts[0]
    for i in range(1, N_PX):
        total = total + parts[i]
    for j in range(N_PY):
        out[j] = total


def second_half(px, py, parts, v, below, above, f_mid, r_mid, cx_mid, cyz_mid, lines, out):
    total = parts[0]
    for j in range(1, N_PY):
        total = total + parts[j]
    lane = iota((8, 128), 1)
    row = iota((ME, MZ), 0)

    def raised(plane, dy):
        held = (py + dy >= 0) & (py + dy < N_PY)
        at = []
        for dx in range(3):
            wanted = (lane == dx * N_PY + py + dy) & held
            found = jnp.sum(jnp.where(wanted, total, 0.0), axis=1, keepdims=True)[0:1]
            at.append(found)
        return plane + jnp.where(row < MH, at[0], jnp.where(row < MH + MX, at[1], at[2]))

    own = raised(v[...], 0)
    beside = raised(below[...], -1) + raised(above[...], 1)
    rho, cx, cy, cz = middle_parts(r_mid, cx_mid, cyz_mid)
    applied = operate(own, near_x(own), beside, rho, cx, cy, cz)
    out[...] = own + solve_z((f_mid[...] - applied) / diagonal(rho, cx, cy, cz), lines)


def to_fine(px, py, v, below, above, u_ext, f_ext, r_ext, cx_ext, sy, cz, lines, out, lower, upper):
    rows = [raise_rows(p[...]) for p in (below, v, above)]
    columns = raise_columns(jnp.concatenate(rows, axis=0)) * 0.25
    raised = [columns[FE * i : FE * (i + 1)] for i in range(3)]
    mids = [
        3.0 * raised[0] + raised[1],
        3.0 * raised[1] + raised[0],
        3.0 * raised[1] + raised[2],
        3.0 * raised[2] + raised[1],
    ]
    inside = inside_fine(px)
    us = []
    for j in range(4):
        held = inside
        if j == 0:
            held = inside & (py > 0)
        if j == 3:
            held = inside & (py < N_PY - 1)
        us.append(u_ext[j] + jnp.where(held, mids[j], 0.0))
    cx_col = cx_ext[:, 0:1]
    cz_row = cz[...]
    parts = []
    for at in range(2):
        own = us[at + 1]
        cy = sy[0:1, at : at + 1]
        applied = operate(own, near_x(own), us[at] + us[at + 2], r_ext[at], cx_col, cy, cz_row)
        parts.append((f_ext[at] - applied) / diagonal(r_ext[at], cx_col, cy, cz_row))
    solved = solve_z(jnp.concatenate(parts, axis=0), lines)
    for at in range(2):
        new = us[at + 1] + solved[FE * at : FE * (at + 1)]
        out[at] = new
        (lower if at == 0 else upper)[...] = new[FH : FH + FX]


def last_scaled(px, py, u, below, above, f_ext, r_ext, cx_ext, sy, cz, slabs):
    cx_col = cx_ext[FH : FH + FX, 0:1]
    cz_row = cz[...]
    inner = slice(FH, FH + FX)
    for at in range(2):
        full = u[at]
        beside_x = near_x(full)[inner]
        own = full[inner]
        beside_y = (below[...] if at == 0 else u[0, inner]) + (above[...] if at == 1 else u[1, inner])
        rho = r_ext[at, inner]
        cy = sy[0:1, at : at + 1]
        applied = operate(own, beside_x, beside_y, rho, cx_col, cy, cz_row)
        scaled = (f_ext[at, inner] - applied) / diagonal(rho, cx_col, cy, cz_row)
        to_slabs(scaled, slabs, at)


def finish(px, py, u, slabs, out):
    for at in range(2):
        out[:, at, :] = u[at, FH : FH + FX] + from_slabs(slabs, at)


class Device:
    def run(self, stage, shapes, *args):
        def kernel(*refs):
            stage(lax.axis_index("px"), lax.axis_index("py"), *refs)

        whole = pl.BlockSpec(memory_space=pltpu.VMEM)
        outs = pl.pallas_call(
            kernel,
            out_shape=[jax.ShapeDtypeStruct(s, f32) for s in shapes],
            in_specs=[whole] * len(args),
            out_specs=[whole] * len(shapes),
            compiler_params=pltpu.CompilerParams(vmem_limit_bytes=24 * 1024 * 1024),
        )(*args)
        return outs if len(shapes) > 1 else outs[0]

    def local(self, fn, *args):
        return fn(*args)

    def block_of(self, lines):
        at = lax.axis_index("px") // 8
        return lax.dynamic_slice_in_dim(lines, at, 1, axis=0)

    def beside(self, axis, low, high):
        n = lax.axis_size(axis)
        up = [(i, i + 1) for i in range(n - 1)]
        down = [(j, i) for i, j in up]
        return lax.ppermute(high, axis, up), lax.ppermute(low, axis, down)

    def across(self, array):
        return lax.ppermute(array, "px", [(15, 16), (16, 15)])

    def swap(self, axis, array, group):
        n = lax.axis_size(axis)
        groups = None
        if group < n:
            groups = [list(range(k, k + group)) for k in range(0, n, group)]
        return lax.all_to_all(array, axis, 0, 0, axis_index_groups=groups, tiled=True)


def arrange_column(coarse):
    table = coarse.reshape(N_PY, N_PX).T
    none = jnp.zeros((1, N_PY), f32)
    before = jnp.concatenate([none, table[:-1]], axis=0)
    after = jnp.concatenate([table[1:], none], axis=0)
    return jnp.concatenate([before, table, after, jnp.zeros((N_PX, 128 - 3 * N_PY), f32)], axis=1)


def cycle(d, forcing, inv_density, stretch_x, stretch_y, stretch_z, lines_z0, lines_x0, lines_z1, lines_x1, coarse_inverse):
    sx = d.local(lambda a: a.reshape(1, FX), stretch_x)
    sy = d.local(lambda a: a.reshape(1, 2), stretch_y)
    cz = d.local(lambda a: a.reshape(1, FZ), stretch_z)
    rows_x1 = d.local(lambda a: a.reshape(MX * N_PX, 256), lines_x1)
    slab, own, mid = (8, 2, FX, 128), (2, FX, FZ), (ME, MZ)

    force, rho, lower, upper, low, high, cx = d.run(
        start,
        [own, own, (72, FZ), (72, FZ), (24, FZ), (24, FZ), (FX, 128)],
        forcing, inv_density, sx, sy,
    )
    y_below, y_above = d.beside("py", lower, upper)
    x_left, x_right = d.beside("px", low, high)
    column = d.local(arrange_column, coarse_inverse)
    block = d.block_of(lines_x0)
    u = d.run(own_lines, [own], force, rho, cx, sy, cz, lines_z0)
    slabs = d.run(
        first_half, [slab],
        force, rho, cx, sy, cz, u, y_below, y_above, x_left, x_right, lines_z0,
    )
    slabs = d.swap("px", slabs, 8)
    cx_mid, cyz_mid, told = d.run(
        middle_statics,
        [(ME, 128), (8, MZ), (16, FZ)],
        rho, cx, sy, cz, x_left, x_right, column,
    )
    slabs = d.run(solve_x_fine, [slab], slabs, block)
    slabs = d.swap("px", slabs, 8)
    u = d.run(add_slabs, [(80, FZ)], u, slabs, told)
    below, above = d.beside("py", u, u)
    q, low, high = d.run(
        half_residual, [(FX, FZ)] * 3,
        u, below, above, force, rho, y_below, y_above, cx, sy, cz,
    )
    left, right = d.beside("px", low, high)
    u_ext, f_ext, r_ext, cx_ext, r_mid, f_mid, v, told = d.run(
        to_middle,
        [(4, FE, FZ), (2, FE, FZ), (2, FE, FZ), (FE, 128), mid, mid, mid, (48, FZ)],
        q, u, below, above, left, right, force, rho, y_below, y_above, x_left, x_right,
        cx, cx_mid, cyz_mid, lines_z1,
    )
    statics = (f_mid, r_mid, cx_mid, cyz_mid)

    below, above = d.beside("py", v, v)
    every = d.run(middle_scaled, [(16, MX, MZ)], v, below, above, *statics)
    every = d.swap("px", every, 16)
    every = d.local(lambda a: a.reshape(256, MZ), every)
    v = d.run(solve_x_block, [mid], every, rows_x1, v)
    other = d.across(v)
    sent = d.run(block_mean, [(N_PX, 8, 128)], v, *statics, told, column)
    parts = d.swap("px", sent, N_PX)
    v = d.run(mend, [mid], v, other)
    below, above = d.beside("py", v, v)
    parts = d.run(sum_x, [(N_PY, 8, 128)], parts)
    parts = d.swap("py", parts, N_PY)
    v = d.run(second_half, [mid], parts, v, below, above, *statics, lines_z1)
    below, above = d.beside("py", v, v)
    every = d.run(middle_scaled, [(N_PX, MX, MZ)], v, below, above, *statics)
    every = d.swap("px", every, N_PX)
    every = d.local(lambda a: a.reshape(MX * N_PX, MZ), every)
    v = d.run(solve_x_middle, [mid], every, rows_x1, v)

    below, above = d.beside("py", v, v)
    u, lower, upper = d.run(
        to_fine,
        [(2, FE, FZ), (FX, FZ), (FX, FZ)],
        v, below, above, u_ext, f_ext, r_ext, cx_ext, sy, cz, lines_z0,
    )
    below, above = d.beside("py", lower, upper)
    slabs = d.run(last_scaled, [slab], u, below, above, f_ext, r_ext, cx_ext, sy, cz)
    slabs = d.swap("px", slabs, 8)
    slabs = d.run(solve_x_fine, [slab], slabs, block)
    slabs = d.swap("px", slabs, 8)
    return d.run(finish, [(FX, 2, FZ)], u, slabs)


def solution(mesh):
    placed = (
        P("px", "py", None),
        P("px", "py", None),
        P("px"),
        P("py"),
        P(),
        P(),
        P(),
        P(),
        P(),
        P(("py", "px"), None),
    )

    def step(*args):
        return cycle(Device(), *args)

    return jax.shard_map(
        step, mesh=mesh, in_specs=placed, out_specs=P("px", "py", None), check_vma=False
    )
```

```python
import jax
import jax.numpy as jnp
from jax import lax
from jax.experimental import pallas as pl
from jax.experimental.pallas import tpu as pltpu
from jax.sharding import PartitionSpec as P


shift_term = 0.1
f32 = jnp.float32
bf16 = jnp.bfloat16

N_PY, N_PX = 16, 32
FX, FZ = 32, 1024
MX, MZ = 16, 512
FH, MH = 8, 4
FE, ME = FX + 2 * FH, MX + 2 * MH


def roll(v, shift, axis):
    return pltpu.roll(v, shift % v.shape[axis], axis)


def dyn(ref, start, size):
    return ref[pl.ds(pl.multiple_of(start, 8), size), :]


def halves(a):
    high = a.astype(bf16)
    return high, (a - high.astype(f32)).astype(bf16)


def thirds(a):
    high, rest = a.astype(bf16), None
    rest = a - high.astype(f32)
    middle = rest.astype(bf16)
    return high, middle, (rest - middle.astype(f32)).astype(bf16)


def product(a, b, dims):
    return lax.dot_general(a, b, (dims, ((), ())), preferred_element_type=f32)


def dot(a, b, dims=((1,), (0,))):
    a_high, a_low = halves(a)
    b_high, b_low = halves(b)
    return product(a_high, b_high, dims) + (product(a_high, b_low, dims) + product(a_low, b_high, dims))


def pick_right(a, weight):
    dims = ((1,), (0,))
    w = weight.astype(bf16)
    high, middle, low = thirds(a)
    return product(high, w, dims) + (product(middle, w, dims) + product(low, w, dims))


def pick_left(weight, a):
    dims = ((1,), (0,))
    w = weight.astype(bf16)
    high, middle, low = thirds(a)
    return product(w, high, dims) + (product(w, middle, dims) + product(w, low, dims))


def iota(shape, axis):
    return lax.broadcasted_iota(jnp.int32, shape, axis)


def rows_of(rows):
    at = iota((8, rows[0].shape[1]), 0)
    total = jnp.zeros((8, rows[0].shape[1]), f32)
    for i, row in enumerate(rows):
        total = jnp.where(at == i, row, total)
    return total


def rows_at(pairs):
    at = iota((8, pairs[0][1].shape[1]), 0)
    total = jnp.zeros((8, pairs[0][1].shape[1]), f32)
    for i, row in pairs:
        total = jnp.where(at == i, row, total)
    return total


def near_z(v):
    lane = iota(v.shape, 1)
    last = v.shape[1] - 1
    below = jnp.where(lane == 0, 0.0, roll(v, 1, 1))
    above = jnp.where(lane == last, 0.0, roll(v, -1, 1))
    return below + above


def near_x(v):
    return roll(v, 1, 0) + roll(v, -1, 0)


def operate(v, v_near_x, v_near_y, rho, cx, cy, cz):
    twice = 2.0 * v
    stencil = cx * (twice - v_near_x) + cy * (twice - v_near_y) + cz * (twice - near_z(v))
    return shift_term * v + rho * stencil


def diagonal(rho, cx, cy, cz):
    return shift_term + 2.0 * rho * (cx + cy + cz)


def solve_z(w, lines):
    count, size = lines.shape[0], lines.shape[1]
    parts = []
    for k in range(count):
        parts.append(dot(w[:, k * size : (k + 1) * size], lines[k], ((1,), (1,))))
    return jnp.concatenate(parts, axis=1)


def columns_by(v, pick):
    cuts = [slice(256 * k, 256 * (k + 1)) for k in range(v.shape[1] // 256)]
    return jnp.concatenate([pick_right(v[:, cut], pick) for cut in cuts], axis=1)


def pair_columns(v, scale):
    fine, coarse = iota((256, 128), 0), iota((256, 128), 1)
    return columns_by(v, jnp.where(fine // 2 == coarse, scale, 0.0))


def even_columns(v, scale):
    fine, coarse = iota((256, 128), 0), iota((256, 128), 1)
    return columns_by(v, jnp.where(fine == 2 * coarse, scale, 0.0))


def restrict_columns(v):
    lane = iota(v.shape, 1)
    last = v.shape[1] - 1
    one = jnp.where(lane == last, 0.0, roll(v, -1, 1))
    two = jnp.where(lane >= last - 1, 0.0, roll(v, -2, 1))
    below = jnp.where(lane == 0, 0.0, roll(v, 1, 1))
    return even_columns(below + 3.0 * v + 3.0 * one + two, 0.125)


def raise_columns(v):
    lane = iota(v.shape, 1)
    last = v.shape[1] - 1
    below = jnp.where(lane == 0, 0.0, roll(v, 1, 1))
    above = jnp.where(lane == last, 0.0, roll(v, -1, 1))
    even = 3.0 * v + below
    odd = 3.0 * v + above
    coarse, fine = iota((128, 256), 0), iota((128, 256), 1)
    at_even = jnp.where(fine == 2 * coarse, 0.25, 0.0)
    at_odd = jnp.where(fine == 2 * coarse + 1, 0.25, 0.0)
    parts = []
    for k in range(v.shape[1] // 128):
        cut = slice(128 * k, 128 * (k + 1))
        parts.append(pick_right(even[:, cut], at_even) + pick_right(odd[:, cut], at_odd))
    return jnp.concatenate(parts, axis=1)


def restrict_rows(v):
    coarse, fine = iota((ME, FE), 0), iota((ME, FE), 1)
    away = fine - 2 * coarse
    weight = jnp.where((away == 0) | (away == 1), 0.375, 0.0)
    weight = weight + jnp.where((away == -1) | (away == 2), 0.125, 0.0)
    return pick_left(weight, v)


def pair_rows(v):
    coarse, fine = iota((ME, FE), 0), iota((ME, FE), 1)
    return pick_left(jnp.where(fine // 2 == coarse, 1.0, 0.0), v)


def raise_rows(v):
    fine, coarse = iota((FE, ME), 0), iota((FE, ME), 1)
    away = fine - 2 * coarse
    weight = jnp.where((away == 0) | (away == 1), 0.75, 0.0)
    weight = weight + jnp.where((away == 2) | (away == -1), 0.25, 0.0)
    return pick_left(weight, v)


def inside_middle(px):
    row = iota((ME, MZ), 0) + MX * px - MH
    return (row >= 0) & (row < MX * N_PX)


def inside_fine(px):
    row = iota((FE, FZ), 0) + FX * px - FH
    return (row >= 0) & (row < FX * N_PX)


def to_slabs(plane, out, at):
    for m in range(8):
        out[m, at] = plane[:, 128 * m : 128 * (m + 1)]


def from_slabs(ref, at):
    return jnp.concatenate([ref[m, at] for m in range(8)], axis=1)


def start(px, py, forcing, inv_density, sx, sy, force, rho, lower, upper, low, high, cx):
    square = iota((FX, FX), 0) == iota((FX, FX), 1)
    column = jnp.sum(jnp.where(square, sx[...], 0.0), axis=1, keepdims=True)
    cx[...] = jnp.broadcast_to(column, (FX, 128))
    wide = jnp.broadcast_to(column, (FX, FZ))
    edges = {}
    for at, out in ((0, lower), (1, upper)):
        f_plane, r_plane = forcing[:, at, :], inv_density[:, at, :]
        force[at] = f_plane
        rho[at] = r_plane
        out[0:32] = f_plane
        out[32:64] = r_plane
        out[64:72] = jnp.broadcast_to(sy[0:1, at : at + 1], (8, FZ))
        for row in (0, FX - 1):
            edges[at, row] = (f_plane[row : row + 1], r_plane[row : row + 1])
    for side, row, cut in ((low, 0, slice(0, 8)), (high, FX - 1, slice(24, 32))):
        for k in range(2):
            side[8 * k : 8 * k + 8] = rows_of([edges[0, row][k], edges[1, row][k]])
        side[16:24] = wide[cut]


def own_lines(px, py, force, rho, cx, sy, cz, lines, u):
    parts = []
    for at in range(2):
        parts.append(force[at] / diagonal(rho[at], cx[:, 0:1], sy[0:1, at : at + 1], cz[...]))
    solved = solve_z(jnp.concatenate(parts, axis=0), lines)
    u[0] = solved[0:FX]
    u[1] = solved[FX : 2 * FX]


def first_half(px, py, force, rho, cx, sy, cz, u, below, above, left, right, lines, slabs):
    cx_col = cx[:, 0:1]
    cz_row = cz[...]
    parts = []
    for side in (below, above):
        parts.append(side[0:32] / diagonal(side[32:64], cx_col, side[64:65], cz_row))
    cy_edge = jnp.where(iota((8, 1), 0) == 0, sy[0:1, 0:1], sy[0:1, 1:2])
    for side, row in ((left, 23), (right, 16)):
        parts.append(side[0:8] / diagonal(side[8:16], side[row : row + 1, 0:1], cy_edge, cz_row))
    solved = solve_z(jnp.concatenate(parts, axis=0), lines)
    planes = [solved[0:32], u[0], u[1], solved[32:64]]
    for at in range(2):
        own = u[at]
        before = rows_at([(7, solved[64 + at : 65 + at])])
        after = rows_at([(0, solved[72 + at : 73 + at])])
        beside_x = near_x(jnp.concatenate([before, own, after], axis=0))[FH : FH + FX]
        beside_y = planes[at] + planes[at + 2]
        cy = sy[0:1, at : at + 1]
        applied = operate(own, beside_x, beside_y, rho[at], cx_col, cy, cz_row)
        to_slabs((force[at] - applied) / diagonal(rho[at], cx_col, cy, cz_row), slabs, at)


def middle_statics(px, py, rho, cx, sy, cz, left, right, column, cx_mid, cyz_mid, told):
    coarse, fine = iota((MX, FX), 0), iota((MX, FX), 1)
    pairs = pick_left(jnp.where(fine // 2 == coarse, 1.0, 0.0), rho[0] + rho[1])
    own = pair_columns(pairs, 0.125)
    columns = jnp.concatenate([left[16:24, 0:128], cx[...], right[16:24, 0:128]], axis=0)
    cym = jnp.broadcast_to((sy[0:1, 0:1] + sy[0:1, 1:2]) * 0.125, (8, MZ))
    czm = pair_columns(jnp.broadcast_to(cz[...], (16, FZ)), 0.125)
    cx_mid[...] = pair_rows(columns) * 0.125
    cyz_mid[...] = jnp.concatenate([czm[0:1], cym[0:7]], axis=0)
    told[0:8, 0:MZ] = own[0:8]
    told[0:8, MZ:FZ] = own[8:16]
    told[8:16, 0:MZ] = jnp.broadcast_to(column[...], (8, MZ))
    told[8:16, MZ:FZ] = cym


def solve_x_fine(px, py, slabs, lines, out):
    block = lines[0]
    for at in range(2):
        column = jnp.concatenate([slabs[m, at] for m in range(8)], axis=0)
        solved = dot(block, column)
        for m in range(8):
            out[m, at] = solved[32 * m : 32 * (m + 1)]


def add_slabs(px, py, u, slabs, told, out):
    for at in range(2):
        out[FX * at : FX * (at + 1)] = u[at] + from_slabs(slabs, at)
    out[64:80] = told[...]


def half_residual(px, py, u, below, above, force, rho, y_below, y_above, cx, sy, cz, q, low, high):
    cx_col = cx[...][:, 0:1]
    cz_row = cz[...]
    us = [below[0:32], below[32:64], u[0:32], u[32:64], above[0:32], above[32:64]]
    fs = [y_below[0:32], force[0], force[1], y_above[0:32]]
    rs = [y_below[32:64], rho[0], rho[1], y_above[32:64]]
    cys = [y_below[64:65], sy[0:1, 0:1], sy[0:1, 1:2], y_above[64:65]]
    row = iota((FX, FZ), 0)
    total = None
    for j in range(4):
        own = us[j + 1]
        beside_x = jnp.where(row == 0, 0.0, roll(own, 1, 0)) + jnp.where(row == FX - 1, 0.0, roll(own, -1, 0))
        left_over = fs[j] - operate(own, beside_x, us[j] + us[j + 2], rs[j], cx_col, cys[j], cz_row)
        if j in (1, 2):
            left_over = 3.0 * left_over
        total = left_over if total is None else total + left_over
    total = total * 0.125
    q[...] = total
    for out, edge, step, cut in ((low, 0, 1, slice(0, 8)), (high, FX - 1, -1, slice(24, 32))):
        out[0:8] = total[cut]
        next_row = edge + step
        picked = [us[j + 1][edge : edge + 1] for j in range(4)]
        out[8:16] = rows_of(picked + [us[j + 1][next_row : next_row + 1] for j in range(4)])
        out[16:24] = rows_of([rs[j][edge : edge + 1] for j in range(4)])
        out[24:32, 0:MZ] = u[72:80, 0:MZ]
        out[24:32, MZ:FZ] = u[64:72, 0:MZ] if edge == 0 else u[64:72, MZ:FZ]


def to_middle(px, py, q, u, below, above, left, right, force, rho, y_below, y_above, x_left, x_right, cx, cx_mid, cyz_mid, lines, u_ext, f_ext, r_ext, cx_ext, r_mid, f_mid, v_out, told):
    columns = jnp.concatenate([x_left[16:24, 0:128], cx[...], x_right[16:24, 0:128]], axis=0)
    cx_ext[...] = columns
    told[0:16] = below[64:80]
    told[16:32] = above[64:80]
    told[32:40] = right[24:32]
    told[40:48] = left[24:32]
    us = [below[32:64], u[0:32], u[32:64], above[0:32]]
    rs = [y_below[32:64], rho[0], rho[1], y_above[32:64]]
    cross = []
    for side, row in ((left, 0), (right, FX - 1)):
        inward = outward = None
        for j in range(4):
            weight = 0.375 if j in (1, 2) else 0.125
            here = weight * rs[j][row : row + 1] * side[8 + j : 9 + j]
            there = weight * side[16 + j : 17 + j] * us[j][row : row + 1]
            inward = here if inward is None else inward + here
            outward = there if outward is None else outward + there
        at = FH + row
        beyond = at - 1 if row == 0 else at + 1
        cross.append((at, inward * columns[at : at + 1, 0:1]))
        cross.append((beyond, outward * columns[beyond : beyond + 1, 0:1]))
    total = jnp.concatenate([left[0:8], q[...], right[0:8]], axis=0)
    line = iota((FE, FZ), 0)
    for at, term in cross:
        total = total + jnp.where(line == at, term, 0.0)
    for j in range(4):
        before = rows_at([(7, left[8 + j : 9 + j]), (6, left[12 + j : 13 + j])])
        after = rows_at([(0, right[8 + j : 9 + j]), (1, right[12 + j : 13 + j])])
        u_ext[j] = jnp.concatenate([before, us[j], after], axis=0)
    for at in range(2):
        for k, own, out in ((0, force, f_ext), (8, rho, r_ext)):
            before = rows_at([(7, x_left[k + at : k + at + 1])])
            after = rows_at([(0, x_right[k + at : k + at + 1])])
            out[at] = jnp.concatenate([before, own[at], after], axis=0)
    dense = [left[24:32, MZ:FZ], u[64:72, 0:MZ], u[64:72, MZ:FZ], right[24:32, MZ:FZ]]
    r_mid[...] = roll(jnp.concatenate(dense, axis=0), MH - 8, 0)[0:ME]
    rhs = restrict_columns(restrict_rows(total))
    rhs = jnp.where(inside_middle(px), rhs, 0.0)
    f_mid[...] = rhs
    diag = diagonal(*middle_parts(r_mid, cx_mid, cyz_mid))
    v_out[...] = solve_z(rhs / diag, lines)


def middle_parts(r_mid, cx_mid, cyz_mid):
    return r_mid[...], cx_mid[:, 0:1], cyz_mid[1:2], cyz_mid[0:1]


def middle_scaled(px, py, v, below, above, f_mid, r_mid, cx_mid, cyz_mid, out):
    rho, cx, cy, cz = middle_parts(r_mid, cx_mid, cyz_mid)
    own = v[...]
    applied = operate(own, near_x(own), below[...] + above[...], rho, cx, cy, cz)
    scaled = (f_mid[...] - applied) / diagonal(rho, cx, cy, cz)
    part = roll(scaled, -MH, 0)[0:MX]
    for i in range(out.shape[0]):
        out[i] = part


def solve_x_middle(px, py, gathered, lines, v, out):
    total = MX * N_PX
    pieces = []
    starts = (
        (jnp.maximum(MX * px - 8, 0), 8),
        (MX * px, MX),
        (jnp.minimum(MX * px + MX, total - 8), 8),
    )
    for start, size in starts:
        rows = dyn(lines, start, size)
        block = (start // 256) * 256
        pieces.append(dot(rows, dyn(gathered, block, 256)))
    full = jnp.concatenate(pieces, axis=0)
    part = roll(full, MH - 8, 0)[0:ME]
    out[...] = v[...] + jnp.where(inside_middle(px), part, 0.0)


def solve_x_block(px, py, gathered, lines, v, out):
    total = MX * N_PX
    pieces = []
    starts = (
        (jnp.maximum(MX * px - 8, 0), 8),
        (MX * px, MX),
        (jnp.minimum(MX * px + MX, total - 8), 8),
    )
    for start, size in starts:
        pieces.append(dyn(lines, start, size))
    full = dot(jnp.concatenate(pieces, axis=0), gathered[...])
    part = roll(full, MH - 8, 0)[0:ME]
    row = iota((ME, MZ), 0) + MX * px - MH
    first = 256 * (px // 16)
    held = (row >= first) & (row < first + 256)
    out[...] = jnp.where(held, v[...] + part, 0.0)


def mend(px, py, v, other, out):
    row = iota((ME, MZ), 0)
    theirs = other[...]
    up = jnp.where((row >= MH + MX) & (px == 15), roll(theirs, MX, 0), 0.0)
    down = jnp.where((row < MH) & (px == 16), roll(theirs, -MX, 0), 0.0)
    out[...] = v[...] + (up + down)


def block_mean(px, py, v, f_mid, r_mid, cx_mid, cyz_mid, told, column, out):
    rho, cx, cy, cz = middle_parts(r_mid, cx_mid, cyz_mid)
    own = v[...]
    applied = operate(own, near_x(own), 0.0, rho, cx, cy, cz)
    row = iota((ME, MZ), 0)
    kept = jnp.where((row >= MH) & (row < MH + MX), f_mid[...] - applied, 0.0)

    def mean(a):
        return jnp.sum(jnp.sum(a, axis=0, keepdims=True), axis=1, keepdims=True) * (1.0 / (MX * MZ))

    sent = column[...] * mean(kept)
    inner = roll(own, -MH, 0)[0:MX]
    for at in (0, 16):
        share = mean(told[at : at + 8, 0:MZ] * inner[0:8] + told[at : at + 8, MZ:FZ] * inner[8:16])
        sent = sent + told[at + 8 : at + 9, 0:MZ] * (share * told[at + 8 : at + 9, MZ : MZ + 1])
    for at, edge, inner_row, mine in ((32, MH + MX, MH + MX - 1, px == 15), (40, MH - 1, MH, px == 16)):
        line = r_mid[edge : edge + 1] * cx_mid[edge : edge + 1, 0:1] * v[inner_row : inner_row + 1]
        sent = sent + told[at : at + 1, 0:MZ] * jnp.where(mine, mean(line), 0.0)
    lane = iota((8, MZ), 1)
    at_x, at_y = lane % N_PX, lane // N_PX
    wide = jnp.broadcast_to(sent, (8, MZ))
    rows = []
    for dy in (-1, 0, 1):
        for dx in (-1, 0, 1):
            held = (at_x + dx >= 0) & (at_x + dx < N_PX) & (at_y + dy >= 0) & (at_y + dy < N_PY)
            rows.append(jnp.where(held, roll(wide, -(dy * N_PX + dx), 1), 0.0)[0:1])
    stacked = jnp.concatenate([rows_of(rows[0:8]), rows_of(rows[8:9])], axis=0)
    unit = jnp.where(iota((16, 128), 0) == iota((16, 128), 1), 1.0, 0.0).astype(bf16)
    high, middle, low = thirds(stacked)
    dims = ((0,), (0,))
    out[...] = product(high, unit, dims) + (product(middle, unit, dims) + product(low, unit, dims))


def second_half(px, py, parts, v, below, above, f_mid, r_mid, cx_mid, cyz_mid, lines, out):
    total = jnp.sum(parts[...], axis=0, keepdims=True)
    row = iota((ME, MZ), 0)

    def raised(plane, dy):
        at = [total[0:1, 3 * (dy + 1) + dx : 3 * (dy + 1) + dx + 1] for dx in range(3)]
        return plane + jnp.where(row < MH, at[0], jnp.where(row < MH + MX, at[1], at[2]))

    own = raised(v[...], 0)
    beside = raised(below[...], -1) + raised(above[...], 1)
    rho, cx, cy, cz = middle_parts(r_mid, cx_mid, cyz_mid)
    applied = operate(own, near_x(own), beside, rho, cx, cy, cz)
    out[...] = own + solve_z((f_mid[...] - applied) / diagonal(rho, cx, cy, cz), lines)


def to_fine(px, py, v, below, above, u_ext, f_ext, r_ext, cx_ext, sy, cz, lines, out, lower, upper):
    rows = [raise_rows(p[...]) for p in (below, v, above)]
    columns = raise_columns(jnp.concatenate(rows, axis=0)) * 0.25
    raised = [columns[FE * i : FE * (i + 1)] for i in range(3)]
    mids = [
        3.0 * raised[0] + raised[1],
        3.0 * raised[1] + raised[0],
        3.0 * raised[1] + raised[2],
        3.0 * raised[2] + raised[1],
    ]
    inside = inside_fine(px)
    us = []
    for j in range(4):
        held = inside
        if j == 0:
            held = inside & (py > 0)
        if j == 3:
            held = inside & (py < N_PY - 1)
        us.append(u_ext[j] + jnp.where(held, mids[j], 0.0))
    cx_col = cx_ext[:, 0:1]
    cz_row = cz[...]
    parts = []
    for at in range(2):
        own = us[at + 1]
        cy = sy[0:1, at : at + 1]
        applied = operate(own, near_x(own), us[at] + us[at + 2], r_ext[at], cx_col, cy, cz_row)
        parts.append((f_ext[at] - applied) / diagonal(r_ext[at], cx_col, cy, cz_row))
    solved = solve_z(jnp.concatenate(parts, axis=0), lines)
    for at in range(2):
        new = us[at + 1] + solved[FE * at : FE * (at + 1)]
        out[at] = new
        (lower if at == 0 else upper)[...] = new[FH : FH + FX]


def last_scaled(px, py, u, below, above, f_ext, r_ext, cx_ext, sy, cz, slabs):
    cx_col = cx_ext[FH : FH + FX, 0:1]
    cz_row = cz[...]
    inner = slice(FH, FH + FX)
    for at in range(2):
        full = u[at]
        beside_x = near_x(full)[inner]
        own = full[inner]
        beside_y = (below[...] if at == 0 else u[0, inner]) + (above[...] if at == 1 else u[1, inner])
        rho = r_ext[at, inner]
        cy = sy[0:1, at : at + 1]
        applied = operate(own, beside_x, beside_y, rho, cx_col, cy, cz_row)
        scaled = (f_ext[at, inner] - applied) / diagonal(rho, cx_col, cy, cz_row)
        to_slabs(scaled, slabs, at)


def finish(px, py, u, slabs, out):
    for at in range(2):
        out[:, at, :] = u[at, FH : FH + FX] + from_slabs(slabs, at)


class Device:
    def run(self, stage, shapes, *args):
        def kernel(*refs):
            stage(lax.axis_index("px"), lax.axis_index("py"), *refs)

        whole = pl.BlockSpec(memory_space=pltpu.VMEM)
        outs = pl.pallas_call(
            kernel,
            out_shape=[jax.ShapeDtypeStruct(s, f32) for s in shapes],
            in_specs=[whole] * len(args),
            out_specs=[whole] * len(shapes),
            compiler_params=pltpu.CompilerParams(vmem_limit_bytes=24 * 1024 * 1024),
        )(*args)
        return outs if len(shapes) > 1 else outs[0]

    def local(self, fn, *args):
        return fn(*args)

    def block_of(self, lines):
        at = lax.axis_index("px") // 8
        return lax.dynamic_slice_in_dim(lines, at, 1, axis=0)

    def beside(self, axis, low, high):
        n = lax.axis_size(axis)
        up = [(i, i + 1) for i in range(n - 1)]
        down = [(j, i) for i, j in up]
        return lax.ppermute(high, axis, up), lax.ppermute(low, axis, down)

    def across(self, array):
        return lax.ppermute(array, "px", [(15, 16), (16, 15)])

    def everyone(self, rows):
        sent = rows.reshape(N_PX * N_PY, 1, 128)
        got = lax.all_to_all(sent, ("py", "px"), 0, 0, tiled=True)
        return got.reshape(N_PX * N_PY, 128)

    def swap(self, axis, array, group):
        n = lax.axis_size(axis)
        groups = None
        if group < n:
            groups = [list(range(k, k + group)) for k in range(0, n, group)]
        return lax.all_to_all(array, axis, 0, 0, axis_index_groups=groups, tiled=True)


def cycle(d, forcing, inv_density, stretch_x, stretch_y, stretch_z, lines_z0, lines_x0, lines_z1, lines_x1, column):
    sx = d.local(lambda a: a.reshape(1, FX), stretch_x)
    sy = d.local(lambda a: a.reshape(1, 2), stretch_y)
    cz = d.local(lambda a: a.reshape(1, FZ), stretch_z)
    rows_x1 = d.local(lambda a: a.reshape(MX * N_PX, 256), lines_x1)
    slab, own, mid = (8, 2, FX, 128), (2, FX, FZ), (ME, MZ)

    force, rho, lower, upper, low, high, cx = d.run(
        start,
        [own, own, (72, FZ), (72, FZ), (24, FZ), (24, FZ), (FX, 128)],
        forcing, inv_density, sx, sy,
    )
    y_below, y_above = d.beside("py", lower, upper)
    x_left, x_right = d.beside("px", low, high)
    block = d.block_of(lines_x0)
    u = d.run(own_lines, [own], force, rho, cx, sy, cz, lines_z0)
    slabs = d.run(
        first_half, [slab],
        force, rho, cx, sy, cz, u, y_below, y_above, x_left, x_right, lines_z0,
    )
    slabs = d.swap("px", slabs, 8)
    cx_mid, cyz_mid, told = d.run(
        middle_statics,
        [(ME, 128), (8, MZ), (16, FZ)],
        rho, cx, sy, cz, x_left, x_right, column,
    )
    slabs = d.run(solve_x_fine, [slab], slabs, block)
    slabs = d.swap("px", slabs, 8)
    u = d.run(add_slabs, [(80, FZ)], u, slabs, told)
    below, above = d.beside("py", u, u)
    q, low, high = d.run(
        half_residual, [(FX, FZ)] * 3,
        u, below, above, force, rho, y_below, y_above, cx, sy, cz,
    )
    left, right = d.beside("px", low, high)
    u_ext, f_ext, r_ext, cx_ext, r_mid, f_mid, v, told = d.run(
        to_middle,
        [(4, FE, FZ), (2, FE, FZ), (2, FE, FZ), (FE, 128), mid, mid, mid, (48, FZ)],
        q, u, below, above, left, right, force, rho, y_below, y_above, x_left, x_right,
        cx, cx_mid, cyz_mid, lines_z1,
    )
    statics = (f_mid, r_mid, cx_mid, cyz_mid)

    below, above = d.beside("py", v, v)
    every = d.run(middle_scaled, [(16, MX, MZ)], v, below, above, *statics)
    every = d.swap("px", every, 16)
    every = d.local(lambda a: a.reshape(256, MZ), every)
    v = d.run(solve_x_block, [mid], every, rows_x1, v)
    other = d.across(v)
    sent = d.run(block_mean, [(N_PX * N_PY, 128)], v, *statics, told, column)
    parts = d.everyone(sent)
    v = d.run(mend, [mid], v, other)
    below, above = d.beside("py", v, v)
    v = d.run(second_half, [mid], parts, v, below, above, *statics, lines_z1)
    below, above = d.beside("py", v, v)
    every = d.run(middle_scaled, [(N_PX, MX, MZ)], v, below, above, *statics)
    every = d.swap("px", every, N_PX)
    every = d.local(lambda a: a.reshape(MX * N_PX, MZ), every)
    v = d.run(solve_x_middle, [mid], every, rows_x1, v)

    below, above = d.beside("py", v, v)
    u, lower, upper = d.run(
        to_fine,
        [(2, FE, FZ), (FX, FZ), (FX, FZ)],
        v, below, above, u_ext, f_ext, r_ext, cx_ext, sy, cz, lines_z0,
    )
    below, above = d.beside("py", lower, upper)
    slabs = d.run(last_scaled, [slab], u, below, above, f_ext, r_ext, cx_ext, sy, cz)
    slabs = d.swap("px", slabs, 8)
    slabs = d.run(solve_x_fine, [slab], slabs, block)
    slabs = d.swap("px", slabs, 8)
    return d.run(finish, [(FX, 2, FZ)], u, slabs)


def solution(mesh):
    placed = (
        P("px", "py", None),
        P("px", "py", None),
        P("px"),
        P("py"),
        P(),
        P(),
        P(),
        P(),
        P(),
        P(("py", "px"), None),
    )

    def step(*args):
        return cycle(Device(), *args)

    return jax.shard_map(
        step, mesh=mesh, in_specs=placed, out_specs=P("px", "py", None), check_vma=False
    )
```

```python
import functools

import jax
import jax.numpy as jnp
from jax import lax
from jax.experimental import pallas as pl
from jax.experimental.pallas import tpu as pltpu
from jax.sharding import PartitionSpec as P

shift_term = 0.1
f32 = jnp.float32
bf16 = jnp.bfloat16

N_PY, N_PX = 16, 32
FX, FZ = 32, 1024
MX, MZ = 16, 512
FH, MH = 8, 4
FE, ME = FX + 2 * FH, MX + 2 * MH


def roll(v, shift, axis):
    return pltpu.roll(v, shift % v.shape[axis], axis)


def dyn(ref, start, size):
    return ref[pl.ds(pl.multiple_of(start, 8), size), :]


def halves(a):
    high = a.astype(bf16)
    return high, (a - high.astype(f32)).astype(bf16)


def thirds(a):
    high, rest = a.astype(bf16), None
    rest = a - high.astype(f32)
    middle = rest.astype(bf16)
    return high, middle, (rest - middle.astype(f32)).astype(bf16)


def product(a, b, dims):
    return lax.dot_general(a, b, (dims, ((), ())), preferred_element_type=f32)


def dot(a, b, dims=((1,), (0,))):
    a_high, a_low = halves(a)
    b_high, b_low = halves(b)
    return product(a_high, b_high, dims) + (product(a_high, b_low, dims) + product(a_low, b_high, dims))


def pick_right(a, weight):
    dims = ((1,), (0,))
    w = weight.astype(bf16)
    high, middle, low = thirds(a)
    return product(high, w, dims) + (product(middle, w, dims) + product(low, w, dims))


def pick_left(weight, a):
    dims = ((1,), (0,))
    w = weight.astype(bf16)
    high, middle, low = thirds(a)
    return product(w, high, dims) + (product(w, middle, dims) + product(w, low, dims))


def iota(shape, axis):
    return lax.broadcasted_iota(jnp.int32, shape, axis)


def rows_of(rows):
    at = iota((8, rows[0].shape[1]), 0)
    total = jnp.zeros((8, rows[0].shape[1]), f32)
    for i, row in enumerate(rows):
        total = jnp.where(at == i, row, total)
    return total


def rows_at(pairs):
    at = iota((8, pairs[0][1].shape[1]), 0)
    total = jnp.zeros((8, pairs[0][1].shape[1]), f32)
    for i, row in pairs:
        total = jnp.where(at == i, row, total)
    return total


def near_z(v):
    lane = iota(v.shape, 1)
    last = v.shape[1] - 1
    below = jnp.where(lane == 0, 0.0, roll(v, 1, 1))
    above = jnp.where(lane == last, 0.0, roll(v, -1, 1))
    return below + above


def near_x(v):
    return roll(v, 1, 0) + roll(v, -1, 0)


def operate(v, v_near_x, v_near_y, rho, cx, cy, cz):
    twice = 2.0 * v
    stencil = cx * (twice - v_near_x) + cy * (twice - v_near_y) + cz * (twice - near_z(v))
    return shift_term * v + rho * stencil


def diagonal(rho, cx, cy, cz):
    return shift_term + 2.0 * rho * (cx + cy + cz)


def solve_z(w, lines):
    count, size = lines.shape[0], lines.shape[1]
    parts = []
    for k in range(count):
        parts.append(dot(w[:, k * size : (k + 1) * size], lines[k], ((1,), (1,))))
    return jnp.concatenate(parts, axis=1)


def columns_by(v, pick):
    cuts = [slice(256 * k, 256 * (k + 1)) for k in range(v.shape[1] // 256)]
    return jnp.concatenate([pick_right(v[:, cut], pick) for cut in cuts], axis=1)


def pair_columns(v, scale):
    fine, coarse = iota((256, 128), 0), iota((256, 128), 1)
    return columns_by(v, jnp.where(fine // 2 == coarse, scale, 0.0))


def even_columns(v, scale):
    fine, coarse = iota((256, 128), 0), iota((256, 128), 1)
    return columns_by(v, jnp.where(fine == 2 * coarse, scale, 0.0))


def restrict_columns(v):
    lane = iota(v.shape, 1)
    last = v.shape[1] - 1
    one = jnp.where(lane == last, 0.0, roll(v, -1, 1))
    two = jnp.where(lane >= last - 1, 0.0, roll(v, -2, 1))
    below = jnp.where(lane == 0, 0.0, roll(v, 1, 1))
    return even_columns(below + 3.0 * v + 3.0 * one + two, 0.125)


def raise_columns(v):
    lane = iota(v.shape, 1)
    last = v.shape[1] - 1
    below = jnp.where(lane == 0, 0.0, roll(v, 1, 1))
    above = jnp.where(lane == last, 0.0, roll(v, -1, 1))
    even = 3.0 * v + below
    odd = 3.0 * v + above
    coarse, fine = iota((128, 256), 0), iota((128, 256), 1)
    at_even = jnp.where(fine == 2 * coarse, 0.25, 0.0)
    at_odd = jnp.where(fine == 2 * coarse + 1, 0.25, 0.0)
    parts = []
    for k in range(v.shape[1] // 128):
        cut = slice(128 * k, 128 * (k + 1))
        parts.append(pick_right(even[:, cut], at_even) + pick_right(odd[:, cut], at_odd))
    return jnp.concatenate(parts, axis=1)


def restrict_rows(v):
    coarse, fine = iota((ME, FE), 0), iota((ME, FE), 1)
    away = fine - 2 * coarse
    weight = jnp.where((away == 0) | (away == 1), 0.375, 0.0)
    weight = weight + jnp.where((away == -1) | (away == 2), 0.125, 0.0)
    return pick_left(weight, v)


def pair_rows(v):
    coarse, fine = iota((ME, FE), 0), iota((ME, FE), 1)
    return pick_left(jnp.where(fine // 2 == coarse, 1.0, 0.0), v)


def raise_rows(v):
    fine, coarse = iota((FE, ME), 0), iota((FE, ME), 1)
    away = fine - 2 * coarse
    weight = jnp.where((away == 0) | (away == 1), 0.75, 0.0)
    weight = weight + jnp.where((away == 2) | (away == -1), 0.25, 0.0)
    return pick_left(weight, v)


def inside_middle(px):
    row = iota((ME, MZ), 0) + MX * px - MH
    return (row >= 0) & (row < MX * N_PX)


def inside_fine(px):
    row = iota((FE, FZ), 0) + FX * px - FH
    return (row >= 0) & (row < FX * N_PX)


def to_slabs(plane, out, at):
    for m in range(8):
        out[m, at] = plane[:, 128 * m : 128 * (m + 1)]


def from_slabs(ref, at):
    return jnp.concatenate([ref[m, at] for m in range(8)], axis=1)


def start(px, py, forcing, inv_density, sx, sy, force, rho, lower, upper, low, high, cx):
    square = iota((FX, FX), 0) == iota((FX, FX), 1)
    column = jnp.sum(jnp.where(square, sx[...], 0.0), axis=1, keepdims=True)
    cx[...] = jnp.broadcast_to(column, (FX, 128))
    wide = jnp.broadcast_to(column, (FX, FZ))
    edges = {}
    for at, out in ((0, lower), (1, upper)):
        f_plane, r_plane = forcing[:, at, :], inv_density[:, at, :]
        force[at] = f_plane
        rho[at] = r_plane
        out[0:32] = f_plane
        out[32:64] = r_plane
        out[64:72] = jnp.broadcast_to(sy[0:1, at : at + 1], (8, FZ))
        for row in (0, FX - 1):
            edges[at, row] = (f_plane[row : row + 1], r_plane[row : row + 1])
    for side, row, cut in ((low, 0, slice(0, 8)), (high, FX - 1, slice(24, 32))):
        for k in range(2):
            side[8 * k : 8 * k + 8] = rows_of([edges[0, row][k], edges[1, row][k]])
        side[16:24] = wide[cut]


def own_lines(px, py, force, rho, cx, sy, cz, lines, u):
    parts = []
    for at in range(2):
        parts.append(force[at] / diagonal(rho[at], cx[:, 0:1], sy[0:1, at : at + 1], cz[...]))
    solved = solve_z(jnp.concatenate(parts, axis=0), lines)
    u[0] = solved[0:FX]
    u[1] = solved[FX : 2 * FX]


def first_half(px, py, force, rho, cx, sy, cz, u, below, above, left, right, lines, slabs):
    cx_col = cx[:, 0:1]
    cz_row = cz[...]
    parts = []
    for side in (below, above):
        parts.append(side[0:32] / diagonal(side[32:64], cx_col, side[64:65], cz_row))
    cy_edge = jnp.where(iota((8, 1), 0) == 0, sy[0:1, 0:1], sy[0:1, 1:2])
    for side, row in ((left, 23), (right, 16)):
        parts.append(side[0:8] / diagonal(side[8:16], side[row : row + 1, 0:1], cy_edge, cz_row))
    solved = solve_z(jnp.concatenate(parts, axis=0), lines)
    planes = [solved[0:32], u[0], u[1], solved[32:64]]
    for at in range(2):
        own = u[at]
        before = rows_at([(7, solved[64 + at : 65 + at])])
        after = rows_at([(0, solved[72 + at : 73 + at])])
        beside_x = near_x(jnp.concatenate([before, own, after], axis=0))[FH : FH + FX]
        beside_y = planes[at] + planes[at + 2]
        cy = sy[0:1, at : at + 1]
        applied = operate(own, beside_x, beside_y, rho[at], cx_col, cy, cz_row)
        to_slabs((force[at] - applied) / diagonal(rho[at], cx_col, cy, cz_row), slabs, at)


def middle_statics(px, py, rho, cx, sy, cz, left, right, column, cx_mid, cyz_mid, told):
    coarse, fine = iota((MX, FX), 0), iota((MX, FX), 1)
    pairs = pick_left(jnp.where(fine // 2 == coarse, 1.0, 0.0), rho[0] + rho[1])
    own = pair_columns(pairs, 0.125)
    columns = jnp.concatenate([left[16:24, 0:128], cx[...], right[16:24, 0:128]], axis=0)
    cym = jnp.broadcast_to((sy[0:1, 0:1] + sy[0:1, 1:2]) * 0.125, (8, MZ))
    czm = pair_columns(jnp.broadcast_to(cz[...], (16, FZ)), 0.125)
    cx_mid[...] = pair_rows(columns) * 0.125
    cyz_mid[...] = jnp.concatenate([czm[0:1], cym[0:7]], axis=0)
    told[0:8, 0:MZ] = own[0:8]
    told[0:8, MZ:FZ] = own[8:16]
    told[8:16, 0:MZ] = jnp.broadcast_to(column[...], (8, MZ))
    told[8:16, MZ:FZ] = cym


def solve_x_fine(px, py, slabs, lines, out):
    block = lines[0]
    for at in range(2):
        column = jnp.concatenate([slabs[m, at] for m in range(8)], axis=0)
        solved = dot(block, column)
        for m in range(8):
            out[m, at] = solved[32 * m : 32 * (m + 1)]


def add_slabs(px, py, u, slabs, told, out):
    for at in range(2):
        out[FX * at : FX * (at + 1)] = u[at] + from_slabs(slabs, at)
    out[64:80] = told[...]


def half_residual(px, py, u, below, above, force, rho, y_below, y_above, cx, sy, cz, q, low, high):
    cx_col = cx[...][:, 0:1]
    cz_row = cz[...]
    us = [below[0:32], below[32:64], u[0:32], u[32:64], above[0:32], above[32:64]]
    fs = [y_below[0:32], force[0], force[1], y_above[0:32]]
    rs = [y_below[32:64], rho[0], rho[1], y_above[32:64]]
    cys = [y_below[64:65], sy[0:1, 0:1], sy[0:1, 1:2], y_above[64:65]]
    row = iota((FX, FZ), 0)
    total = None
    for j in range(4):
        own = us[j + 1]
        beside_x = jnp.where(row == 0, 0.0, roll(own, 1, 0)) + jnp.where(row == FX - 1, 0.0, roll(own, -1, 0))
        left_over = fs[j] - operate(own, beside_x, us[j] + us[j + 2], rs[j], cx_col, cys[j], cz_row)
        if j in (1, 2):
            left_over = 3.0 * left_over
        total = left_over if total is None else total + left_over
    total = total * 0.125
    q[...] = total
    for out, edge, step, cut in ((low, 0, 1, slice(0, 8)), (high, FX - 1, -1, slice(24, 32))):
        out[0:8] = total[cut]
        next_row = edge + step
        picked = [us[j + 1][edge : edge + 1] for j in range(4)]
        out[8:16] = rows_of(picked + [us[j + 1][next_row : next_row + 1] for j in range(4)])
        out[16:24] = rows_of([rs[j][edge : edge + 1] for j in range(4)])
        out[24:32, 0:MZ] = u[64:72, 0:MZ] if edge == 0 else u[64:72, MZ:FZ]
        out[24:32, MZ:FZ] = jnp.zeros((8, MZ), f32)


def to_middle(px, py, q, u, below, above, left, right, force, rho, y_below, y_above, x_left, x_right, cx, cx_mid, cyz_mid, lines, u_ext, f_ext, r_ext, cx_ext, r_mid, f_mid, v_out, told):
    columns = jnp.concatenate([x_left[16:24, 0:128], cx[...], x_right[16:24, 0:128]], axis=0)
    cx_ext[...] = columns
    told[0:16] = below[64:80]
    told[16:32] = above[64:80]
    us = [below[32:64], u[0:32], u[32:64], above[0:32]]
    rs = [y_below[32:64], rho[0], rho[1], y_above[32:64]]
    cross = []
    for side, row in ((left, 0), (right, FX - 1)):
        inward = outward = None
        for j in range(4):
            weight = 0.375 if j in (1, 2) else 0.125
            here = weight * rs[j][row : row + 1] * side[8 + j : 9 + j]
            there = weight * side[16 + j : 17 + j] * us[j][row : row + 1]
            inward = here if inward is None else inward + here
            outward = there if outward is None else outward + there
        at = FH + row
        beyond = at - 1 if row == 0 else at + 1
        cross.append((at, inward * columns[at : at + 1, 0:1]))
        cross.append((beyond, outward * columns[beyond : beyond + 1, 0:1]))
    total = jnp.concatenate([left[0:8], q[...], right[0:8]], axis=0)
    line = iota((FE, FZ), 0)
    for at, term in cross:
        total = total + jnp.where(line == at, term, 0.0)
    for j in range(4):
        before = rows_at([(7, left[8 + j : 9 + j]), (6, left[12 + j : 13 + j])])
        after = rows_at([(0, right[8 + j : 9 + j]), (1, right[12 + j : 13 + j])])
        u_ext[j] = jnp.concatenate([before, us[j], after], axis=0)
    for at in range(2):
        for k, own, out in ((0, force, f_ext), (8, rho, r_ext)):
            before = rows_at([(7, x_left[k + at : k + at + 1])])
            after = rows_at([(0, x_right[k + at : k + at + 1])])
            out[at] = jnp.concatenate([before, own[at], after], axis=0)
    dense = [left[24:32, 0:MZ], u[64:72, 0:MZ], u[64:72, MZ:FZ], right[24:32, 0:MZ]]
    r_mid[...] = roll(jnp.concatenate(dense, axis=0), MH - 8, 0)[0:ME]
    rhs = restrict_columns(restrict_rows(total))
    rhs = jnp.where(inside_middle(px), rhs, 0.0)
    f_mid[...] = rhs
    diag = diagonal(*middle_parts(r_mid, cx_mid, cyz_mid))
    v_out[...] = solve_z(rhs / diag, lines)


def middle_parts(r_mid, cx_mid, cyz_mid):
    return r_mid[...], cx_mid[:, 0:1], cyz_mid[1:2], cyz_mid[0:1]


def middle_scaled(px, py, v, below, above, f_mid, r_mid, cx_mid, cyz_mid, out):
    rho, cx, cy, cz = middle_parts(r_mid, cx_mid, cyz_mid)
    own = v[...]
    applied = operate(own, near_x(own), below[...] + above[...], rho, cx, cy, cz)
    scaled = (f_mid[...] - applied) / diagonal(rho, cx, cy, cz)
    part = roll(scaled, -MH, 0)[0:MX]
    for i in range(out.shape[0]):
        out[i] = part


def rows_for_x(px, py, lines, out):
    place, row_of_four = px % 4, px // 4
    total = MX * N_PX
    parts = []
    for i in range(8):
        base = MX * (4 * i + place)
        pieces = [
            dyn(lines, jnp.maximum(base - 8, 0), 8),
            dyn(lines, base, MX),
            dyn(lines, jnp.minimum(base + MX, total - 8), 8),
        ]
        rows = roll(jnp.concatenate(pieces, axis=0), MH - 8, 0)[0:ME]
        at = iota((ME, 256), 0) + base - MH
        first = 256 * (row_of_four // 4)
        parts.append(jnp.where((at >= first) & (at < first + 256), rows, 0.0))
    full = jnp.concatenate(parts, axis=0)
    held = None
    for i in range(4):
        cut = jnp.where(row_of_four % 4 == i, full[:, 64 * i : 64 * (i + 1)], 0.0)
        held = cut if held is None else held + cut
    out[...] = held


def spread_x(px, py, gathered, rows, out):
    solved = dot(rows[...], gathered[...])
    for i in range(8):
        out[i] = solved[ME * i : ME * (i + 1)]


def gain_x(px, py, v, parts, out):
    total = v[...]
    for i in range(8):
        total = total + parts[i]
    out[...] = total


def block_mean(px, py, before, parts, f_mid, r_mid, cx_mid, cyz_mid, told, column, v, out):
    rho, cx, cy, cz = middle_parts(r_mid, cx_mid, cyz_mid)
    gain_x(px, py, before, parts, v)
    own = v[...]
    applied = operate(own, near_x(own), 0.0, rho, cx, cy, cz)
    row = iota((ME, MZ), 0)
    kept = jnp.where((row >= MH) & (row < MH + MX), f_mid[...] - applied, 0.0)

    def mean(a):
        return jnp.sum(jnp.sum(a, axis=0, keepdims=True), axis=1, keepdims=True) * (1.0 / (MX * MZ))

    sent = column[...] * mean(kept)
    inner = roll(own, -MH, 0)[0:MX]
    for at in (0, 16):
        share = mean(told[at : at + 8, 0:MZ] * inner[0:8] + told[at : at + 8, MZ:FZ] * inner[8:16])
        sent = sent + told[at + 8 : at + 9, 0:MZ] * (share * told[at + 8 : at + 9, MZ : MZ + 1])
    lane = iota((8, MZ), 1)
    at_x, at_y = lane % N_PX, lane // N_PX
    wide = jnp.broadcast_to(sent, (8, MZ))
    rows = []
    for dy in (-1, 0, 1):
        for dx in (-1, 0, 1):
            held = (at_x + dx >= 0) & (at_x + dx < N_PX) & (at_y + dy >= 0) & (at_y + dy < N_PY)
            rows.append(jnp.where(held, roll(wide, -(dy * N_PX + dx), 1), 0.0)[0:1])
    stacked = jnp.concatenate([rows_of(rows[0:8]), rows_of(rows[8:9])], axis=0)
    unit = jnp.where(iota((16, 128), 0) == iota((16, 128), 1), 1.0, 0.0).astype(bf16)
    high, middle, low = thirds(stacked)
    dims = ((0,), (0,))
    out[...] = product(high, unit, dims) + (product(middle, unit, dims) + product(low, unit, dims))


def second_half(px, py, parts, v, below, above, f_mid, r_mid, cx_mid, cyz_mid, lines, out):
    total = jnp.sum(parts[...], axis=0, keepdims=True)
    row = iota((ME, MZ), 0)

    def raised(plane, dy):
        at = [total[0:1, 3 * (dy + 1) + dx : 3 * (dy + 1) + dx + 1] for dx in range(3)]
        return plane + jnp.where(row < MH, at[0], jnp.where(row < MH + MX, at[1], at[2]))

    own = raised(v[...], 0)
    beside = raised(below[...], -1) + raised(above[...], 1)
    rho, cx, cy, cz = middle_parts(r_mid, cx_mid, cyz_mid)
    applied = operate(own, near_x(own), beside, rho, cx, cy, cz)
    out[...] = own + solve_z((f_mid[...] - applied) / diagonal(rho, cx, cy, cz), lines)


def to_fine(px, py, v, below, above, u_ext, f_ext, r_ext, cx_ext, sy, cz, lines, out, lower, upper):
    rows = [raise_rows(p[...]) for p in (below, v, above)]
    columns = raise_columns(jnp.concatenate(rows, axis=0)) * 0.25
    raised = [columns[FE * i : FE * (i + 1)] for i in range(3)]
    mids = [
        3.0 * raised[0] + raised[1],
        3.0 * raised[1] + raised[0],
        3.0 * raised[1] + raised[2],
        3.0 * raised[2] + raised[1],
    ]
    inside = inside_fine(px)
    us = []
    for j in range(4):
        held = inside
        if j == 0:
            held = inside & (py > 0)
        if j == 3:
            held = inside & (py < N_PY - 1)
        us.append(u_ext[j] + jnp.where(held, mids[j], 0.0))
    cx_col = cx_ext[:, 0:1]
    cz_row = cz[...]
    parts = []
    for at in range(2):
        own = us[at + 1]
        cy = sy[0:1, at : at + 1]
        applied = operate(own, near_x(own), us[at] + us[at + 2], r_ext[at], cx_col, cy, cz_row)
        parts.append((f_ext[at] - applied) / diagonal(r_ext[at], cx_col, cy, cz_row))
    solved = solve_z(jnp.concatenate(parts, axis=0), lines)
    for at in range(2):
        new = us[at + 1] + solved[FE * at : FE * (at + 1)]
        out[at] = new
        (lower if at == 0 else upper)[...] = new[FH : FH + FX]


def last_scaled(px, py, u, below, above, f_ext, r_ext, cx_ext, sy, cz, slabs):
    cx_col = cx_ext[FH : FH + FX, 0:1]
    cz_row = cz[...]
    inner = slice(FH, FH + FX)
    for at in range(2):
        full = u[at]
        beside_x = near_x(full)[inner]
        own = full[inner]
        beside_y = (below[...] if at == 0 else u[0, inner]) + (above[...] if at == 1 else u[1, inner])
        rho = r_ext[at, inner]
        cy = sy[0:1, at : at + 1]
        applied = operate(own, beside_x, beside_y, rho, cx_col, cy, cz_row)
        scaled = (f_ext[at, inner] - applied) / diagonal(rho, cx_col, cy, cz_row)
        to_slabs(scaled, slabs, at)


def finish(px, py, u, slabs, out):
    for at in range(2):
        out[:, at, :] = u[at, FH : FH + FX] + from_slabs(slabs, at)


class Device:
    def run(self, stage, shapes, *args):
        def kernel(*refs):
            stage(lax.axis_index("px"), lax.axis_index("py"), *refs)

        whole = pl.BlockSpec(memory_space=pltpu.VMEM)
        outs = pl.pallas_call(
            kernel,
            out_shape=[jax.ShapeDtypeStruct(s, f32) for s in shapes],
            in_specs=[whole] * len(args),
            out_specs=[whole] * len(shapes),
            compiler_params=pltpu.CompilerParams(vmem_limit_bytes=24 * 1024 * 1024),
            name=stage.__name__,
        )(*args)
        return outs if len(shapes) > 1 else outs[0]

    def local(self, fn, *args):
        return fn(*args)

    def block_of(self, lines):
        at = lax.axis_index("px") // 8
        return lax.dynamic_slice_in_dim(lines, at, 1, axis=0)

    def beside(self, axis, low, high):
        n = lax.axis_size(axis)
        up = [(i, i + 1) for i in range(n - 1)]
        down = [(j, i) for i, j in up]
        return lax.ppermute(high, axis, up), lax.ppermute(low, axis, down)

    def everyone(self, rows):
        sent = rows.reshape(N_PX * N_PY, 1, 128)
        got = lax.all_to_all(sent, ("py", "px"), 0, 0, tiled=True)
        return got.reshape(N_PX * N_PY, 128)

    def solve_x(self, every, rows):
        fours = [list(range(k, k + 4)) for k in range(0, N_PX, 4)]
        eights = [list(range(k, N_PX, 4)) for k in range(4)]
        every = lax.all_to_all(every, "px", 0, 0, axis_index_groups=fours, tiled=True)
        parts = self.run(spread_x, [(8, ME, MZ)], every.reshape(4 * MX, MZ), rows)
        return lax.all_to_all(parts, "px", 0, 0, axis_index_groups=eights, tiled=True)

    def swap(self, axis, array, group):
        n = lax.axis_size(axis)
        groups = None
        if group < n:
            groups = [list(range(k, k + group)) for k in range(0, n, group)]
        return lax.all_to_all(array, axis, 0, 0, axis_index_groups=groups, tiled=True)


def cycle(d, forcing, inv_density, stretch_x, stretch_y, stretch_z, lines_z0, lines_x0, lines_z1, lines_x1, column):
    sx = d.local(lambda a: a.reshape(1, FX), stretch_x)
    sy = d.local(lambda a: a.reshape(1, 2), stretch_y)
    cz = d.local(lambda a: a.reshape(1, FZ), stretch_z)
    rows_x1 = d.local(lambda a: a.reshape(MX * N_PX, 256), lines_x1)
    slab, own, mid = (8, 2, FX, 128), (2, FX, FZ), (ME, MZ)

    force, rho, lower, upper, low, high, cx = d.run(
        start,
        [own, own, (72, FZ), (72, FZ), (24, FZ), (24, FZ), (FX, 128)],
        forcing, inv_density, sx, sy,
    )
    y_below, y_above = d.beside("py", lower, upper)
    x_left, x_right = d.beside("px", low, high)
    block = d.block_of(lines_x0)
    rows_x = d.run(rows_for_x, [(8 * ME, 64)], rows_x1)
    u = d.run(own_lines, [own], force, rho, cx, sy, cz, lines_z0)
    slabs = d.run(
        first_half, [slab],
        force, rho, cx, sy, cz, u, y_below, y_above, x_left, x_right, lines_z0,
    )
    slabs = d.swap("px", slabs, 8)
    cx_mid, cyz_mid, told = d.run(
        middle_statics,
        [(ME, 128), (8, MZ), (16, FZ)],
        rho, cx, sy, cz, x_left, x_right, column,
    )
    slabs = d.run(solve_x_fine, [slab], slabs, block)
    slabs = d.swap("px", slabs, 8)
    u = d.run(add_slabs, [(80, FZ)], u, slabs, told)
    below, above = d.beside("py", u, u)
    q, low, high = d.run(
        half_residual, [(FX, FZ)] * 3,
        u, below, above, force, rho, y_below, y_above, cx, sy, cz,
    )
    left, right = d.beside("px", low, high)
    u_ext, f_ext, r_ext, cx_ext, r_mid, f_mid, v, told = d.run(
        to_middle,
        [(4, FE, FZ), (2, FE, FZ), (2, FE, FZ), (FE, 128), mid, mid, mid, (32, FZ)],
        q, u, below, above, left, right, force, rho, y_below, y_above, x_left, x_right,
        cx, cx_mid, cyz_mid, lines_z1,
    )
    statics = (f_mid, r_mid, cx_mid, cyz_mid)

    below, above = d.beside("py", v, v)
    parts = d.solve_x(d.run(middle_scaled, [(4, MX, MZ)], v, below, above, *statics), rows_x)
    v, sent = d.run(block_mean, [mid, (N_PX * N_PY, 128)], v, parts, *statics, told, column)
    with jax.named_scope("means"):
        parts = d.everyone(sent)
    below, above = d.beside("py", v, v)
    v = d.run(second_half, [mid], parts, v, below, above, *statics, lines_z1)
    below, above = d.beside("py", v, v)
    parts = d.solve_x(d.run(middle_scaled, [(4, MX, MZ)], v, below, above, *statics), rows_x)
    v = d.run(gain_x, [mid], v, parts)

    below, above = d.beside("py", v, v)
    u, lower, upper = d.run(
        to_fine,
        [(2, FE, FZ), (FX, FZ), (FX, FZ)],
        v, below, above, u_ext, f_ext, r_ext, cx_ext, sy, cz, lines_z0,
    )
    below, above = d.beside("py", lower, upper)
    slabs = d.run(last_scaled, [slab], u, below, above, f_ext, r_ext, cx_ext, sy, cz)
    slabs = d.swap("px", slabs, 8)
    slabs = d.run(solve_x_fine, [slab], slabs, block)
    slabs = d.swap("px", slabs, 8)
    return d.run(finish, [(FX, 2, FZ)], u, slabs)


def solution(mesh):
    placed = (
        P("px", "py", None),
        P("px", "py", None),
        P("px"),
        P("py"),
        P(),
        P(),
        P(),
        P(),
        P(),
        P(("py", "px"), None),
    )
    return jax.shard_map(
        functools.partial(cycle, Device()),
        mesh=mesh,
        in_specs=placed,
        out_specs=P("px", "py", None),
        check_vma=False,
    )
```

```python
import jax
import jax.numpy as jnp
from jax import lax
from jax.experimental import pallas as pl
from jax.experimental.pallas import tpu as pltpu
from jax.sharding import PartitionSpec as P


shift_term = 0.1
f32 = jnp.float32
bf16 = jnp.bfloat16

N_PY, N_PX = 16, 32
FX, FZ = 32, 1024
MX, MZ = 16, 512
FH, MH = 8, 4
FE, ME = FX + 2 * FH, MX + 2 * MH


def roll(v, shift, axis):
    return pltpu.roll(v, shift % v.shape[axis], axis)


def dyn(ref, start, size):
    return ref[pl.ds(pl.multiple_of(start, 8), size), :]


def halves(a):
    high = a.astype(bf16)
    return high, (a - high.astype(f32)).astype(bf16)


def thirds(a):
    high, rest = a.astype(bf16), None
    rest = a - high.astype(f32)
    middle = rest.astype(bf16)
    return high, middle, (rest - middle.astype(f32)).astype(bf16)


def product(a, b, dims):
    return lax.dot_general(a, b, (dims, ((), ())), preferred_element_type=f32)


def dot(a, b, dims=((1,), (0,))):
    a_high, a_low = halves(a)
    b_high, b_low = halves(b)
    return product(a_high, b_high, dims) + (product(a_high, b_low, dims) + product(a_low, b_high, dims))


def pick_right(a, weight):
    dims = ((1,), (0,))
    w = weight.astype(bf16)
    high, middle, low = thirds(a)
    return product(high, w, dims) + (product(middle, w, dims) + product(low, w, dims))


def pick_left(weight, a):
    dims = ((1,), (0,))
    w = weight.astype(bf16)
    high, middle, low = thirds(a)
    return product(w, high, dims) + (product(w, middle, dims) + product(w, low, dims))


def iota(shape, axis):
    return lax.broadcasted_iota(jnp.int32, shape, axis)


def rows_of(rows):
    at = iota((8, rows[0].shape[1]), 0)
    total = jnp.zeros((8, rows[0].shape[1]), f32)
    for i, row in enumerate(rows):
        total = jnp.where(at == i, row, total)
    return total


def rows_at(pairs):
    at = iota((8, pairs[0][1].shape[1]), 0)
    total = jnp.zeros((8, pairs[0][1].shape[1]), f32)
    for i, row in pairs:
        total = jnp.where(at == i, row, total)
    return total


def near_z(v):
    lane = iota(v.shape, 1)
    last = v.shape[1] - 1
    below = jnp.where(lane == 0, 0.0, roll(v, 1, 1))
    above = jnp.where(lane == last, 0.0, roll(v, -1, 1))
    return below + above


def near_x(v):
    return roll(v, 1, 0) + roll(v, -1, 0)


def operate(v, v_near_x, v_near_y, rho, cx, cy, cz):
    twice = 2.0 * v
    stencil = cx * (twice - v_near_x) + cy * (twice - v_near_y) + cz * (twice - near_z(v))
    return shift_term * v + rho * stencil


def diagonal(rho, cx, cy, cz):
    return shift_term + 2.0 * rho * (cx + cy + cz)


def solve_z(w, lines):
    count, size = lines.shape[0], lines.shape[1]
    parts = []
    for k in range(count):
        parts.append(dot(w[:, k * size : (k + 1) * size], lines[k], ((1,), (1,))))
    return jnp.concatenate(parts, axis=1)


def columns_by(v, pick):
    cuts = [slice(256 * k, 256 * (k + 1)) for k in range(v.shape[1] // 256)]
    return jnp.concatenate([pick_right(v[:, cut], pick) for cut in cuts], axis=1)


def pair_columns(v, scale):
    fine, coarse = iota((256, 128), 0), iota((256, 128), 1)
    return columns_by(v, jnp.where(fine // 2 == coarse, scale, 0.0))


def even_columns(v, scale):
    fine, coarse = iota((256, 128), 0), iota((256, 128), 1)
    return columns_by(v, jnp.where(fine == 2 * coarse, scale, 0.0))


def restrict_columns(v):
    lane = iota(v.shape, 1)
    last = v.shape[1] - 1
    one = jnp.where(lane == last, 0.0, roll(v, -1, 1))
    two = jnp.where(lane >= last - 1, 0.0, roll(v, -2, 1))
    below = jnp.where(lane == 0, 0.0, roll(v, 1, 1))
    return even_columns(below + 3.0 * v + 3.0 * one + two, 0.125)


def raise_columns(v):
    lane = iota(v.shape, 1)
    last = v.shape[1] - 1
    below = jnp.where(lane == 0, 0.0, roll(v, 1, 1))
    above = jnp.where(lane == last, 0.0, roll(v, -1, 1))
    even = 3.0 * v + below
    odd = 3.0 * v + above
    coarse, fine = iota((128, 256), 0), iota((128, 256), 1)
    at_even = jnp.where(fine == 2 * coarse, 0.25, 0.0)
    at_odd = jnp.where(fine == 2 * coarse + 1, 0.25, 0.0)
    parts = []
    for k in range(v.shape[1] // 128):
        cut = slice(128 * k, 128 * (k + 1))
        parts.append(pick_right(even[:, cut], at_even) + pick_right(odd[:, cut], at_odd))
    return jnp.concatenate(parts, axis=1)


def restrict_rows(v):
    coarse, fine = iota((ME, FE), 0), iota((ME, FE), 1)
    away = fine - 2 * coarse
    weight = jnp.where((away == 0) | (away == 1), 0.375, 0.0)
    weight = weight + jnp.where((away == -1) | (away == 2), 0.125, 0.0)
    return pick_left(weight, v)


def pair_rows(v):
    coarse, fine = iota((ME, FE), 0), iota((ME, FE), 1)
    return pick_left(jnp.where(fine // 2 == coarse, 1.0, 0.0), v)


def raise_rows(v):
    fine, coarse = iota((FE, ME), 0), iota((FE, ME), 1)
    away = fine - 2 * coarse
    weight = jnp.where((away == 0) | (away == 1), 0.75, 0.0)
    weight = weight + jnp.where((away == 2) | (away == -1), 0.25, 0.0)
    return pick_left(weight, v)


def inside_middle(px):
    row = iota((ME, MZ), 0) + MX * px - MH
    return (row >= 0) & (row < MX * N_PX)


def inside_fine(px):
    row = iota((FE, FZ), 0) + FX * px - FH
    return (row >= 0) & (row < FX * N_PX)


def to_slabs(plane, out, at):
    for m in range(8):
        out[m, at] = plane[:, 128 * m : 128 * (m + 1)]


def from_slabs(ref, at):
    return jnp.concatenate([ref[m, at] for m in range(8)], axis=1)


def start(px, py, forcing, inv_density, sx, sy, force, rho, lower, upper, low, high, cx):
    square = iota((FX, FX), 0) == iota((FX, FX), 1)
    column = jnp.sum(jnp.where(square, sx[...], 0.0), axis=1, keepdims=True)
    cx[...] = jnp.broadcast_to(column, (FX, 128))
    wide = jnp.broadcast_to(column, (FX, FZ))
    edges = {}
    for at, out in ((0, lower), (1, upper)):
        f_plane, r_plane = forcing[:, at, :], inv_density[:, at, :]
        force[at] = f_plane
        rho[at] = r_plane
        out[0:32] = f_plane
        out[32:64] = r_plane
        out[64:72] = jnp.broadcast_to(sy[0:1, at : at + 1], (8, FZ))
        for row in (0, FX - 1):
            edges[at, row] = (f_plane[row : row + 1], r_plane[row : row + 1])
    for side, row, cut in ((low, 0, slice(0, 8)), (high, FX - 1, slice(24, 32))):
        for k in range(2):
            side[8 * k : 8 * k + 8] = rows_of([edges[0, row][k], edges[1, row][k]])
        side[16:24] = wide[cut]


def own_lines(px, py, force, rho, cx, sy, cz, lines, u):
    parts = []
    for at in range(2):
        parts.append(force[at] / diagonal(rho[at], cx[:, 0:1], sy[0:1, at : at + 1], cz[...]))
    solved = solve_z(jnp.concatenate(parts, axis=0), lines)
    u[0] = solved[0:FX]
    u[1] = solved[FX : 2 * FX]


def first_half(px, py, force, rho, cx, sy, cz, u, below, above, left, right, lines, slabs):
    cx_col = cx[:, 0:1]
    cz_row = cz[...]
    parts = []
    for side in (below, above):
        parts.append(side[0:32] / diagonal(side[32:64], cx_col, side[64:65], cz_row))
    cy_edge = jnp.where(iota((8, 1), 0) == 0, sy[0:1, 0:1], sy[0:1, 1:2])
    for side, row in ((left, 23), (right, 16)):
        parts.append(side[0:8] / diagonal(side[8:16], side[row : row + 1, 0:1], cy_edge, cz_row))
    solved = solve_z(jnp.concatenate(parts, axis=0), lines)
    planes = [solved[0:32], u[0], u[1], solved[32:64]]
    for at in range(2):
        own = u[at]
        before = rows_at([(7, solved[64 + at : 65 + at])])
        after = rows_at([(0, solved[72 + at : 73 + at])])
        beside_x = near_x(jnp.concatenate([before, own, after], axis=0))[FH : FH + FX]
        beside_y = planes[at] + planes[at + 2]
        cy = sy[0:1, at : at + 1]
        applied = operate(own, beside_x, beside_y, rho[at], cx_col, cy, cz_row)
        to_slabs((force[at] - applied) / diagonal(rho[at], cx_col, cy, cz_row), slabs, at)


def middle_statics(px, py, rho, cx, sy, cz, left, right, column, cx_mid, cyz_mid, told):
    coarse, fine = iota((MX, FX), 0), iota((MX, FX), 1)
    pairs = pick_left(jnp.where(fine // 2 == coarse, 1.0, 0.0), rho[0] + rho[1])
    own = pair_columns(pairs, 0.125)
    columns = jnp.concatenate([left[16:24, 0:128], cx[...], right[16:24, 0:128]], axis=0)
    cym = jnp.broadcast_to((sy[0:1, 0:1] + sy[0:1, 1:2]) * 0.125, (8, MZ))
    czm = pair_columns(jnp.broadcast_to(cz[...], (16, FZ)), 0.125)
    cx_mid[...] = pair_rows(columns) * 0.125
    cyz_mid[...] = jnp.concatenate([czm[0:1], cym[0:7]], axis=0)
    told[0:8, 0:MZ] = own[0:8]
    told[0:8, MZ:FZ] = own[8:16]
    told[8:16, 0:MZ] = jnp.broadcast_to(column[...], (8, MZ))
    told[8:16, MZ:FZ] = cym


def solve_x_fine(px, py, slabs, lines, out):
    block = lines[0]
    for at in range(2):
        column = jnp.concatenate([slabs[m, at] for m in range(8)], axis=0)
        solved = dot(block, column)
        for m in range(8):
            out[m, at] = solved[32 * m : 32 * (m + 1)]


def add_slabs(px, py, u, slabs, told, out):
    for at in range(2):
        out[FX * at : FX * (at + 1)] = u[at] + from_slabs(slabs, at)
    out[64:80] = told[...]


def half_residual(px, py, u, below, above, force, rho, y_below, y_above, cx, sy, cz, q, low, high):
    cx_col = cx[...][:, 0:1]
    cz_row = cz[...]
    us = [below[0:32], below[32:64], u[0:32], u[32:64], above[0:32], above[32:64]]
    fs = [y_below[0:32], force[0], force[1], y_above[0:32]]
    rs = [y_below[32:64], rho[0], rho[1], y_above[32:64]]
    cys = [y_below[64:65], sy[0:1, 0:1], sy[0:1, 1:2], y_above[64:65]]
    row = iota((FX, FZ), 0)
    total = None
    for j in range(4):
        own = us[j + 1]
        beside_x = jnp.where(row == 0, 0.0, roll(own, 1, 0)) + jnp.where(row == FX - 1, 0.0, roll(own, -1, 0))
        left_over = fs[j] - operate(own, beside_x, us[j] + us[j + 2], rs[j], cx_col, cys[j], cz_row)
        if j in (1, 2):
            left_over = 3.0 * left_over
        total = left_over if total is None else total + left_over
    total = total * 0.125
    q[...] = total
    for out, edge, step, cut in ((low, 0, 1, slice(0, 8)), (high, FX - 1, -1, slice(24, 32))):
        out[0:8] = total[cut]
        next_row = edge + step
        picked = [us[j + 1][edge : edge + 1] for j in range(4)]
        out[8:16] = rows_of(picked + [us[j + 1][next_row : next_row + 1] for j in range(4)])
        middle = u[64:68, 0:MZ] if edge == 0 else u[68:72, MZ:FZ]
        pairs = [jnp.concatenate([middle[2 * i : 2 * i + 1], middle[2 * i + 1 : 2 * i + 2]], axis=1) for i in range(2)]
        coarse = jnp.concatenate([u[72:73, 0:MZ], u[72:73, 0:MZ]], axis=1)
        out[16:24] = rows_of([rs[j][edge : edge + 1] for j in range(4)] + pairs + [coarse])


def to_middle(px, py, q, u, below, above, left, right, force, rho, y_below, y_above, x_left, x_right, cx, cx_mid, cyz_mid, lines, u_ext, f_ext, r_ext, cx_ext, r_mid, f_mid, v_out, told):
    columns = jnp.concatenate([x_left[16:24, 0:128], cx[...], x_right[16:24, 0:128]], axis=0)
    cx_ext[...] = columns
    told[0:16] = below[64:80]
    told[16:32] = above[64:80]
    told[32:40] = jnp.broadcast_to(right[22:23], (8, FZ))
    told[40:48] = jnp.broadcast_to(left[22:23], (8, FZ))
    us = [below[32:64], u[0:32], u[32:64], above[0:32]]
    rs = [y_below[32:64], rho[0], rho[1], y_above[32:64]]
    cross = []
    for side, row in ((left, 0), (right, FX - 1)):
        inward = outward = None
        for j in range(4):
            weight = 0.375 if j in (1, 2) else 0.125
            here = weight * rs[j][row : row + 1] * side[8 + j : 9 + j]
            there = weight * side[16 + j : 17 + j] * us[j][row : row + 1]
            inward = here if inward is None else inward + here
            outward = there if outward is None else outward + there
        at = FH + row
        beyond = at - 1 if row == 0 else at + 1
        cross.append((at, inward * columns[at : at + 1, 0:1]))
        cross.append((beyond, outward * columns[beyond : beyond + 1, 0:1]))
    total = jnp.concatenate([left[0:8], q[...], right[0:8]], axis=0)
    line = iota((FE, FZ), 0)
    for at, term in cross:
        total = total + jnp.where(line == at, term, 0.0)
    for j in range(4):
        before = rows_at([(7, left[8 + j : 9 + j]), (6, left[12 + j : 13 + j])])
        after = rows_at([(0, right[8 + j : 9 + j]), (1, right[12 + j : 13 + j])])
        u_ext[j] = jnp.concatenate([before, us[j], after], axis=0)
    for at in range(2):
        for k, own, out in ((0, force, f_ext), (8, rho, r_ext)):
            before = rows_at([(7, x_left[k + at : k + at + 1])])
            after = rows_at([(0, x_right[k + at : k + at + 1])])
            out[at] = jnp.concatenate([before, own[at], after], axis=0)
    dense = []
    for side, first in ((left, 4), (right, 0)):
        rows = []
        for i in range(2):
            line = side[20 + i : 21 + i]
            rows.append((first + 2 * i, line[:, 0:MZ]))
            rows.append((first + 2 * i + 1, line[:, MZ:FZ]))
        dense.append(rows_at(rows))
    dense[1:1] = [u[64:72, 0:MZ], u[64:72, MZ:FZ]]
    r_mid[...] = roll(jnp.concatenate(dense, axis=0), MH - 8, 0)[0:ME]
    rhs = restrict_columns(restrict_rows(total))
    rhs = jnp.where(inside_middle(px), rhs, 0.0)
    f_mid[...] = rhs
    diag = diagonal(*middle_parts(r_mid, cx_mid, cyz_mid))
    v_out[...] = solve_z(rhs / diag, lines)


def middle_parts(r_mid, cx_mid, cyz_mid):
    return r_mid[...], cx_mid[:, 0:1], cyz_mid[1:2], cyz_mid[0:1]


def middle_scaled(px, py, v, below, above, f_mid, r_mid, cx_mid, cyz_mid, out):
    rho, cx, cy, cz = middle_parts(r_mid, cx_mid, cyz_mid)
    own = v[...]
    applied = operate(own, near_x(own), below[...] + above[...], rho, cx, cy, cz)
    scaled = (f_mid[...] - applied) / diagonal(rho, cx, cy, cz)
    part = roll(scaled, -MH, 0)[0:MX]
    for i in range(out.shape[0]):
        out[i] = part


def rows_for_x(px, py, lines, out):
    place, row_of_four = px % 4, px // 4
    total = MX * N_PX
    parts = []
    for i in range(8):
        base = MX * (4 * i + place)
        pieces = [
            dyn(lines, jnp.maximum(base - 8, 0), 8),
            dyn(lines, base, MX),
            dyn(lines, jnp.minimum(base + MX, total - 8), 8),
        ]
        rows = roll(jnp.concatenate(pieces, axis=0), MH - 8, 0)[0:ME]
        at = iota((ME, 256), 0) + base - MH
        first = 256 * (row_of_four // 4)
        parts.append(jnp.where((at >= first) & (at < first + 256), rows, 0.0))
    full = jnp.concatenate(parts, axis=0)
    held = None
    for i in range(4):
        cut = jnp.where(row_of_four % 4 == i, full[:, 64 * i : 64 * (i + 1)], 0.0)
        held = cut if held is None else held + cut
    out[...] = held


def spread_x(px, py, gathered, rows, out):
    solved = dot(rows[...], gathered[...])
    for i in range(8):
        out[i] = solved[ME * i : ME * (i + 1)]


def gain_x(px, py, v, parts, out):
    total = v[...]
    for i in range(8):
        total = total + parts[i]
    out[...] = total


def solve_x_block(px, py, gathered, lines, v, out):
    total = MX * N_PX
    pieces = []
    starts = (
        (jnp.maximum(MX * px - 8, 0), 8),
        (MX * px, MX),
        (jnp.minimum(MX * px + MX, total - 8), 8),
    )
    for start, size in starts:
        pieces.append(dyn(lines, start, size))
    full = dot(jnp.concatenate(pieces, axis=0), gathered[...])
    part = roll(full, MH - 8, 0)[0:ME]
    row = iota((ME, MZ), 0) + MX * px - MH
    first = 256 * (px // 16)
    held = (row >= first) & (row < first + 256)
    out[...] = jnp.where(held, v[...] + part, 0.0)


def mend(px, py, v, other, out):
    row = iota((ME, MZ), 0)
    theirs = other[...]
    up = jnp.where((row >= MH + MX) & (px == 15), roll(theirs, MX, 0), 0.0)
    down = jnp.where((row < MH) & (px == 16), roll(theirs, -MX, 0), 0.0)
    out[...] = v[...] + (up + down)


def block_mean(px, py, v, f_mid, r_mid, cx_mid, cyz_mid, told, column, out):
    rho, cx, cy, cz = middle_parts(r_mid, cx_mid, cyz_mid)
    own = v[...]
    applied = operate(own, near_x(own), 0.0, rho, cx, cy, cz)
    row = iota((ME, MZ), 0)
    kept = jnp.where((row >= MH) & (row < MH + MX), f_mid[...] - applied, 0.0)

    def mean(a):
        return jnp.sum(jnp.sum(a, axis=0, keepdims=True), axis=1, keepdims=True) * (1.0 / (MX * MZ))

    sent = column[...] * mean(kept)
    inner = roll(own, -MH, 0)[0:MX]
    for at in (0, 16):
        share = mean(told[at : at + 8, 0:MZ] * inner[0:8] + told[at : at + 8, MZ:FZ] * inner[8:16])
        sent = sent + told[at + 8 : at + 9, 0:MZ] * (share * told[at + 8 : at + 9, MZ : MZ + 1])
    for at, edge, inner_row, mine in ((32, MH + MX, MH + MX - 1, px == 15), (40, MH - 1, MH, px == 16)):
        line = r_mid[edge : edge + 1] * cx_mid[edge : edge + 1, 0:1] * v[inner_row : inner_row + 1]
        sent = sent + told[at : at + 1, 0:MZ] * jnp.where(mine, mean(line), 0.0)
    lane = iota((8, MZ), 1)
    at_x, at_y = lane % N_PX, lane // N_PX
    wide = jnp.broadcast_to(sent, (8, MZ))
    rows = []
    for dy in (-1, 0, 1):
        for dx in (-1, 0, 1):
            held = (at_x + dx >= 0) & (at_x + dx < N_PX) & (at_y + dy >= 0) & (at_y + dy < N_PY)
            rows.append(jnp.where(held, roll(wide, -(dy * N_PX + dx), 1), 0.0)[0:1])
    stacked = jnp.concatenate([rows_of(rows[0:8]), rows_of(rows[8:9])], axis=0)
    unit = jnp.where(iota((16, 128), 0) == iota((16, 128), 1), 1.0, 0.0).astype(bf16)
    high, middle, low = thirds(stacked)
    dims = ((0,), (0,))
    out[...] = product(high, unit, dims) + (product(middle, unit, dims) + product(low, unit, dims))


def second_half(px, py, parts, v, below, above, f_mid, r_mid, cx_mid, cyz_mid, lines, out):
    total = jnp.sum(parts[...], axis=0, keepdims=True)
    row = iota((ME, MZ), 0)

    def raised(plane, dy):
        at = [total[0:1, 3 * (dy + 1) + dx : 3 * (dy + 1) + dx + 1] for dx in range(3)]
        return plane + jnp.where(row < MH, at[0], jnp.where(row < MH + MX, at[1], at[2]))

    own = raised(v[...], 0)
    beside = raised(below[...], -1) + raised(above[...], 1)
    rho, cx, cy, cz = middle_parts(r_mid, cx_mid, cyz_mid)
    applied = operate(own, near_x(own), beside, rho, cx, cy, cz)
    out[...] = own + solve_z((f_mid[...] - applied) / diagonal(rho, cx, cy, cz), lines)


def to_fine(px, py, v, below, above, u_ext, f_ext, r_ext, cx_ext, sy, cz, lines, out, lower, upper):
    rows = [raise_rows(p[...]) for p in (below, v, above)]
    columns = raise_columns(jnp.concatenate(rows, axis=0)) * 0.25
    raised = [columns[FE * i : FE * (i + 1)] for i in range(3)]
    mids = [
        3.0 * raised[0] + raised[1],
        3.0 * raised[1] + raised[0],
        3.0 * raised[1] + raised[2],
        3.0 * raised[2] + raised[1],
    ]
    inside = inside_fine(px)
    us = []
    for j in range(4):
        held = inside
        if j == 0:
            held = inside & (py > 0)
        if j == 3:
            held = inside & (py < N_PY - 1)
        us.append(u_ext[j] + jnp.where(held, mids[j], 0.0))
    cx_col = cx_ext[:, 0:1]
    cz_row = cz[...]
    parts = []
    for at in range(2):
        own = us[at + 1]
        cy = sy[0:1, at : at + 1]
        applied = operate(own, near_x(own), us[at] + us[at + 2], r_ext[at], cx_col, cy, cz_row)
        parts.append((f_ext[at] - applied) / diagonal(r_ext[at], cx_col, cy, cz_row))
    solved = solve_z(jnp.concatenate(parts, axis=0), lines)
    for at in range(2):
        new = us[at + 1] + solved[FE * at : FE * (at + 1)]
        out[at] = new
        (lower if at == 0 else upper)[...] = new[FH : FH + FX]


def last_scaled(px, py, u, below, above, f_ext, r_ext, cx_ext, sy, cz, slabs):
    cx_col = cx_ext[FH : FH + FX, 0:1]
    cz_row = cz[...]
    inner = slice(FH, FH + FX)
    for at in range(2):
        full = u[at]
        beside_x = near_x(full)[inner]
        own = full[inner]
        beside_y = (below[...] if at == 0 else u[0, inner]) + (above[...] if at == 1 else u[1, inner])
        rho = r_ext[at, inner]
        cy = sy[0:1, at : at + 1]
        applied = operate(own, beside_x, beside_y, rho, cx_col, cy, cz_row)
        scaled = (f_ext[at, inner] - applied) / diagonal(rho, cx_col, cy, cz_row)
        to_slabs(scaled, slabs, at)


def finish(px, py, u, slabs, out):
    for at in range(2):
        out[:, at, :] = u[at, FH : FH + FX] + from_slabs(slabs, at)


class Device:
    def run(self, stage, shapes, *args):
        def kernel(*refs):
            stage(lax.axis_index("px"), lax.axis_index("py"), *refs)

        whole = pl.BlockSpec(memory_space=pltpu.VMEM)
        outs = pl.pallas_call(
            kernel,
            out_shape=[jax.ShapeDtypeStruct(s, f32) for s in shapes],
            in_specs=[whole] * len(args),
            out_specs=[whole] * len(shapes),
            compiler_params=pltpu.CompilerParams(vmem_limit_bytes=24 * 1024 * 1024),
        )(*args)
        return outs if len(shapes) > 1 else outs[0]

    def local(self, fn, *args):
        return fn(*args)

    def block_of(self, lines):
        at = lax.axis_index("px") // 8
        return lax.dynamic_slice_in_dim(lines, at, 1, axis=0)

    def beside(self, axis, low, high):
        n = lax.axis_size(axis)
        up = [(i, i + 1) for i in range(n - 1)]
        down = [(j, i) for i, j in up]
        return lax.ppermute(high, axis, up), lax.ppermute(low, axis, down)

    def across(self, array):
        return lax.ppermute(array, "px", [(15, 16), (16, 15)])

    def everyone(self, rows):
        sent = rows.reshape(N_PX * N_PY, 1, 128)
        got = lax.all_to_all(sent, ("py", "px"), 0, 0, tiled=True)
        return got.reshape(N_PX * N_PY, 128)

    def solve_x(self, every, rows):
        fours = [list(range(k, k + 4)) for k in range(0, N_PX, 4)]
        eights = [list(range(k, N_PX, 4)) for k in range(4)]
        every = lax.all_to_all(every, "px", 0, 0, axis_index_groups=fours, tiled=True)
        parts = self.run(spread_x, [(8, ME, MZ)], every.reshape(4 * MX, MZ), rows)
        return lax.all_to_all(parts, "px", 0, 0, axis_index_groups=eights, tiled=True)

    def swap(self, axis, array, group):
        n = lax.axis_size(axis)
        groups = None
        if group < n:
            groups = [list(range(k, k + group)) for k in range(0, n, group)]
        return lax.all_to_all(array, axis, 0, 0, axis_index_groups=groups, tiled=True)


def cycle(d, forcing, inv_density, stretch_x, stretch_y, stretch_z, lines_z0, lines_x0, lines_z1, lines_x1, column):
    sx = d.local(lambda a: a.reshape(1, FX), stretch_x)
    sy = d.local(lambda a: a.reshape(1, 2), stretch_y)
    cz = d.local(lambda a: a.reshape(1, FZ), stretch_z)
    rows_x1 = d.local(lambda a: a.reshape(MX * N_PX, 256), lines_x1)
    slab, own, mid = (8, 2, FX, 128), (2, FX, FZ), (ME, MZ)

    force, rho, lower, upper, low, high, cx = d.run(
        start,
        [own, own, (72, FZ), (72, FZ), (24, FZ), (24, FZ), (FX, 128)],
        forcing, inv_density, sx, sy,
    )
    y_below, y_above = d.beside("py", lower, upper)
    x_left, x_right = d.beside("px", low, high)
    block = d.block_of(lines_x0)
    rows_x = d.run(rows_for_x, [(8 * ME, 64)], rows_x1)
    u = d.run(own_lines, [own], force, rho, cx, sy, cz, lines_z0)
    slabs = d.run(
        first_half, [slab],
        force, rho, cx, sy, cz, u, y_below, y_above, x_left, x_right, lines_z0,
    )
    slabs = d.swap("px", slabs, 8)
    cx_mid, cyz_mid, told = d.run(
        middle_statics,
        [(ME, 128), (8, MZ), (16, FZ)],
        rho, cx, sy, cz, x_left, x_right, column,
    )
    slabs = d.run(solve_x_fine, [slab], slabs, block)
    slabs = d.swap("px", slabs, 8)
    u = d.run(add_slabs, [(80, FZ)], u, slabs, told)
    below, above = d.beside("py", u, u)
    q, low, high = d.run(
        half_residual, [(FX, FZ), (24, FZ), (24, FZ)],
        u, below, above, force, rho, y_below, y_above, cx, sy, cz,
    )
    left, right = d.beside("px", low, high)
    u_ext, f_ext, r_ext, cx_ext, r_mid, f_mid, v, told = d.run(
        to_middle,
        [(4, FE, FZ), (2, FE, FZ), (2, FE, FZ), (FE, 128), mid, mid, mid, (48, FZ)],
        q, u, below, above, left, right, force, rho, y_below, y_above, x_left, x_right,
        cx, cx_mid, cyz_mid, lines_z1,
    )
    statics = (f_mid, r_mid, cx_mid, cyz_mid)

    below, above = d.beside("py", v, v)
    every = d.run(middle_scaled, [(16, MX, MZ)], v, below, above, *statics)
    every = d.swap("px", every, 16)
    every = d.local(lambda a: a.reshape(256, MZ), every)
    v = d.run(solve_x_block, [mid], every, rows_x1, v)
    other = d.across(v)
    sent = d.run(block_mean, [(N_PX * N_PY, 128)], v, *statics, told, column)
    parts = d.everyone(sent)
    v = d.run(mend, [mid], v, other)
    below, above = d.beside("py", v, v)
    v = d.run(second_half, [mid], parts, v, below, above, *statics, lines_z1)
    below, above = d.beside("py", v, v)
    parts = d.solve_x(d.run(middle_scaled, [(4, MX, MZ)], v, below, above, *statics), rows_x)
    v = d.run(gain_x, [mid], v, parts)

    below, above = d.beside("py", v, v)
    u, lower, upper = d.run(
        to_fine,
        [(2, FE, FZ), (FX, FZ), (FX, FZ)],
        v, below, above, u_ext, f_ext, r_ext, cx_ext, sy, cz, lines_z0,
    )
    below, above = d.beside("py", lower, upper)
    slabs = d.run(last_scaled, [slab], u, below, above, f_ext, r_ext, cx_ext, sy, cz)
    slabs = d.swap("px", slabs, 8)
    slabs = d.run(solve_x_fine, [slab], slabs, block)
    slabs = d.swap("px", slabs, 8)
    return d.run(finish, [(FX, 2, FZ)], u, slabs)


def solution(mesh):
    placed = (
        P("px", "py", None),
        P("px", "py", None),
        P("px"),
        P("py"),
        P(),
        P(),
        P(),
        P(),
        P(),
        P(("py", "px"), None),
    )

    def step(*args):
        return cycle(Device(), *args)

    return jax.shard_map(
        step, mesh=mesh, in_specs=placed, out_specs=P("px", "py", None), check_vma=False
    )
```

```python
import jax
import jax.numpy as jnp
from jax import lax
from jax.experimental import pallas as pl
from jax.experimental.pallas import tpu as pltpu
from jax.sharding import PartitionSpec as P


shift_term = 0.1
f32 = jnp.float32
bf16 = jnp.bfloat16

N_PY, N_PX = 16, 32
FX, FZ = 32, 1024
MX, MZ = 16, 512
FH, MH = 8, 4
FE, ME = FX + 2 * FH, MX + 2 * MH


def roll(v, shift, axis):
    return pltpu.roll(v, shift % v.shape[axis], axis)


def dyn(ref, start, size):
    return ref[pl.ds(pl.multiple_of(start, 8), size), :]


def halves(a):
    high = a.astype(bf16)
    return high, (a - high.astype(f32)).astype(bf16)


def thirds(a):
    high, rest = a.astype(bf16), None
    rest = a - high.astype(f32)
    middle = rest.astype(bf16)
    return high, middle, (rest - middle.astype(f32)).astype(bf16)


def product(a, b, dims):
    return lax.dot_general(a, b, (dims, ((), ())), preferred_element_type=f32)


def dot(a, b, dims=((1,), (0,))):
    a_high, a_low = halves(a)
    b_high, b_low = halves(b)
    return product(a_high, b_high, dims) + (product(a_high, b_low, dims) + product(a_low, b_high, dims))


def pick_right(a, weight):
    dims = ((1,), (0,))
    w = weight.astype(bf16)
    high, middle, low = thirds(a)
    return product(high, w, dims) + (product(middle, w, dims) + product(low, w, dims))


def pick_left(weight, a):
    dims = ((1,), (0,))
    w = weight.astype(bf16)
    high, middle, low = thirds(a)
    return product(w, high, dims) + (product(w, middle, dims) + product(w, low, dims))


def iota(shape, axis):
    return lax.broadcasted_iota(jnp.int32, shape, axis)


def rows_of(rows):
    at = iota((8, rows[0].shape[1]), 0)
    total = jnp.zeros((8, rows[0].shape[1]), f32)
    for i, row in enumerate(rows):
        total = jnp.where(at == i, row, total)
    return total


def rows_at(pairs):
    at = iota((8, pairs[0][1].shape[1]), 0)
    total = jnp.zeros((8, pairs[0][1].shape[1]), f32)
    for i, row in pairs:
        total = jnp.where(at == i, row, total)
    return total


def near_z(v):
    lane = iota(v.shape, 1)
    last = v.shape[1] - 1
    below = jnp.where(lane == 0, 0.0, roll(v, 1, 1))
    above = jnp.where(lane == last, 0.0, roll(v, -1, 1))
    return below + above


def near_x(v):
    return roll(v, 1, 0) + roll(v, -1, 0)


def operate(v, v_near_x, v_near_y, rho, cx, cy, cz):
    twice = 2.0 * v
    stencil = cx * (twice - v_near_x) + cy * (twice - v_near_y) + cz * (twice - near_z(v))
    return shift_term * v + rho * stencil


def diagonal(rho, cx, cy, cz):
    return shift_term + 2.0 * rho * (cx + cy + cz)


def solve_z(w, lines):
    count, size = lines.shape[0], lines.shape[1]
    parts = []
    for k in range(count):
        parts.append(dot(w[:, k * size : (k + 1) * size], lines[k], ((1,), (1,))))
    return jnp.concatenate(parts, axis=1)


def columns_by(v, pick):
    cuts = [slice(256 * k, 256 * (k + 1)) for k in range(v.shape[1] // 256)]
    return jnp.concatenate([pick_right(v[:, cut], pick) for cut in cuts], axis=1)


def pair_columns(v, scale):
    fine, coarse = iota((256, 128), 0), iota((256, 128), 1)
    return columns_by(v, jnp.where(fine // 2 == coarse, scale, 0.0))


def even_columns(v, scale):
    fine, coarse = iota((256, 128), 0), iota((256, 128), 1)
    return columns_by(v, jnp.where(fine == 2 * coarse, scale, 0.0))


def restrict_columns(v):
    lane = iota(v.shape, 1)
    last = v.shape[1] - 1
    one = jnp.where(lane == last, 0.0, roll(v, -1, 1))
    two = jnp.where(lane >= last - 1, 0.0, roll(v, -2, 1))
    below = jnp.where(lane == 0, 0.0, roll(v, 1, 1))
    return even_columns(below + 3.0 * v + 3.0 * one + two, 0.125)


def raise_columns(v):
    lane = iota(v.shape, 1)
    last = v.shape[1] - 1
    below = jnp.where(lane == 0, 0.0, roll(v, 1, 1))
    above = jnp.where(lane == last, 0.0, roll(v, -1, 1))
    even = 3.0 * v + below
    odd = 3.0 * v + above
    coarse, fine = iota((128, 256), 0), iota((128, 256), 1)
    at_even = jnp.where(fine == 2 * coarse, 0.25, 0.0)
    at_odd = jnp.where(fine == 2 * coarse + 1, 0.25, 0.0)
    parts = []
    for k in range(v.shape[1] // 128):
        cut = slice(128 * k, 128 * (k + 1))
        parts.append(pick_right(even[:, cut], at_even) + pick_right(odd[:, cut], at_odd))
    return jnp.concatenate(parts, axis=1)


def restrict_rows(v):
    coarse, fine = iota((ME, FE), 0), iota((ME, FE), 1)
    away = fine - 2 * coarse
    weight = jnp.where((away == 0) | (away == 1), 0.375, 0.0)
    weight = weight + jnp.where((away == -1) | (away == 2), 0.125, 0.0)
    return pick_left(weight, v)


def pair_rows(v):
    coarse, fine = iota((ME, FE), 0), iota((ME, FE), 1)
    return pick_left(jnp.where(fine // 2 == coarse, 1.0, 0.0), v)


def raise_rows(v):
    fine, coarse = iota((FE, ME), 0), iota((FE, ME), 1)
    away = fine - 2 * coarse
    weight = jnp.where((away == 0) | (away == 1), 0.75, 0.0)
    weight = weight + jnp.where((away == 2) | (away == -1), 0.25, 0.0)
    return pick_left(weight, v)


def inside_middle(px):
    row = iota((ME, MZ), 0) + MX * px - MH
    return (row >= 0) & (row < MX * N_PX)


def inside_fine(px):
    row = iota((FE, FZ), 0) + FX * px - FH
    return (row >= 0) & (row < FX * N_PX)


def to_slabs(plane, out, at):
    for m in range(8):
        out[m, at] = plane[:, 128 * m : 128 * (m + 1)]


def from_slabs(ref, at):
    return jnp.concatenate([ref[m, at] for m in range(8)], axis=1)


def start(px, py, forcing, inv_density, sx, sy, force, rho, lower, upper, low, high, cx):
    square = iota((FX, FX), 0) == iota((FX, FX), 1)
    column = jnp.sum(jnp.where(square, sx[...], 0.0), axis=1, keepdims=True)
    cx[...] = jnp.broadcast_to(column, (FX, 128))
    wide = jnp.broadcast_to(column, (FX, FZ))
    edges = {}
    for at, out in ((0, lower), (1, upper)):
        f_plane, r_plane = forcing[:, at, :], inv_density[:, at, :]
        force[at] = f_plane
        rho[at] = r_plane
        out[0:32] = f_plane
        out[32:64] = r_plane
        out[64:72] = jnp.broadcast_to(sy[0:1, at : at + 1], (8, FZ))
        for row in (0, FX - 1):
            edges[at, row] = (f_plane[row : row + 1], r_plane[row : row + 1])
    for side, row, cut in ((low, 0, slice(0, 8)), (high, FX - 1, slice(24, 32))):
        for k in range(2):
            side[8 * k : 8 * k + 8] = rows_of([edges[0, row][k], edges[1, row][k]])
        side[16:24] = wide[cut]


def own_lines(px, py, force, rho, cx, sy, cz, lines, u):
    parts = []
    for at in range(2):
        parts.append(force[at] / diagonal(rho[at], cx[:, 0:1], sy[0:1, at : at + 1], cz[...]))
    solved = solve_z(jnp.concatenate(parts, axis=0), lines)
    u[0] = solved[0:FX]
    u[1] = solved[FX : 2 * FX]


def first_half(px, py, force, rho, cx, sy, cz, u, below, above, left, right, lines, slabs):
    cx_col = cx[:, 0:1]
    cz_row = cz[...]
    parts = []
    for side in (below, above):
        parts.append(side[0:32] / diagonal(side[32:64], cx_col, side[64:65], cz_row))
    cy_edge = jnp.where(iota((8, 1), 0) == 0, sy[0:1, 0:1], sy[0:1, 1:2])
    for side, row in ((left, 23), (right, 16)):
        parts.append(side[0:8] / diagonal(side[8:16], side[row : row + 1, 0:1], cy_edge, cz_row))
    solved = solve_z(jnp.concatenate(parts, axis=0), lines)
    planes = [solved[0:32], u[0], u[1], solved[32:64]]
    for at in range(2):
        own = u[at]
        before = rows_at([(7, solved[64 + at : 65 + at])])
        after = rows_at([(0, solved[72 + at : 73 + at])])
        beside_x = near_x(jnp.concatenate([before, own, after], axis=0))[FH : FH + FX]
        beside_y = planes[at] + planes[at + 2]
        cy = sy[0:1, at : at + 1]
        applied = operate(own, beside_x, beside_y, rho[at], cx_col, cy, cz_row)
        to_slabs((force[at] - applied) / diagonal(rho[at], cx_col, cy, cz_row), slabs, at)


def middle_statics(px, py, rho, cx, sy, cz, left, right, column, cx_mid, cyz_mid, told):
    coarse, fine = iota((MX, FX), 0), iota((MX, FX), 1)
    pairs = pick_left(jnp.where(fine // 2 == coarse, 1.0, 0.0), rho[0] + rho[1])
    own = pair_columns(pairs, 0.125)
    columns = jnp.concatenate([left[16:24, 0:128], cx[...], right[16:24, 0:128]], axis=0)
    cym = jnp.broadcast_to((sy[0:1, 0:1] + sy[0:1, 1:2]) * 0.125, (8, MZ))
    czm = pair_columns(jnp.broadcast_to(cz[...], (16, FZ)), 0.125)
    cx_mid[...] = pair_rows(columns) * 0.125
    cyz_mid[...] = jnp.concatenate([czm[0:1], cym[0:7]], axis=0)
    told[0:8, 0:MZ] = own[0:8]
    told[0:8, MZ:FZ] = own[8:16]
    told[8:16, 0:MZ] = jnp.broadcast_to(column[...], (8, MZ))
    told[8:16, MZ:FZ] = cym


def solve_x_fine(px, py, slabs, lines, out):
    block = lines[0]
    for at in range(2):
        column = jnp.concatenate([slabs[m, at] for m in range(8)], axis=0)
        solved = dot(block, column)
        for m in range(8):
            out[m, at] = solved[32 * m : 32 * (m + 1)]


def add_slabs(px, py, u, slabs, told, out):
    for at in range(2):
        out[FX * at : FX * (at + 1)] = u[at] + from_slabs(slabs, at)
    out[64:80] = told[...]


def half_residual(px, py, u, below, above, force, rho, y_below, y_above, cx, sy, cz, q, low, high):
    cx_col = cx[...][:, 0:1]
    cz_row = cz[...]
    us = [below[0:32], below[32:64], u[0:32], u[32:64], above[0:32], above[32:64]]
    fs = [y_below[0:32], force[0], force[1], y_above[0:32]]
    rs = [y_below[32:64], rho[0], rho[1], y_above[32:64]]
    cys = [y_below[64:65], sy[0:1, 0:1], sy[0:1, 1:2], y_above[64:65]]
    row = iota((FX, FZ), 0)
    total = None
    for j in range(4):
        own = us[j + 1]
        beside_x = jnp.where(row == 0, 0.0, roll(own, 1, 0)) + jnp.where(row == FX - 1, 0.0, roll(own, -1, 0))
        left_over = fs[j] - operate(own, beside_x, us[j] + us[j + 2], rs[j], cx_col, cys[j], cz_row)
        if j in (1, 2):
            left_over = 3.0 * left_over
        total = left_over if total is None else total + left_over
    total = total * 0.125
    q[...] = total
    for out, edge, step, cut in ((low, 0, 1, slice(0, 8)), (high, FX - 1, -1, slice(24, 32))):
        out[0:8] = total[cut]
        next_row = edge + step
        picked = [us[j + 1][edge : edge + 1] for j in range(4)]
        out[8:16] = rows_of(picked + [us[j + 1][next_row : next_row + 1] for j in range(4)])
        middle = u[64:68, 0:MZ] if edge == 0 else u[68:72, MZ:FZ]
        pairs = [jnp.concatenate([middle[2 * i : 2 * i + 1], middle[2 * i + 1 : 2 * i + 2]], axis=1) for i in range(2)]
        coarse = jnp.concatenate([u[72:73, 0:MZ], u[72:73, 0:MZ]], axis=1)
        out[16:24] = rows_of([rs[j][edge : edge + 1] for j in range(4)] + pairs + [coarse])


def to_middle(px, py, q, u, below, above, left, right, force, rho, y_below, y_above, x_left, x_right, cx, sy, cx_mid, cyz_mid, lines, u_ext, f_ext, r_ext, cx_ext, cy_ext, r_mid, f_mid, v_out, told):
    columns = jnp.concatenate([x_left[16:24, 0:128], cx[...], x_right[16:24, 0:128]], axis=0)
    cx_ext[...] = columns
    told[0:16] = below[64:80]
    told[16:32] = above[64:80]
    told[32:40] = jnp.broadcast_to(right[22:23], (8, FZ))
    told[40:48] = jnp.broadcast_to(left[22:23], (8, FZ))
    us = [below[32:64], u[0:32], u[32:64], above[0:32]]
    rs = [y_below[32:64], rho[0], rho[1], y_above[32:64]]
    cross = []
    for side, row in ((left, 0), (right, FX - 1)):
        inward = outward = None
        for j in range(4):
            weight = 0.375 if j in (1, 2) else 0.125
            here = weight * rs[j][row : row + 1] * side[8 + j : 9 + j]
            there = weight * side[16 + j : 17 + j] * us[j][row : row + 1]
            inward = here if inward is None else inward + here
            outward = there if outward is None else outward + there
        at = FH + row
        beyond = at - 1 if row == 0 else at + 1
        cross.append((at, inward * columns[at : at + 1, 0:1]))
        cross.append((beyond, outward * columns[beyond : beyond + 1, 0:1]))
    total = jnp.concatenate([left[0:8], q[...], right[0:8]], axis=0)
    line = iota((FE, FZ), 0)
    for at, term in cross:
        total = total + jnp.where(line == at, term, 0.0)
    none = jnp.zeros((8, FZ), f32)
    u_ext[0] = jnp.concatenate([none, below[0:32], none], axis=0)
    u_ext[5] = jnp.concatenate([none, above[32:64], none], axis=0)
    for j in range(4):
        before = rows_at([(7, left[8 + j : 9 + j]), (6, left[12 + j : 13 + j])])
        after = rows_at([(0, right[8 + j : 9 + j]), (1, right[12 + j : 13 + j])])
        u_ext[j + 1] = jnp.concatenate([before, us[j], after], axis=0)
    for at in range(2):
        for k, own, out in ((0, force, f_ext), (8, rho, r_ext)):
            before = rows_at([(7, x_left[k + at : k + at + 1])])
            after = rows_at([(0, x_right[k + at : k + at + 1])])
            out[at + 1] = jnp.concatenate([before, own[at], after], axis=0)
    for side, at in ((y_below, 0), (y_above, 3)):
        f_ext[at] = jnp.concatenate([none, side[0:32], none], axis=0)
        r_ext[at] = jnp.concatenate([none, side[32:64], none], axis=0)
    cy_rows = [jnp.broadcast_to(sy[0:1, at : at + 1], (1, FZ)) for at in range(2)]
    cy_ext[...] = rows_of([y_below[64:65], cy_rows[0], cy_rows[1], y_above[64:65]])
    dense = []
    for side, first in ((left, 4), (right, 0)):
        rows = []
        for i in range(2):
            line = side[20 + i : 21 + i]
            rows.append((first + 2 * i, line[:, 0:MZ]))
            rows.append((first + 2 * i + 1, line[:, MZ:FZ]))
        dense.append(rows_at(rows))
    dense[1:1] = [u[64:72, 0:MZ], u[64:72, MZ:FZ]]
    r_mid[...] = roll(jnp.concatenate(dense, axis=0), MH - 8, 0)[0:ME]
    rhs = restrict_columns(restrict_rows(total))
    rhs = jnp.where(inside_middle(px), rhs, 0.0)
    f_mid[...] = rhs
    diag = diagonal(*middle_parts(r_mid, cx_mid, cyz_mid))
    v_out[...] = solve_z(rhs / diag, lines)


def middle_parts(r_mid, cx_mid, cyz_mid):
    return r_mid[...], cx_mid[:, 0:1], cyz_mid[1:2], cyz_mid[0:1]


def middle_scaled(px, py, v, below, above, f_mid, r_mid, cx_mid, cyz_mid, out):
    rho, cx, cy, cz = middle_parts(r_mid, cx_mid, cyz_mid)
    own = v[...]
    applied = operate(own, near_x(own), below[...] + above[...], rho, cx, cy, cz)
    scaled = (f_mid[...] - applied) / diagonal(rho, cx, cy, cz)
    part = roll(scaled, -MH, 0)[0:MX]
    for i in range(out.shape[0]):
        out[i] = part


def rows_for_x(px, py, lines, out):
    place, row_of_four = px % 4, px // 4
    total = MX * N_PX
    parts = []
    for i in range(8):
        base = MX * (4 * i + place)
        pieces = [
            dyn(lines, jnp.maximum(base - 8, 0), 8),
            dyn(lines, base, MX),
            dyn(lines, jnp.minimum(base + MX, total - 8), 8),
        ]
        rows = roll(jnp.concatenate(pieces, axis=0), MH - 8, 0)[0:ME]
        at = iota((ME, 256), 0) + base - MH
        first = 256 * (row_of_four // 4)
        parts.append(jnp.where((at >= first) & (at < first + 256), rows, 0.0))
    full = jnp.concatenate(parts, axis=0)
    held = None
    for i in range(4):
        cut = jnp.where(row_of_four % 4 == i, full[:, 64 * i : 64 * (i + 1)], 0.0)
        held = cut if held is None else held + cut
    out[...] = held


def spread_x(px, py, gathered, rows, out):
    solved = dot(rows[...], gathered[...])
    for i in range(8):
        out[i] = solved[ME * i : ME * (i + 1)]


def gain_x(px, py, v, parts, out):
    total = v[...]
    for i in range(8):
        total = total + parts[i]
    out[...] = total


def solve_x_block(px, py, gathered, lines, v, out):
    total = MX * N_PX
    pieces = []
    starts = (
        (jnp.maximum(MX * px - 8, 0), 8),
        (MX * px, MX),
        (jnp.minimum(MX * px + MX, total - 8), 8),
    )
    for start, size in starts:
        pieces.append(dyn(lines, start, size))
    full = dot(jnp.concatenate(pieces, axis=0), gathered[...])
    part = roll(full, MH - 8, 0)[0:ME]
    row = iota((ME, MZ), 0) + MX * px - MH
    first = 256 * (px // 16)
    held = (row >= first) & (row < first + 256)
    out[...] = jnp.where(held, v[...] + part, 0.0)


def mend(px, py, v, other, out):
    row = iota((ME, MZ), 0)
    theirs = other[...]
    up = jnp.where((row >= MH + MX) & (px == 15), roll(theirs, MX, 0), 0.0)
    down = jnp.where((row < MH) & (px == 16), roll(theirs, -MX, 0), 0.0)
    out[...] = v[...] + (up + down)


def block_mean(px, py, v, f_mid, r_mid, cx_mid, cyz_mid, told, column, out):
    rho, cx, cy, cz = middle_parts(r_mid, cx_mid, cyz_mid)
    own = v[...]
    applied = operate(own, near_x(own), 0.0, rho, cx, cy, cz)
    row = iota((ME, MZ), 0)
    kept = jnp.where((row >= MH) & (row < MH + MX), f_mid[...] - applied, 0.0)

    def mean(a):
        return jnp.sum(jnp.sum(a, axis=0, keepdims=True), axis=1, keepdims=True) * (1.0 / (MX * MZ))

    sent = column[...] * mean(kept)
    inner = roll(own, -MH, 0)[0:MX]
    for at in (0, 16):
        share = mean(told[at : at + 8, 0:MZ] * inner[0:8] + told[at : at + 8, MZ:FZ] * inner[8:16])
        sent = sent + told[at + 8 : at + 9, 0:MZ] * (share * told[at + 8 : at + 9, MZ : MZ + 1])
    for at, edge, inner_row, mine in ((32, MH + MX, MH + MX - 1, px == 15), (40, MH - 1, MH, px == 16)):
        line = r_mid[edge : edge + 1] * cx_mid[edge : edge + 1, 0:1] * v[inner_row : inner_row + 1]
        sent = sent + told[at : at + 1, 0:MZ] * jnp.where(mine, mean(line), 0.0)
    lane = iota((8, MZ), 1)
    at_x, at_y = lane % N_PX, lane // N_PX
    wide = jnp.broadcast_to(sent, (8, MZ))
    rows = []
    for dy in (-1, 0, 1):
        for dx in (-1, 0, 1):
            held = (at_x + dx >= 0) & (at_x + dx < N_PX) & (at_y + dy >= 0) & (at_y + dy < N_PY)
            rows.append(jnp.where(held, roll(wide, -(dy * N_PX + dx), 1), 0.0)[0:1])
    stacked = jnp.concatenate([rows_of(rows[0:8]), rows_of(rows[8:9])], axis=0)
    unit = jnp.where(iota((16, 128), 0) == iota((16, 128), 1), 1.0, 0.0).astype(bf16)
    high, middle, low = thirds(stacked)
    dims = ((0,), (0,))
    out[...] = product(high, unit, dims) + (product(middle, unit, dims) + product(low, unit, dims))


def second_half(px, py, parts, v, below, above, f_mid, r_mid, cx_mid, cyz_mid, lines, out):
    total = jnp.sum(parts[...], axis=0, keepdims=True)
    row = iota((ME, MZ), 0)

    def raised(plane, dy):
        at = [total[0:1, 3 * (dy + 1) + dx : 3 * (dy + 1) + dx + 1] for dx in range(3)]
        return plane + jnp.where(row < MH, at[0], jnp.where(row < MH + MX, at[1], at[2]))

    own = raised(v[...], 0)
    beside = raised(below[...], -1) + raised(above[...], 1)
    rho, cx, cy, cz = middle_parts(r_mid, cx_mid, cyz_mid)
    applied = operate(own, near_x(own), beside, rho, cx, cy, cz)
    out[...] = own + solve_z((f_mid[...] - applied) / diagonal(rho, cx, cy, cz), lines)


def to_fine(px, py, v, below, above, far_below, far_above, u_ext, f_ext, r_ext, cx_ext, cy_ext, cz, lines, out, slabs):
    rows = [raise_rows(p[...]) for p in (far_below, below, v, above, far_above)]
    columns = raise_columns(jnp.concatenate(rows, axis=0)) * 0.25
    raised = [columns[FE * i : FE * (i + 1)] for i in range(5)]
    inside = inside_fine(px)
    us = []
    for j in range(6):
        at = 1 + j // 2
        other = at - 1 if j % 2 == 0 else at + 1
        held = inside
        if j < 2:
            held = inside & (py > 0)
        if j > 3:
            held = inside & (py < N_PY - 1)
        us.append(u_ext[j] + jnp.where(held, 3.0 * raised[at] + raised[other], 0.0))
    cx_col = cx_ext[:, 0:1]
    cz_row = cz[...]
    parts = []
    for j in range(4):
        own = us[j + 1]
        cy = cy_ext[j : j + 1]
        applied = operate(own, near_x(own), us[j] + us[j + 2], r_ext[j], cx_col, cy, cz_row)
        parts.append((f_ext[j] - applied) / diagonal(r_ext[j], cx_col, cy, cz_row))
    solved = solve_z(jnp.concatenate(parts, axis=0), lines)
    news = [us[j + 1] + solved[FE * j : FE * (j + 1)] for j in range(4)]
    inner = slice(FH, FH + FX)
    for at in range(2):
        full = news[at + 1]
        own = full[inner]
        out[at] = own
        beside_y = news[at][inner] + news[at + 2][inner]
        rho = r_ext[at + 1, inner]
        cy = cy_ext[at + 1 : at + 2]
        applied = operate(own, near_x(full)[inner], beside_y, rho, cx_col[inner], cy, cz_row)
        to_slabs((f_ext[at + 1, inner] - applied) / diagonal(rho, cx_col[inner], cy, cz_row), slabs, at)


def finish(px, py, u, slabs, out):
    for at in range(2):
        out[:, at, :] = u[at] + from_slabs(slabs, at)


class Device:
    def run(self, stage, shapes, *args, keep=()):
        used = len(args)
        args = args + tuple(keep)

        def kernel(*refs):
            refs = refs[:used] + refs[len(args) :]
            stage(lax.axis_index("px"), lax.axis_index("py"), *refs)

        whole = pl.BlockSpec(memory_space=pltpu.VMEM)
        outs = pl.pallas_call(
            kernel,
            out_shape=[jax.ShapeDtypeStruct(s, f32) for s in shapes],
            in_specs=[whole] * len(args),
            out_specs=[whole] * len(shapes),
            compiler_params=pltpu.CompilerParams(vmem_limit_bytes=24 * 1024 * 1024),
        )(*args)
        return outs if len(shapes) > 1 else outs[0]

    def local(self, fn, *args):
        return fn(*args)

    def block_of(self, lines):
        at = lax.axis_index("px") // 8
        return lax.dynamic_slice_in_dim(lines, at, 1, axis=0)

    def beside(self, axis, low, high, step=1):
        n = lax.axis_size(axis)
        up = [(i, i + step) for i in range(n - step)]
        down = [(j, i) for i, j in up]
        return lax.ppermute(high, axis, up), lax.ppermute(low, axis, down)

    def across(self, array):
        return lax.ppermute(array, "px", [(15, 16), (16, 15)])

    def everyone(self, rows):
        sent = rows.reshape(N_PX * N_PY, 1, 128)
        got = lax.all_to_all(sent, ("py", "px"), 0, 0, tiled=True)
        return got.reshape(N_PX * N_PY, 128)

    def solve_x(self, every, rows):
        fours = [list(range(k, k + 4)) for k in range(0, N_PX, 4)]
        eights = [list(range(k, N_PX, 4)) for k in range(4)]
        every = lax.all_to_all(every, "px", 0, 0, axis_index_groups=fours, tiled=True)
        parts = self.run(spread_x, [(8, ME, MZ)], every.reshape(4 * MX, MZ), rows)
        return lax.all_to_all(parts, "px", 0, 0, axis_index_groups=eights, tiled=True)

    def swap(self, axis, array, group):
        n = lax.axis_size(axis)
        groups = None
        if group < n:
            groups = [list(range(k, k + group)) for k in range(0, n, group)]
        return lax.all_to_all(array, axis, 0, 0, axis_index_groups=groups, tiled=True)


def cycle(d, forcing, inv_density, stretch_x, stretch_y, stretch_z, lines_z0, lines_x0, lines_z1, lines_x1, column):
    sx = d.local(lambda a: a.reshape(1, FX), stretch_x)
    sy = d.local(lambda a: a.reshape(1, 2), stretch_y)
    cz = d.local(lambda a: a.reshape(1, FZ), stretch_z)
    rows_x1 = d.local(lambda a: a.reshape(MX * N_PX, 256), lines_x1)
    slab, own, mid = (8, 2, FX, 128), (2, FX, FZ), (ME, MZ)

    force, rho, lower, upper, low, high, cx = d.run(
        start,
        [own, own, (72, FZ), (72, FZ), (24, FZ), (24, FZ), (FX, 128)],
        forcing, inv_density, sx, sy,
    )
    y_below, y_above = d.beside("py", lower, upper)
    x_left, x_right = d.beside("px", low, high)
    block = d.block_of(lines_x0)
    rows_x = d.run(rows_for_x, [(8 * ME, 64)], rows_x1)
    u = d.run(own_lines, [own], force, rho, cx, sy, cz, lines_z0)
    slabs = d.run(
        first_half, [slab],
        force, rho, cx, sy, cz, u, y_below, y_above, x_left, x_right, lines_z0,
    )
    slabs = d.swap("px", slabs, 8)
    cx_mid, cyz_mid, told = d.run(
        middle_statics,
        [(ME, 128), (8, MZ), (16, FZ)],
        rho, cx, sy, cz, x_left, x_right, column,
    )
    slabs = d.run(solve_x_fine, [slab], slabs, block)
    slabs = d.swap("px", slabs, 8)
    u = d.run(add_slabs, [(80, FZ)], u, slabs, told)
    below, above = d.beside("py", u, u)
    q, low, high = d.run(
        half_residual, [(FX, FZ), (24, FZ), (24, FZ)],
        u, below, above, force, rho, y_below, y_above, cx, sy, cz,
    )
    left, right = d.beside("px", low, high)
    u_ext, f_ext, r_ext, cx_ext, cy_ext, r_mid, f_mid, v, told = d.run(
        to_middle,
        [(6, FE, FZ), (4, FE, FZ), (4, FE, FZ), (FE, 128), (8, FZ), mid, mid, mid, (48, FZ)],
        q, u, below, above, left, right, force, rho, y_below, y_above, x_left, x_right,
        cx, sy, cx_mid, cyz_mid, lines_z1,
    )
    statics = (f_mid, r_mid, cx_mid, cyz_mid)
    keep = statics + (u_ext, f_ext, r_ext, cx_ext, cy_ext, cz)

    below, above = d.beside("py", v, v)
    every = d.run(middle_scaled, [(16, MX, MZ)], v, below, above, *statics, keep=keep)
    every = d.swap("px", every, 16)
    every = d.local(lambda a: a.reshape(256, MZ), every)
    v = d.run(solve_x_block, [mid], every, rows_x1, v, keep=keep)
    other = d.across(v)
    sent = d.run(block_mean, [(N_PX * N_PY, 128)], v, *statics, told, column, keep=keep)
    parts = d.everyone(sent)
    v = d.run(mend, [mid], v, other, keep=keep)
    below, above = d.beside("py", v, v)
    v = d.run(second_half, [mid], parts, v, below, above, *statics, lines_z1, keep=keep)
    below, above = d.beside("py", v, v)
    parts = d.solve_x(d.run(middle_scaled, [(4, MX, MZ)], v, below, above, *statics, keep=keep), rows_x)
    v = d.run(gain_x, [mid], v, parts, keep=keep)

    below, above = d.beside("py", v, v)
    far_below, far_above = d.beside("py", v, v, 2)
    u, slabs = d.run(
        to_fine,
        [own, slab],
        v, below, above, far_below, far_above, u_ext, f_ext, r_ext, cx_ext, cy_ext, cz, lines_z0,
    )
    slabs = d.swap("px", slabs, 8)
    slabs = d.run(solve_x_fine, [slab], slabs, block)
    slabs = d.swap("px", slabs, 8)
    return d.run(finish, [(FX, 2, FZ)], u, slabs)


def solution(mesh):
    placed = (
        P("px", "py", None),
        P("px", "py", None),
        P("px"),
        P("py"),
        P(),
        P(),
        P(),
        P(),
        P(),
        P(("py", "px"), None),
    )

    def step(*args):
        return cycle(Device(), *args)

    return jax.shard_map(
        step, mesh=mesh, in_specs=placed, out_specs=P("px", "py", None), check_vma=False
    )
```

```python
import jax
import jax.numpy as jnp
from jax import lax
from jax.experimental import pallas as pl
from jax.experimental.pallas import tpu as pltpu
from jax.sharding import PartitionSpec as P


shift_term = 0.1
f32 = jnp.float32
bf16 = jnp.bfloat16

N_PY, N_PX = 16, 32
FX, FZ = 32, 1024
MX, MZ = 16, 512
FH, MH = 8, 4
FE, ME = FX + 2 * FH, MX + 2 * MH


def roll(v, shift, axis):
    return pltpu.roll(v, shift % v.shape[axis], axis)


def dyn(ref, start, size):
    return ref[pl.ds(pl.multiple_of(start, 8), size), :]


def halves(a):
    high = a.astype(bf16)
    return high, (a - high.astype(f32)).astype(bf16)


def thirds(a):
    high, rest = a.astype(bf16), None
    rest = a - high.astype(f32)
    middle = rest.astype(bf16)
    return high, middle, (rest - middle.astype(f32)).astype(bf16)


def product(a, b, dims):
    return lax.dot_general(a, b, (dims, ((), ())), preferred_element_type=f32)


def dot(a, b, dims=((1,), (0,))):
    a_high, a_low = halves(a)
    b_high, b_low = halves(b)
    return product(a_high, b_high, dims) + (product(a_high, b_low, dims) + product(a_low, b_high, dims))


def pick_right(a, weight):
    dims = ((1,), (0,))
    w = weight.astype(bf16)
    high, middle, low = thirds(a)
    return product(high, w, dims) + (product(middle, w, dims) + product(low, w, dims))


def pick_left(weight, a):
    dims = ((1,), (0,))
    w = weight.astype(bf16)
    high, middle, low = thirds(a)
    return product(w, high, dims) + (product(w, middle, dims) + product(w, low, dims))


def iota(shape, axis):
    return lax.broadcasted_iota(jnp.int32, shape, axis)


def rows_of(rows):
    at = iota((8, rows[0].shape[1]), 0)
    total = jnp.zeros((8, rows[0].shape[1]), f32)
    for i, row in enumerate(rows):
        total = jnp.where(at == i, row, total)
    return total


def rows_at(pairs):
    at = iota((8, pairs[0][1].shape[1]), 0)
    total = jnp.zeros((8, pairs[0][1].shape[1]), f32)
    for i, row in pairs:
        total = jnp.where(at == i, row, total)
    return total


def near_z(v):
    lane = iota(v.shape, 1)
    last = v.shape[1] - 1
    below = jnp.where(lane == 0, 0.0, roll(v, 1, 1))
    above = jnp.where(lane == last, 0.0, roll(v, -1, 1))
    return below + above


def near_x(v):
    return roll(v, 1, 0) + roll(v, -1, 0)


def operate(v, v_near_x, v_near_y, rho, cx, cy, cz):
    twice = 2.0 * v
    stencil = cx * (twice - v_near_x) + cy * (twice - v_near_y) + cz * (twice - near_z(v))
    return shift_term * v + rho * stencil


def diagonal(rho, cx, cy, cz):
    return shift_term + 2.0 * rho * (cx + cy + cz)


def solve_z(w, lines):
    count, size = lines.shape[0], lines.shape[1]
    parts = []
    for k in range(count):
        parts.append(dot(w[:, k * size : (k + 1) * size], lines[k], ((1,), (1,))))
    return jnp.concatenate(parts, axis=1)


def columns_by(v, pick):
    cuts = [slice(256 * k, 256 * (k + 1)) for k in range(v.shape[1] // 256)]
    return jnp.concatenate([pick_right(v[:, cut], pick) for cut in cuts], axis=1)


def pair_columns(v, scale):
    fine, coarse = iota((256, 128), 0), iota((256, 128), 1)
    return columns_by(v, jnp.where(fine // 2 == coarse, scale, 0.0))


def even_columns(v, scale):
    fine, coarse = iota((256, 128), 0), iota((256, 128), 1)
    return columns_by(v, jnp.where(fine == 2 * coarse, scale, 0.0))


def restrict_columns(v):
    lane = iota(v.shape, 1)
    last = v.shape[1] - 1
    one = jnp.where(lane == last, 0.0, roll(v, -1, 1))
    two = jnp.where(lane >= last - 1, 0.0, roll(v, -2, 1))
    below = jnp.where(lane == 0, 0.0, roll(v, 1, 1))
    return even_columns(below + 3.0 * v + 3.0 * one + two, 0.125)


def raise_columns(v):
    lane = iota(v.shape, 1)
    last = v.shape[1] - 1
    below = jnp.where(lane == 0, 0.0, roll(v, 1, 1))
    above = jnp.where(lane == last, 0.0, roll(v, -1, 1))
    even = 3.0 * v + below
    odd = 3.0 * v + above
    coarse, fine = iota((128, 256), 0), iota((128, 256), 1)
    at_even = jnp.where(fine == 2 * coarse, 0.25, 0.0)
    at_odd = jnp.where(fine == 2 * coarse + 1, 0.25, 0.0)
    parts = []
    for k in range(v.shape[1] // 128):
        cut = slice(128 * k, 128 * (k + 1))
        parts.append(pick_right(even[:, cut], at_even) + pick_right(odd[:, cut], at_odd))
    return jnp.concatenate(parts, axis=1)


def restrict_rows(v):
    coarse, fine = iota((ME, FE), 0), iota((ME, FE), 1)
    away = fine - 2 * coarse
    weight = jnp.where((away == 0) | (away == 1), 0.375, 0.0)
    weight = weight + jnp.where((away == -1) | (away == 2), 0.125, 0.0)
    return pick_left(weight, v)


def pair_rows(v):
    coarse, fine = iota((ME, FE), 0), iota((ME, FE), 1)
    return pick_left(jnp.where(fine // 2 == coarse, 1.0, 0.0), v)


def raise_rows(v):
    fine, coarse = iota((FE, ME), 0), iota((FE, ME), 1)
    away = fine - 2 * coarse
    weight = jnp.where((away == 0) | (away == 1), 0.75, 0.0)
    weight = weight + jnp.where((away == 2) | (away == -1), 0.25, 0.0)
    return pick_left(weight, v)


def inside_middle(px):
    row = iota((ME, MZ), 0) + MX * px - MH
    return (row >= 0) & (row < MX * N_PX)


def inside_fine(px):
    row = iota((FE, FZ), 0) + FX * px - FH
    return (row >= 0) & (row < FX * N_PX)


def to_slabs(plane, out, at):
    for m in range(8):
        out[m, at] = plane[:, 128 * m : 128 * (m + 1)]


def from_slabs(ref, at):
    return jnp.concatenate([ref[m, at] for m in range(8)], axis=1)


def start(px, py, forcing, inv_density, sx, sy, force, rho, lower, upper, low, high, cx):
    square = iota((FX, FX), 0) == iota((FX, FX), 1)
    column = jnp.sum(jnp.where(square, sx[...], 0.0), axis=1, keepdims=True)
    cx[...] = jnp.broadcast_to(column, (FX, 128))
    wide = jnp.broadcast_to(column, (FX, FZ))
    edges = {}
    for at, out in ((0, lower), (1, upper)):
        f_plane, r_plane = forcing[:, at, :], inv_density[:, at, :]
        force[at] = f_plane
        rho[at] = r_plane
        out[0:32] = f_plane
        out[32:64] = r_plane
        out[64:72] = jnp.broadcast_to(sy[0:1, at : at + 1], (8, FZ))
        for row in (0, FX - 1):
            edges[at, row] = (f_plane[row : row + 1], r_plane[row : row + 1])
    for side, row, cut in ((low, 0, slice(0, 8)), (high, FX - 1, slice(24, 32))):
        for k in range(2):
            side[8 * k : 8 * k + 8] = rows_of([edges[0, row][k], edges[1, row][k]])
        side[16:24] = wide[cut]


def own_lines(px, py, force, rho, cx, sy, cz, lines, u):
    parts = []
    for at in range(2):
        parts.append(force[at] / diagonal(rho[at], cx[:, 0:1], sy[0:1, at : at + 1], cz[...]))
    solved = solve_z(jnp.concatenate(parts, axis=0), lines)
    u[0] = solved[0:FX]
    u[1] = solved[FX : 2 * FX]


def first_half(px, py, force, rho, cx, sy, cz, u, below, above, left, right, lines, slabs):
    cx_col = cx[:, 0:1]
    cz_row = cz[...]
    parts = []
    for side in (below, above):
        parts.append(side[0:32] / diagonal(side[32:64], cx_col, side[64:65], cz_row))
    cy_edge = jnp.where(iota((8, 1), 0) == 0, sy[0:1, 0:1], sy[0:1, 1:2])
    for side, row in ((left, 23), (right, 16)):
        parts.append(side[0:8] / diagonal(side[8:16], side[row : row + 1, 0:1], cy_edge, cz_row))
    solved = solve_z(jnp.concatenate(parts, axis=0), lines)
    planes = [solved[0:32], u[0], u[1], solved[32:64]]
    for at in range(2):
        own = u[at]
        before = rows_at([(7, solved[64 + at : 65 + at])])
        after = rows_at([(0, solved[72 + at : 73 + at])])
        beside_x = near_x(jnp.concatenate([before, own, after], axis=0))[FH : FH + FX]
        beside_y = planes[at] + planes[at + 2]
        cy = sy[0:1, at : at + 1]
        applied = operate(own, beside_x, beside_y, rho[at], cx_col, cy, cz_row)
        to_slabs((force[at] - applied) / diagonal(rho[at], cx_col, cy, cz_row), slabs, at)


def middle_statics(px, py, rho, cx, sy, cz, left, right, column, cx_mid, cyz_mid, told):
    coarse, fine = iota((MX, FX), 0), iota((MX, FX), 1)
    pairs = pick_left(jnp.where(fine // 2 == coarse, 1.0, 0.0), rho[0] + rho[1])
    own = pair_columns(pairs, 0.125)
    columns = jnp.concatenate([left[16:24, 0:128], cx[...], right[16:24, 0:128]], axis=0)
    cym = jnp.broadcast_to((sy[0:1, 0:1] + sy[0:1, 1:2]) * 0.125, (8, MZ))
    czm = pair_columns(jnp.broadcast_to(cz[...], (16, FZ)), 0.125)
    cx_mid[...] = pair_rows(columns) * 0.125
    cyz_mid[...] = jnp.concatenate([czm[0:1], cym[0:7]], axis=0)
    told[0:8, 0:MZ] = own[0:8]
    told[0:8, MZ:FZ] = own[8:16]
    told[8:16, 0:MZ] = jnp.broadcast_to(column[...], (8, MZ))
    told[8:16, MZ:FZ] = cym


def solve_x_fine(px, py, slabs, lines, out):
    block = lines[0]
    for at in range(2):
        column = jnp.concatenate([slabs[m, at] for m in range(8)], axis=0)
        solved = dot(block, column)
        for m in range(8):
            out[m, at] = solved[32 * m : 32 * (m + 1)]


def add_slabs(px, py, u, slabs, told, out):
    for at in range(2):
        out[FX * at : FX * (at + 1)] = u[at] + from_slabs(slabs, at)
    out[64:80] = told[...]


def half_residual(px, py, u, below, above, force, rho, y_below, y_above, cx, sy, cz, q, low, high):
    cx_col = cx[...][:, 0:1]
    cz_row = cz[...]
    us = [below[0:32], below[32:64], u[0:32], u[32:64], above[0:32], above[32:64]]
    fs = [y_below[0:32], force[0], force[1], y_above[0:32]]
    rs = [y_below[32:64], rho[0], rho[1], y_above[32:64]]
    cys = [y_below[64:65], sy[0:1, 0:1], sy[0:1, 1:2], y_above[64:65]]
    row = iota((FX, FZ), 0)
    total = None
    for j in range(4):
        own = us[j + 1]
        beside_x = jnp.where(row == 0, 0.0, roll(own, 1, 0)) + jnp.where(row == FX - 1, 0.0, roll(own, -1, 0))
        left_over = fs[j] - operate(own, beside_x, us[j] + us[j + 2], rs[j], cx_col, cys[j], cz_row)
        if j in (1, 2):
            left_over = 3.0 * left_over
        total = left_over if total is None else total + left_over
    total = total * 0.125
    q[...] = total
    for out, edge, step, cut in ((low, 0, 1, slice(0, 8)), (high, FX - 1, -1, slice(24, 32))):
        out[0:8] = total[cut]
        next_row = edge + step
        picked = [us[j + 1][edge : edge + 1] for j in range(4)]
        out[8:16] = rows_of(picked + [us[j + 1][next_row : next_row + 1] for j in range(4)])
        middle = u[64:68, 0:MZ] if edge == 0 else u[68:72, MZ:FZ]
        pairs = [jnp.concatenate([middle[2 * i : 2 * i + 1], middle[2 * i + 1 : 2 * i + 2]], axis=1) for i in range(2)]
        coarse = jnp.concatenate([u[72:73, 0:MZ], u[72:73, 0:MZ]], axis=1)
        out[16:24] = rows_of([rs[j][edge : edge + 1] for j in range(4)] + pairs + [coarse])


def to_middle(px, py, q, u, below, above, left, right, force, rho, y_below, y_above, x_left, x_right, cx, sy, cx_mid, cyz_mid, lines, u_ext, f_ext, r_ext, cx_ext, cy_ext, r_mid, f_mid, v_out, told):
    columns = jnp.concatenate([x_left[16:24, 0:128], cx[...], x_right[16:24, 0:128]], axis=0)
    cx_ext[...] = columns
    told[0:16] = below[64:80]
    told[16:32] = above[64:80]
    told[32:40] = jnp.broadcast_to(right[22:23], (8, FZ))
    told[40:48] = jnp.broadcast_to(left[22:23], (8, FZ))
    us = [below[32:64], u[0:32], u[32:64], above[0:32]]
    rs = [y_below[32:64], rho[0], rho[1], y_above[32:64]]
    cross = []
    for side, row in ((left, 0), (right, FX - 1)):
        inward = outward = None
        for j in range(4):
            weight = 0.375 if j in (1, 2) else 0.125
            here = weight * rs[j][row : row + 1] * side[8 + j : 9 + j]
            there = weight * side[16 + j : 17 + j] * us[j][row : row + 1]
            inward = here if inward is None else inward + here
            outward = there if outward is None else outward + there
        at = FH + row
        beyond = at - 1 if row == 0 else at + 1
        cross.append((at, inward * columns[at : at + 1, 0:1]))
        cross.append((beyond, outward * columns[beyond : beyond + 1, 0:1]))
    total = jnp.concatenate([left[0:8], q[...], right[0:8]], axis=0)
    line = iota((FE, FZ), 0)
    for at, term in cross:
        total = total + jnp.where(line == at, term, 0.0)
    none = jnp.zeros((8, FZ), f32)
    u_ext[0] = jnp.concatenate([none, below[0:32], none], axis=0)
    u_ext[5] = jnp.concatenate([none, above[32:64], none], axis=0)
    for j in range(4):
        before = rows_at([(7, left[8 + j : 9 + j]), (6, left[12 + j : 13 + j])])
        after = rows_at([(0, right[8 + j : 9 + j]), (1, right[12 + j : 13 + j])])
        u_ext[j + 1] = jnp.concatenate([before, us[j], after], axis=0)
    for at in range(2):
        for k, own, out in ((0, force, f_ext), (8, rho, r_ext)):
            before = rows_at([(7, x_left[k + at : k + at + 1])])
            after = rows_at([(0, x_right[k + at : k + at + 1])])
            out[at + 1] = jnp.concatenate([before, own[at], after], axis=0)
    for side, at in ((y_below, 0), (y_above, 3)):
        f_ext[at] = jnp.concatenate([none, side[0:32], none], axis=0)
        r_ext[at] = jnp.concatenate([none, side[32:64], none], axis=0)
    cy_rows = [jnp.broadcast_to(sy[0:1, at : at + 1], (1, FZ)) for at in range(2)]
    cy_ext[...] = rows_of([y_below[64:65], cy_rows[0], cy_rows[1], y_above[64:65]])
    dense = []
    for side, first in ((left, 4), (right, 0)):
        rows = []
        for i in range(2):
            line = side[20 + i : 21 + i]
            rows.append((first + 2 * i, line[:, 0:MZ]))
            rows.append((first + 2 * i + 1, line[:, MZ:FZ]))
        dense.append(rows_at(rows))
    dense[1:1] = [u[64:72, 0:MZ], u[64:72, MZ:FZ]]
    r_mid[...] = roll(jnp.concatenate(dense, axis=0), MH - 8, 0)[0:ME]
    rhs = restrict_columns(restrict_rows(total))
    rhs = jnp.where(inside_middle(px), rhs, 0.0)
    f_mid[...] = rhs
    diag = diagonal(*middle_parts(r_mid, cx_mid, cyz_mid))
    v_out[...] = solve_z(rhs / diag, lines)


def middle_parts(r_mid, cx_mid, cyz_mid):
    return r_mid[...], cx_mid[:, 0:1], cyz_mid[1:2], cyz_mid[0:1]


def middle_scaled(px, py, v, below, above, f_mid, r_mid, cx_mid, cyz_mid, out):
    rho, cx, cy, cz = middle_parts(r_mid, cx_mid, cyz_mid)
    own = v[...]
    applied = operate(own, near_x(own), below[...] + above[...], rho, cx, cy, cz)
    scaled = (f_mid[...] - applied) / diagonal(rho, cx, cy, cz)
    part = roll(scaled, -MH, 0)[0:MX]
    for i in range(out.shape[0]):
        out[i] = part


def rows_for_x(px, py, lines, out):
    place, row_of_four = px % 4, px // 4
    total = MX * N_PX
    parts = []
    for i in range(8):
        base = MX * (4 * i + place)
        pieces = [
            dyn(lines, jnp.maximum(base - 8, 0), 8),
            dyn(lines, base, MX),
            dyn(lines, jnp.minimum(base + MX, total - 8), 8),
        ]
        rows = roll(jnp.concatenate(pieces, axis=0), MH - 8, 0)[0:ME]
        at = iota((ME, 256), 0) + base - MH
        first = 256 * (row_of_four // 4)
        parts.append(jnp.where((at >= first) & (at < first + 256), rows, 0.0))
    full = jnp.concatenate(parts, axis=0)
    held = None
    for i in range(4):
        cut = jnp.where(row_of_four % 4 == i, full[:, 64 * i : 64 * (i + 1)], 0.0)
        held = cut if held is None else held + cut
    out[...] = held


def spread_x(px, py, gathered, rows, out):
    solved = dot(rows[...], gathered[...])
    for i in range(8):
        out[i] = solved[ME * i : ME * (i + 1)]


def gain_x(px, py, v, parts, out):
    total = v[...]
    for i in range(8):
        total = total + parts[i]
    out[...] = total


def solve_x_block(px, py, gathered, lines, v, out):
    total = MX * N_PX
    pieces = []
    starts = (
        (jnp.maximum(MX * px - 8, 0), 8),
        (MX * px, MX),
        (jnp.minimum(MX * px + MX, total - 8), 8),
    )
    for start, size in starts:
        pieces.append(dyn(lines, start, size))
    full = dot(jnp.concatenate(pieces, axis=0), gathered[...])
    part = roll(full, MH - 8, 0)[0:ME]
    row = iota((ME, MZ), 0) + MX * px - MH
    first = 256 * (px // 16)
    held = (row >= first) & (row < first + 256)
    out[...] = jnp.where(held, v[...] + part, 0.0)


def mend(px, py, v, other, out):
    row = iota((ME, MZ), 0)
    theirs = other[...]
    up = jnp.where((row >= MH + MX) & (px == 15), roll(theirs, MX, 0), 0.0)
    down = jnp.where((row < MH) & (px == 16), roll(theirs, -MX, 0), 0.0)
    out[...] = v[...] + (up + down)


def block_mean(px, py, v, f_mid, r_mid, cx_mid, cyz_mid, told, column, out):
    rho, cx, cy, cz = middle_parts(r_mid, cx_mid, cyz_mid)
    own = v[...]
    applied = operate(own, near_x(own), 0.0, rho, cx, cy, cz)
    row = iota((ME, MZ), 0)
    kept = jnp.where((row >= MH) & (row < MH + MX), f_mid[...] - applied, 0.0)

    def mean(a):
        return jnp.sum(jnp.sum(a, axis=0, keepdims=True), axis=1, keepdims=True) * (1.0 / (MX * MZ))

    sent = column[...] * mean(kept)
    inner = roll(own, -MH, 0)[0:MX]
    for at in (0, 16):
        share = mean(told[at : at + 8, 0:MZ] * inner[0:8] + told[at : at + 8, MZ:FZ] * inner[8:16])
        sent = sent + told[at + 8 : at + 9, 0:MZ] * (share * told[at + 8 : at + 9, MZ : MZ + 1])
    for at, edge, inner_row, mine in ((32, MH + MX, MH + MX - 1, px == 15), (40, MH - 1, MH, px == 16)):
        line = r_mid[edge : edge + 1] * cx_mid[edge : edge + 1, 0:1] * v[inner_row : inner_row + 1]
        sent = sent + told[at : at + 1, 0:MZ] * jnp.where(mine, mean(line), 0.0)
    lane = iota((8, MZ), 1)
    at_x, at_y = lane % N_PX, lane // N_PX
    wide = jnp.broadcast_to(sent, (8, MZ))
    rows = []
    for dy in (-1, 0, 1):
        for dx in (-1, 0, 1):
            held = (at_x + dx >= 0) & (at_x + dx < N_PX) & (at_y + dy >= 0) & (at_y + dy < N_PY)
            rows.append(jnp.where(held, roll(wide, -(dy * N_PX + dx), 1), 0.0)[0:1])
    stacked = jnp.concatenate([rows_of(rows[0:8]), rows_of(rows[8:9])], axis=0)
    unit = jnp.where(iota((16, 128), 0) == iota((16, 128), 1), 1.0, 0.0).astype(bf16)
    high, middle, low = thirds(stacked)
    dims = ((0,), (0,))
    out[...] = product(high, unit, dims) + (product(middle, unit, dims) + product(low, unit, dims))


def second_half(px, py, parts, v, below, above, f_mid, r_mid, cx_mid, cyz_mid, lines, out):
    total = jnp.sum(parts[...], axis=0, keepdims=True)
    row = iota((ME, MZ), 0)

    def raised(plane, dy):
        at = [total[0:1, 3 * (dy + 1) + dx : 3 * (dy + 1) + dx + 1] for dx in range(3)]
        return plane + jnp.where(row < MH, at[0], jnp.where(row < MH + MX, at[1], at[2]))

    own = raised(v[...], 0)
    beside = raised(below[...], -1) + raised(above[...], 1)
    rho, cx, cy, cz = middle_parts(r_mid, cx_mid, cyz_mid)
    applied = operate(own, near_x(own), beside, rho, cx, cy, cz)
    out[...] = own + solve_z((f_mid[...] - applied) / diagonal(rho, cx, cy, cz), lines)


def to_fine(px, py, v, below, above, far_below, far_above, u_ext, f_ext, r_ext, cx_ext, cy_ext, cz, lines, out, slabs):
    rows = [raise_rows(p[...]) for p in (far_below, below, v, above, far_above)]
    columns = raise_columns(jnp.concatenate(rows, axis=0)) * 0.25
    raised = [columns[FE * i : FE * (i + 1)] for i in range(5)]
    inside = inside_fine(px)
    us = []
    for j in range(6):
        at = 1 + j // 2
        other = at - 1 if j % 2 == 0 else at + 1
        held = inside
        if j < 2:
            held = inside & (py > 0)
        if j > 3:
            held = inside & (py < N_PY - 1)
        us.append(u_ext[j] + jnp.where(held, 3.0 * raised[at] + raised[other], 0.0))
    cx_col = cx_ext[:, 0:1]
    cz_row = cz[...]
    parts = []
    for j in range(4):
        own = us[j + 1]
        cy = cy_ext[j : j + 1]
        applied = operate(own, near_x(own), us[j] + us[j + 2], r_ext[j], cx_col, cy, cz_row)
        parts.append((f_ext[j] - applied) / diagonal(r_ext[j], cx_col, cy, cz_row))
    solved = solve_z(jnp.concatenate(parts, axis=0), lines)
    news = [us[j + 1] + solved[FE * j : FE * (j + 1)] for j in range(4)]
    inner = slice(FH, FH + FX)
    for at in range(2):
        full = news[at + 1]
        own = full[inner]
        out[at] = own
        beside_y = news[at][inner] + news[at + 2][inner]
        rho = r_ext[at + 1, inner]
        cy = cy_ext[at + 1 : at + 2]
        applied = operate(own, near_x(full)[inner], beside_y, rho, cx_col[inner], cy, cz_row)
        to_slabs((f_ext[at + 1, inner] - applied) / diagonal(rho, cx_col[inner], cy, cz_row), slabs, at)


def finish(px, py, u, slabs, out):
    for at in range(2):
        out[:, at, :] = u[at] + from_slabs(slabs, at)


class Device:
    def run(self, stage, shapes, *args, grant=24):
        def kernel(*refs):
            stage(lax.axis_index("px"), lax.axis_index("py"), *refs)

        whole = pl.BlockSpec(memory_space=pltpu.VMEM)
        outs = pl.pallas_call(
            kernel,
            out_shape=[jax.ShapeDtypeStruct(s, f32) for s in shapes],
            in_specs=[whole] * len(args),
            out_specs=[whole] * len(shapes),
            compiler_params=pltpu.CompilerParams(vmem_limit_bytes=grant * 1024 * 1024),
        )(*args)
        return outs if len(shapes) > 1 else outs[0]

    def local(self, fn, *args):
        return fn(*args)

    def block_of(self, lines):
        at = lax.axis_index("px") // 8
        return lax.dynamic_slice_in_dim(lines, at, 1, axis=0)

    def beside(self, axis, low, high, step=1):
        n = lax.axis_size(axis)
        up = [(i, i + step) for i in range(n - step)]
        down = [(j, i) for i, j in up]
        return lax.ppermute(high, axis, up), lax.ppermute(low, axis, down)

    def across(self, array):
        return lax.ppermute(array, "px", [(15, 16), (16, 15)])

    def everyone(self, rows):
        sent = rows.reshape(N_PX * N_PY, 1, 128)
        got = lax.all_to_all(sent, ("py", "px"), 0, 0, tiled=True)
        return got.reshape(N_PX * N_PY, 128)

    def solve_x(self, every, rows):
        fours = [list(range(k, k + 4)) for k in range(0, N_PX, 4)]
        eights = [list(range(k, N_PX, 4)) for k in range(4)]
        every = lax.all_to_all(every, "px", 0, 0, axis_index_groups=fours, tiled=True)
        parts = self.run(spread_x, [(8, ME, MZ)], every.reshape(4 * MX, MZ), rows)
        return lax.all_to_all(parts, "px", 0, 0, axis_index_groups=eights, tiled=True)

    def swap(self, axis, array, group):
        n = lax.axis_size(axis)
        groups = None
        if group < n:
            groups = [list(range(k, k + group)) for k in range(0, n, group)]
        return lax.all_to_all(array, axis, 0, 0, axis_index_groups=groups, tiled=True)


def cycle(d, forcing, inv_density, stretch_x, stretch_y, stretch_z, lines_z0, lines_x0, lines_z1, lines_x1, column):
    sx = d.local(lambda a: a.reshape(1, FX), stretch_x)
    sy = d.local(lambda a: a.reshape(1, 2), stretch_y)
    cz = d.local(lambda a: a.reshape(1, FZ), stretch_z)
    rows_x1 = d.local(lambda a: a.reshape(MX * N_PX, 256), lines_x1)
    slab, own, mid = (8, 2, FX, 128), (2, FX, FZ), (ME, MZ)

    force, rho, lower, upper, low, high, cx = d.run(
        start,
        [own, own, (72, FZ), (72, FZ), (24, FZ), (24, FZ), (FX, 128)],
        forcing, inv_density, sx, sy,
    )
    y_below, y_above = d.beside("py", lower, upper)
    x_left, x_right = d.beside("px", low, high)
    block = d.block_of(lines_x0)
    rows_x = d.run(rows_for_x, [(8 * ME, 64)], rows_x1)
    u = d.run(own_lines, [own], force, rho, cx, sy, cz, lines_z0)
    slabs = d.run(
        first_half, [slab],
        force, rho, cx, sy, cz, u, y_below, y_above, x_left, x_right, lines_z0,
    )
    slabs = d.swap("px", slabs, 8)
    cx_mid, cyz_mid, told = d.run(
        middle_statics,
        [(ME, 128), (8, MZ), (16, FZ)],
        rho, cx, sy, cz, x_left, x_right, column,
    )
    slabs = d.run(solve_x_fine, [slab], slabs, block)
    slabs = d.swap("px", slabs, 8)
    u = d.run(add_slabs, [(80, FZ)], u, slabs, told)
    below, above = d.beside("py", u, u)
    q, low, high = d.run(
        half_residual, [(FX, FZ), (24, FZ), (24, FZ)],
        u, below, above, force, rho, y_below, y_above, cx, sy, cz,
    )
    left, right = d.beside("px", low, high)
    u_ext, f_ext, r_ext, cx_ext, cy_ext, r_mid, f_mid, v, told = d.run(
        to_middle,
        [(6, FE, FZ), (4, FE, FZ), (4, FE, FZ), (FE, 128), (8, FZ), mid, mid, mid, (48, FZ)],
        q, u, below, above, left, right, force, rho, y_below, y_above, x_left, x_right,
        cx, sy, cx_mid, cyz_mid, lines_z1,
    )
    statics = (f_mid, r_mid, cx_mid, cyz_mid)

    below, above = d.beside("py", v, v)
    every = d.run(middle_scaled, [(16, MX, MZ)], v, below, above, *statics)
    every = d.swap("px", every, 16)
    every = d.local(lambda a: a.reshape(256, MZ), every)
    v = d.run(solve_x_block, [mid], every, rows_x1, v)
    other = d.across(v)
    sent = d.run(block_mean, [(N_PX * N_PY, 128)], v, *statics, told, column)
    parts = d.everyone(sent)
    v = d.run(mend, [mid], v, other)
    below, above = d.beside("py", v, v)
    v = d.run(second_half, [mid], parts, v, below, above, *statics, lines_z1)
    below, above = d.beside("py", v, v)
    parts = d.solve_x(d.run(middle_scaled, [(4, MX, MZ)], v, below, above, *statics), rows_x)
    v = d.run(gain_x, [mid], v, parts)

    below, above = d.beside("py", v, v)
    far_below, far_above = d.beside("py", v, v, 2)
    u, slabs = d.run(
        to_fine,
        [own, slab],
        v, below, above, far_below, far_above, u_ext, f_ext, r_ext, cx_ext, cy_ext, cz, lines_z0,
    )
    slabs = d.swap("px", slabs, 8)
    slabs = d.run(solve_x_fine, [slab], slabs, block)
    slabs = d.swap("px", slabs, 8)
    return d.run(finish, [(FX, 2, FZ)], u, slabs)


def solution(mesh):
    placed = (
        P("px", "py", None),
        P("px", "py", None),
        P("px"),
        P("py"),
        P(),
        P(),
        P(),
        P(),
        P(),
        P(("py", "px"), None),
    )

    def step(*args):
        return cycle(Device(), *args)

    return jax.shard_map(
        step, mesh=mesh, in_specs=placed, out_specs=P("px", "py", None), check_vma=False
    )
```

```python
import jax
import jax.numpy as jnp
from jax import lax
from jax.experimental import pallas as pl
from jax.experimental.pallas import tpu as pltpu
from jax.sharding import PartitionSpec as P


shift_term = 0.1
f32 = jnp.float32
bf16 = jnp.bfloat16

N_PY, N_PX = 16, 32
FX, FZ = 32, 1024
MX, MZ = 16, 512
FH, MH = 8, 4
FE, ME = FX + 2 * FH, MX + 2 * MH


def roll(v, shift, axis):
    return pltpu.roll(v, shift % v.shape[axis], axis)


def dyn(ref, start, size):
    return ref[pl.ds(pl.multiple_of(start, 8), size), :]


def halves(a):
    high = a.astype(bf16)
    return high, (a - high.astype(f32)).astype(bf16)


def thirds(a):
    high, rest = a.astype(bf16), None
    rest = a - high.astype(f32)
    middle = rest.astype(bf16)
    return high, middle, (rest - middle.astype(f32)).astype(bf16)


def product(a, b, dims):
    return lax.dot_general(a, b, (dims, ((), ())), preferred_element_type=f32)


def dot(a, b, dims=((1,), (0,))):
    a_high, a_low = halves(a)
    b_high, b_low = halves(b)
    return product(a_high, b_high, dims) + (product(a_high, b_low, dims) + product(a_low, b_high, dims))


def pick_right(a, weight):
    dims = ((1,), (0,))
    w = weight.astype(bf16)
    high, middle, low = thirds(a)
    return product(high, w, dims) + (product(middle, w, dims) + product(low, w, dims))


def pick_left(weight, a):
    dims = ((1,), (0,))
    w = weight.astype(bf16)
    high, middle, low = thirds(a)
    return product(w, high, dims) + (product(w, middle, dims) + product(w, low, dims))


def iota(shape, axis):
    return lax.broadcasted_iota(jnp.int32, shape, axis)


def rows_of(rows):
    at = iota((8, rows[0].shape[1]), 0)
    total = jnp.zeros((8, rows[0].shape[1]), f32)
    for i, row in enumerate(rows):
        total = jnp.where(at == i, row, total)
    return total


def rows_at(pairs):
    at = iota((8, pairs[0][1].shape[1]), 0)
    total = jnp.zeros((8, pairs[0][1].shape[1]), f32)
    for i, row in pairs:
        total = jnp.where(at == i, row, total)
    return total


def near_z(v):
    lane = iota(v.shape, 1)
    last = v.shape[1] - 1
    below = jnp.where(lane == 0, 0.0, roll(v, 1, 1))
    above = jnp.where(lane == last, 0.0, roll(v, -1, 1))
    return below + above


def near_x(v):
    return roll(v, 1, 0) + roll(v, -1, 0)


def operate(v, v_near_x, v_near_y, rho, cx, cy, cz):
    twice = 2.0 * v
    stencil = cx * (twice - v_near_x) + cy * (twice - v_near_y) + cz * (twice - near_z(v))
    return shift_term * v + rho * stencil


def diagonal(rho, cx, cy, cz):
    return shift_term + 2.0 * rho * (cx + cy + cz)


def solve_z(w, lines):
    count, size = lines.shape[0], lines.shape[1]
    parts = []
    for k in range(count):
        parts.append(dot(w[:, k * size : (k + 1) * size], lines[k], ((1,), (1,))))
    return jnp.concatenate(parts, axis=1)


def columns_by(v, pick):
    cuts = [slice(256 * k, 256 * (k + 1)) for k in range(v.shape[1] // 256)]
    return jnp.concatenate([pick_right(v[:, cut], pick) for cut in cuts], axis=1)


def pair_columns(v, scale):
    fine, coarse = iota((256, 128), 0), iota((256, 128), 1)
    return columns_by(v, jnp.where(fine // 2 == coarse, scale, 0.0))


def even_columns(v, scale):
    fine, coarse = iota((256, 128), 0), iota((256, 128), 1)
    return columns_by(v, jnp.where(fine == 2 * coarse, scale, 0.0))


def restrict_columns(v):
    lane = iota(v.shape, 1)
    last = v.shape[1] - 1
    one = jnp.where(lane == last, 0.0, roll(v, -1, 1))
    two = jnp.where(lane >= last - 1, 0.0, roll(v, -2, 1))
    below = jnp.where(lane == 0, 0.0, roll(v, 1, 1))
    return even_columns(below + 3.0 * v + 3.0 * one + two, 0.125)


def raise_columns(v):
    lane = iota(v.shape, 1)
    last = v.shape[1] - 1
    below = jnp.where(lane == 0, 0.0, roll(v, 1, 1))
    above = jnp.where(lane == last, 0.0, roll(v, -1, 1))
    even = 3.0 * v + below
    odd = 3.0 * v + above
    coarse, fine = iota((128, 256), 0), iota((128, 256), 1)
    at_even = jnp.where(fine == 2 * coarse, 0.25, 0.0)
    at_odd = jnp.where(fine == 2 * coarse + 1, 0.25, 0.0)
    parts = []
    for k in range(v.shape[1] // 128):
        cut = slice(128 * k, 128 * (k + 1))
        parts.append(pick_right(even[:, cut], at_even) + pick_right(odd[:, cut], at_odd))
    return jnp.concatenate(parts, axis=1)


def restrict_rows(v):
    coarse, fine = iota((ME, FE), 0), iota((ME, FE), 1)
    away = fine - 2 * coarse
    weight = jnp.where((away == 0) | (away == 1), 0.375, 0.0)
    weight = weight + jnp.where((away == -1) | (away == 2), 0.125, 0.0)
    return pick_left(weight, v)


def pair_rows(v):
    coarse, fine = iota((ME, FE), 0), iota((ME, FE), 1)
    return pick_left(jnp.where(fine // 2 == coarse, 1.0, 0.0), v)


def raise_rows(v):
    fine, coarse = iota((FE, ME), 0), iota((FE, ME), 1)
    away = fine - 2 * coarse
    weight = jnp.where((away == 0) | (away == 1), 0.75, 0.0)
    weight = weight + jnp.where((away == 2) | (away == -1), 0.25, 0.0)
    return pick_left(weight, v)


def inside_middle(px):
    row = iota((ME, MZ), 0) + MX * px - MH
    return (row >= 0) & (row < MX * N_PX)


def inside_fine(px):
    row = iota((FE, FZ), 0) + FX * px - FH
    return (row >= 0) & (row < FX * N_PX)


def to_slabs(plane, out, at):
    for m in range(8):
        out[m, at] = plane[:, 128 * m : 128 * (m + 1)]


def from_slabs(ref, at):
    return jnp.concatenate([ref[m, at] for m in range(8)], axis=1)


def start(px, py, forcing, inv_density, sxy, force, rho, lower, upper, low, high, cx):
    square = iota((FX, FX), 0) == iota((FX, FX), 1)
    column = jnp.sum(jnp.where(square, sxy[0:1, 0:FX], 0.0), axis=1, keepdims=True)
    cx[...] = jnp.broadcast_to(column, (FX, 128))
    wide = jnp.broadcast_to(column, (FX, FZ))
    edges = {}
    for at, out in ((0, lower), (1, upper)):
        f_plane, r_plane = forcing[:, at, :], inv_density[:, at, :]
        force[at] = f_plane
        rho[at] = r_plane
        out[0:32] = f_plane
        out[32:64] = r_plane
        out[64:72] = jnp.broadcast_to(sxy[0:1, FX + at : FX + at + 1], (8, FZ))
        for row in (0, FX - 1):
            edges[at, row] = (f_plane[row : row + 1], r_plane[row : row + 1])
    for side, row, cut in ((low, 0, slice(0, 8)), (high, FX - 1, slice(24, 32))):
        for k in range(2):
            side[8 * k : 8 * k + 8] = rows_of([edges[0, row][k], edges[1, row][k]])
        side[16:24] = wide[cut]


def own_lines(px, py, force, rho, cx, sy, cz, lines, u):
    parts = []
    for at in range(2):
        parts.append(force[at] / diagonal(rho[at], cx[:, 0:1], sy[0:1, at : at + 1], cz[...]))
    solved = solve_z(jnp.concatenate(parts, axis=0), lines)
    u[0] = solved[0:FX]
    u[1] = solved[FX : 2 * FX]


def first_half(px, py, force, rho, cx, sy, cz, u, below, above, left, right, lines, slabs):
    cx_col = cx[:, 0:1]
    cz_row = cz[...]
    parts = []
    for side in (below, above):
        parts.append(side[0:32] / diagonal(side[32:64], cx_col, side[64:65], cz_row))
    cy_edge = jnp.where(iota((8, 1), 0) == 0, sy[0:1, 0:1], sy[0:1, 1:2])
    for side, row in ((left, 23), (right, 16)):
        parts.append(side[0:8] / diagonal(side[8:16], side[row : row + 1, 0:1], cy_edge, cz_row))
    solved = solve_z(jnp.concatenate(parts, axis=0), lines)
    planes = [solved[0:32], u[0], u[1], solved[32:64]]
    for at in range(2):
        own = u[at]
        before = rows_at([(7, solved[64 + at : 65 + at])])
        after = rows_at([(0, solved[72 + at : 73 + at])])
        beside_x = near_x(jnp.concatenate([before, own, after], axis=0))[FH : FH + FX]
        beside_y = planes[at] + planes[at + 2]
        cy = sy[0:1, at : at + 1]
        applied = operate(own, beside_x, beside_y, rho[at], cx_col, cy, cz_row)
        to_slabs((force[at] - applied) / diagonal(rho[at], cx_col, cy, cz_row), slabs, at)


def middle_statics(px, py, rho, cx, sy, cz, left, right, column, cx_mid, cyz_mid, told):
    coarse, fine = iota((MX, FX), 0), iota((MX, FX), 1)
    pairs = pick_left(jnp.where(fine // 2 == coarse, 1.0, 0.0), rho[0] + rho[1])
    own = pair_columns(pairs, 0.125)
    columns = jnp.concatenate([left[16:24, 0:128], cx[...], right[16:24, 0:128]], axis=0)
    cym = jnp.broadcast_to((sy[0:1, 0:1] + sy[0:1, 1:2]) * 0.125, (8, MZ))
    czm = pair_columns(jnp.broadcast_to(cz[...], (16, FZ)), 0.125)
    cx_mid[...] = pair_rows(columns) * 0.125
    cyz_mid[...] = jnp.concatenate([czm[0:1], cym[0:7]], axis=0)
    told[0:8, 0:MZ] = own[0:8]
    told[0:8, MZ:FZ] = own[8:16]
    told[8:16, 0:MZ] = jnp.broadcast_to(column[...], (8, MZ))
    told[8:16, MZ:FZ] = cym


def solve_x_fine(px, py, slabs, lines, out):
    block = lines[0]
    for at in range(2):
        column = jnp.concatenate([slabs[m, at] for m in range(8)], axis=0)
        solved = dot(block, column)
        for m in range(8):
            out[m, at] = solved[32 * m : 32 * (m + 1)]


def add_slabs(px, py, u, slabs, told, out):
    for at in range(2):
        out[FX * at : FX * (at + 1)] = u[at] + from_slabs(slabs, at)
    out[64:80] = told[...]


def half_residual(px, py, u, below, above, force, rho, y_below, y_above, cx, sy, cz, q, low, high):
    cx_col = cx[...][:, 0:1]
    cz_row = cz[...]
    us = [below[0:32], below[32:64], u[0:32], u[32:64], above[0:32], above[32:64]]
    fs = [y_below[0:32], force[0], force[1], y_above[0:32]]
    rs = [y_below[32:64], rho[0], rho[1], y_above[32:64]]
    cys = [y_below[64:65], sy[0:1, 0:1], sy[0:1, 1:2], y_above[64:65]]
    row = iota((FX, FZ), 0)
    total = None
    for j in range(4):
        own = us[j + 1]
        beside_x = jnp.where(row == 0, 0.0, roll(own, 1, 0)) + jnp.where(row == FX - 1, 0.0, roll(own, -1, 0))
        left_over = fs[j] - operate(own, beside_x, us[j] + us[j + 2], rs[j], cx_col, cys[j], cz_row)
        if j in (1, 2):
            left_over = 3.0 * left_over
        total = left_over if total is None else total + left_over
    total = total * 0.125
    q[...] = total
    for out, edge, step, cut in ((low, 0, 1, slice(0, 8)), (high, FX - 1, -1, slice(24, 32))):
        out[0:8] = total[cut]
        next_row = edge + step
        picked = [us[j + 1][edge : edge + 1] for j in range(4)]
        out[8:16] = rows_of(picked + [us[j + 1][next_row : next_row + 1] for j in range(4)])
        middle = u[64:68, 0:MZ] if edge == 0 else u[68:72, MZ:FZ]
        pairs = [jnp.concatenate([middle[2 * i : 2 * i + 1], middle[2 * i + 1 : 2 * i + 2]], axis=1) for i in range(2)]
        coarse = jnp.concatenate([u[72:73, 0:MZ], u[72:73, 0:MZ]], axis=1)
        out[16:24] = rows_of([rs[j][edge : edge + 1] for j in range(4)] + pairs + [coarse])


def to_middle(px, py, q, u, below, above, left, right, force, rho, y_below, y_above, x_left, x_right, cx, sy, cx_mid, cyz_mid, lines, u_ext, f_ext, r_ext, cx_ext, cy_ext, r_mid, f_mid, v_out, told):
    columns = jnp.concatenate([x_left[16:24, 0:128], cx[...], x_right[16:24, 0:128]], axis=0)
    cx_ext[...] = columns
    told[0:16] = below[64:80]
    told[16:32] = above[64:80]
    told[32:40] = jnp.broadcast_to(right[22:23], (8, FZ))
    told[40:48] = jnp.broadcast_to(left[22:23], (8, FZ))
    us = [below[32:64], u[0:32], u[32:64], above[0:32]]
    rs = [y_below[32:64], rho[0], rho[1], y_above[32:64]]
    cross = []
    for side, row in ((left, 0), (right, FX - 1)):
        inward = outward = None
        for j in range(4):
            weight = 0.375 if j in (1, 2) else 0.125
            here = weight * rs[j][row : row + 1] * side[8 + j : 9 + j]
            there = weight * side[16 + j : 17 + j] * us[j][row : row + 1]
            inward = here if inward is None else inward + here
            outward = there if outward is None else outward + there
        at = FH + row
        beyond = at - 1 if row == 0 else at + 1
        cross.append((at, inward * columns[at : at + 1, 0:1]))
        cross.append((beyond, outward * columns[beyond : beyond + 1, 0:1]))
    total = jnp.concatenate([left[0:8], q[...], right[0:8]], axis=0)
    line = iota((FE, FZ), 0)
    for at, term in cross:
        total = total + jnp.where(line == at, term, 0.0)
    none = jnp.zeros((8, FZ), f32)
    u_ext[0] = jnp.concatenate([none, below[0:32], none], axis=0)
    u_ext[5] = jnp.concatenate([none, above[32:64], none], axis=0)
    for j in range(4):
        before = rows_at([(7, left[8 + j : 9 + j]), (6, left[12 + j : 13 + j])])
        after = rows_at([(0, right[8 + j : 9 + j]), (1, right[12 + j : 13 + j])])
        u_ext[j + 1] = jnp.concatenate([before, us[j], after], axis=0)
    for at in range(2):
        for k, own, out in ((0, force, f_ext), (8, rho, r_ext)):
            before = rows_at([(7, x_left[k + at : k + at + 1])])
            after = rows_at([(0, x_right[k + at : k + at + 1])])
            out[at + 1] = jnp.concatenate([before, own[at], after], axis=0)
    for side, at in ((y_below, 0), (y_above, 3)):
        f_ext[at] = jnp.concatenate([none, side[0:32], none], axis=0)
        r_ext[at] = jnp.concatenate([none, side[32:64], none], axis=0)
    cy_rows = [jnp.broadcast_to(sy[0:1, at : at + 1], (1, FZ)) for at in range(2)]
    cy_ext[...] = rows_of([y_below[64:65], cy_rows[0], cy_rows[1], y_above[64:65]])
    dense = []
    for side, first in ((left, 4), (right, 0)):
        rows = []
        for i in range(2):
            line = side[20 + i : 21 + i]
            rows.append((first + 2 * i, line[:, 0:MZ]))
            rows.append((first + 2 * i + 1, line[:, MZ:FZ]))
        dense.append(rows_at(rows))
    dense[1:1] = [u[64:72, 0:MZ], u[64:72, MZ:FZ]]
    r_mid[...] = roll(jnp.concatenate(dense, axis=0), MH - 8, 0)[0:ME]
    rhs = restrict_columns(restrict_rows(total))
    rhs = jnp.where(inside_middle(px), rhs, 0.0)
    f_mid[...] = rhs
    diag = diagonal(*middle_parts(r_mid, cx_mid, cyz_mid))
    v_out[...] = solve_z(rhs / diag, lines)


def middle_parts(r_mid, cx_mid, cyz_mid):
    return r_mid[...], cx_mid[:, 0:1], cyz_mid[1:2], cyz_mid[0:1]


def middle_scaled(px, py, v, below, above, f_mid, r_mid, cx_mid, cyz_mid, out):
    rho, cx, cy, cz = middle_parts(r_mid, cx_mid, cyz_mid)
    own = v[...]
    applied = operate(own, near_x(own), below[...] + above[...], rho, cx, cy, cz)
    scaled = (f_mid[...] - applied) / diagonal(rho, cx, cy, cz)
    part = roll(scaled, -MH, 0)[0:MX]
    for i in range(out.shape[0]):
        out[i] = part


def rows_for_x(px, py, lines, out):
    place, row_of_four = px % 4, px // 4
    total = MX * N_PX
    parts = []
    for i in range(8):
        base = MX * (4 * i + place)
        pieces = [
            dyn(lines, jnp.maximum(base - 8, 0), 8),
            dyn(lines, base, MX),
            dyn(lines, jnp.minimum(base + MX, total - 8), 8),
        ]
        rows = roll(jnp.concatenate(pieces, axis=0), MH - 8, 0)[0:ME]
        at = iota((ME, 256), 0) + base - MH
        first = 256 * (row_of_four // 4)
        parts.append(jnp.where((at >= first) & (at < first + 256), rows, 0.0))
    full = jnp.concatenate(parts, axis=0)
    held = None
    for i in range(4):
        cut = jnp.where(row_of_four % 4 == i, full[:, 64 * i : 64 * (i + 1)], 0.0)
        held = cut if held is None else held + cut
    out[...] = held


def spread_x(px, py, gathered, rows, out):
    solved = dot(rows[...], gathered[...])
    for i in range(8):
        out[i] = solved[ME * i : ME * (i + 1)]


def gain_x(px, py, v, parts, out):
    total = v[...]
    for i in range(8):
        total = total + parts[i]
    out[...] = total


def solve_x_block(px, py, gathered, lines, v, out):
    total = MX * N_PX
    pieces = []
    starts = (
        (jnp.maximum(MX * px - 8, 0), 8),
        (MX * px, MX),
        (jnp.minimum(MX * px + MX, total - 8), 8),
    )
    for start, size in starts:
        pieces.append(dyn(lines, start, size))
    full = dot(jnp.concatenate(pieces, axis=0), gathered[...])
    part = roll(full, MH - 8, 0)[0:ME]
    row = iota((ME, MZ), 0) + MX * px - MH
    first = 256 * (px // 16)
    held = (row >= first) & (row < first + 256)
    out[...] = jnp.where(held, v[...] + part, 0.0)


def mend(px, py, v, other, out):
    row = iota((ME, MZ), 0)
    theirs = other[...]
    up = jnp.where((row >= MH + MX) & (px == 15), roll(theirs, MX, 0), 0.0)
    down = jnp.where((row < MH) & (px == 16), roll(theirs, -MX, 0), 0.0)
    out[...] = v[...] + (up + down)


def block_mean(px, py, v, f_mid, r_mid, cx_mid, cyz_mid, told, column, out):
    rho, cx, cy, cz = middle_parts(r_mid, cx_mid, cyz_mid)
    own = v[...]
    applied = operate(own, near_x(own), 0.0, rho, cx, cy, cz)
    row = iota((ME, MZ), 0)
    kept = jnp.where((row >= MH) & (row < MH + MX), f_mid[...] - applied, 0.0)

    def mean(a):
        return jnp.sum(jnp.sum(a, axis=0, keepdims=True), axis=1, keepdims=True) * (1.0 / (MX * MZ))

    sent = column[...] * mean(kept)
    inner = roll(own, -MH, 0)[0:MX]
    for at in (0, 16):
        share = mean(told[at : at + 8, 0:MZ] * inner[0:8] + told[at : at + 8, MZ:FZ] * inner[8:16])
        sent = sent + told[at + 8 : at + 9, 0:MZ] * (share * told[at + 8 : at + 9, MZ : MZ + 1])
    for at, edge, inner_row, mine in ((32, MH + MX, MH + MX - 1, px == 15), (40, MH - 1, MH, px == 16)):
        line = r_mid[edge : edge + 1] * cx_mid[edge : edge + 1, 0:1] * v[inner_row : inner_row + 1]
        sent = sent + told[at : at + 1, 0:MZ] * jnp.where(mine, mean(line), 0.0)
    lane = iota((8, MZ), 1)
    at_x, at_y = lane % N_PX, lane // N_PX
    wide = jnp.broadcast_to(sent, (8, MZ))
    rows = []
    for dy in (-1, 0, 1):
        for dx in (-1, 0, 1):
            held = (at_x + dx >= 0) & (at_x + dx < N_PX) & (at_y + dy >= 0) & (at_y + dy < N_PY)
            rows.append(jnp.where(held, roll(wide, -(dy * N_PX + dx), 1), 0.0)[0:1])
    stacked = jnp.concatenate([rows_of(rows[0:8]), rows_of(rows[8:9])], axis=0)
    unit = jnp.where(iota((16, 128), 0) == iota((16, 128), 1), 1.0, 0.0).astype(bf16)
    high, middle, low = thirds(stacked)
    dims = ((0,), (0,))
    out[...] = product(high, unit, dims) + (product(middle, unit, dims) + product(low, unit, dims))


def second_half(px, py, parts, v, below, above, f_mid, r_mid, cx_mid, cyz_mid, lines, out):
    total = jnp.sum(parts[...], axis=0, keepdims=True)
    row = iota((ME, MZ), 0)

    def raised(plane, dy):
        at = [total[0:1, 3 * (dy + 1) + dx : 3 * (dy + 1) + dx + 1] for dx in range(3)]
        return plane + jnp.where(row < MH, at[0], jnp.where(row < MH + MX, at[1], at[2]))

    own = raised(v[...], 0)
    beside = raised(below[...], -1) + raised(above[...], 1)
    rho, cx, cy, cz = middle_parts(r_mid, cx_mid, cyz_mid)
    applied = operate(own, near_x(own), beside, rho, cx, cy, cz)
    out[...] = own + solve_z((f_mid[...] - applied) / diagonal(rho, cx, cy, cz), lines)


def to_fine(px, py, v, below, above, far_below, far_above, u_ext, f_ext, r_ext, cx_ext, cy_ext, cz, lines, out, slabs):
    rows = [raise_rows(p[...]) for p in (far_below, below, v, above, far_above)]
    columns = raise_columns(jnp.concatenate(rows, axis=0)) * 0.25
    raised = [columns[FE * i : FE * (i + 1)] for i in range(5)]
    inside = inside_fine(px)
    us = []
    for j in range(6):
        at = 1 + j // 2
        other = at - 1 if j % 2 == 0 else at + 1
        held = inside
        if j < 2:
            held = inside & (py > 0)
        if j > 3:
            held = inside & (py < N_PY - 1)
        us.append(u_ext[j] + jnp.where(held, 3.0 * raised[at] + raised[other], 0.0))
    cx_col = cx_ext[:, 0:1]
    cz_row = cz[...]
    parts = []
    for j in range(4):
        own = us[j + 1]
        cy = cy_ext[j : j + 1]
        applied = operate(own, near_x(own), us[j] + us[j + 2], r_ext[j], cx_col, cy, cz_row)
        parts.append((f_ext[j] - applied) / diagonal(r_ext[j], cx_col, cy, cz_row))
    solved = solve_z(jnp.concatenate(parts, axis=0), lines)
    news = [us[j + 1] + solved[FE * j : FE * (j + 1)] for j in range(4)]
    inner = slice(FH, FH + FX)
    for at in range(2):
        full = news[at + 1]
        own = full[inner]
        out[at] = own
        beside_y = news[at][inner] + news[at + 2][inner]
        rho = r_ext[at + 1, inner]
        cy = cy_ext[at + 1 : at + 2]
        applied = operate(own, near_x(full)[inner], beside_y, rho, cx_col[inner], cy, cz_row)
        to_slabs((f_ext[at + 1, inner] - applied) / diagonal(rho, cx_col[inner], cy, cz_row), slabs, at)


def finish(px, py, u, slabs, out):
    for at in range(2):
        out[:, at, :] = u[at] + from_slabs(slabs, at)


class Device:
    def run(self, stage, shapes, *args):
        def kernel(*refs):
            stage(lax.axis_index("px"), lax.axis_index("py"), *refs)

        whole = pl.BlockSpec(memory_space=pltpu.VMEM)
        outs = pl.pallas_call(
            kernel,
            out_shape=[jax.ShapeDtypeStruct(s, f32) for s in shapes],
            in_specs=[whole] * len(args),
            out_specs=[whole] * len(shapes),
            compiler_params=pltpu.CompilerParams(vmem_limit_bytes=24 * 1024 * 1024),
        )(*args)
        return outs if len(shapes) > 1 else outs[0]

    def local(self, fn, *args):
        return fn(*args)

    def block_of(self, lines):
        at = lax.axis_index("px") // 8
        return lax.dynamic_slice_in_dim(lines, at, 1, axis=0)

    def beside(self, axis, low, high, step=1):
        n = lax.axis_size(axis)
        up = [(i, i + step) for i in range(n - step)]
        down = [(j, i) for i, j in up]
        return lax.ppermute(high, axis, up), lax.ppermute(low, axis, down)

    def across(self, array):
        return lax.ppermute(array, "px", [(15, 16), (16, 15)])

    def everyone(self, rows):
        sent = rows.reshape(N_PX * N_PY, 1, 128)
        got = lax.all_to_all(sent, ("py", "px"), 0, 0, tiled=True)
        return got.reshape(N_PX * N_PY, 128)

    def solve_x(self, every, rows):
        fours = [list(range(k, k + 4)) for k in range(0, N_PX, 4)]
        eights = [list(range(k, N_PX, 4)) for k in range(4)]
        every = lax.all_to_all(every, "px", 0, 0, axis_index_groups=fours, tiled=True)
        parts = self.run(spread_x, [(8, ME, MZ)], every.reshape(4 * MX, MZ), rows)
        return lax.all_to_all(parts, "px", 0, 0, axis_index_groups=eights, tiled=True)

    def swap(self, axis, array, group):
        n = lax.axis_size(axis)
        groups = None
        if group < n:
            groups = [list(range(k, k + group)) for k in range(0, n, group)]
        return lax.all_to_all(array, axis, 0, 0, axis_index_groups=groups, tiled=True)


def cycle(d, forcing, inv_density, stretch_x, stretch_y, stretch_z, lines_z0, lines_x0, lines_z1, lines_x1, column):
    sxy = d.local(lambda a, b: jnp.concatenate([a, b])[None], stretch_x, stretch_y)
    sy = d.local(lambda a: a.reshape(1, 2), stretch_y)
    cz = d.local(lambda a: a.reshape(1, FZ), stretch_z)
    rows_x1 = d.local(lambda a: a.reshape(MX * N_PX, 256), lines_x1)
    slab, own, mid = (8, 2, FX, 128), (2, FX, FZ), (ME, MZ)

    force, rho, lower, upper, low, high, cx = d.run(
        start,
        [own, own, (72, FZ), (72, FZ), (24, FZ), (24, FZ), (FX, 128)],
        forcing, inv_density, sxy,
    )
    y_below, y_above = d.beside("py", lower, upper)
    x_left, x_right = d.beside("px", low, high)
    block = d.block_of(lines_x0)
    rows_x = d.run(rows_for_x, [(8 * ME, 64)], rows_x1)
    u = d.run(own_lines, [own], force, rho, cx, sy, cz, lines_z0)
    slabs = d.run(
        first_half, [slab],
        force, rho, cx, sy, cz, u, y_below, y_above, x_left, x_right, lines_z0,
    )
    slabs = d.swap("px", slabs, 8)
    cx_mid, cyz_mid, told = d.run(
        middle_statics,
        [(ME, 128), (8, MZ), (16, FZ)],
        rho, cx, sy, cz, x_left, x_right, column,
    )
    slabs = d.run(solve_x_fine, [slab], slabs, block)
    slabs = d.swap("px", slabs, 8)
    u = d.run(add_slabs, [(80, FZ)], u, slabs, told)
    below, above = d.beside("py", u, u)
    q, low, high = d.run(
        half_residual, [(FX, FZ), (24, FZ), (24, FZ)],
        u, below, above, force, rho, y_below, y_above, cx, sy, cz,
    )
    left, right = d.beside("px", low, high)
    u_ext, f_ext, r_ext, cx_ext, cy_ext, r_mid, f_mid, v, told = d.run(
        to_middle,
        [(6, FE, FZ), (4, FE, FZ), (4, FE, FZ), (FE, 128), (8, FZ), mid, mid, mid, (48, FZ)],
        q, u, below, above, left, right, force, rho, y_below, y_above, x_left, x_right,
        cx, sy, cx_mid, cyz_mid, lines_z1,
    )
    statics = (f_mid, r_mid, cx_mid, cyz_mid)

    below, above = d.beside("py", v, v)
    every = d.run(middle_scaled, [(16, MX, MZ)], v, below, above, *statics)
    every = d.swap("px", every, 16)
    every = d.local(lambda a: a.reshape(256, MZ), every)
    v = d.run(solve_x_block, [mid], every, rows_x1, v)
    other = d.across(v)
    sent = d.run(block_mean, [(N_PX * N_PY, 128)], v, *statics, told, column)
    parts = d.everyone(sent)
    v = d.run(mend, [mid], v, other)
    below, above = d.beside("py", v, v)
    v = d.run(second_half, [mid], parts, v, below, above, *statics, lines_z1)
    below, above = d.beside("py", v, v)
    parts = d.solve_x(d.run(middle_scaled, [(4, MX, MZ)], v, below, above, *statics), rows_x)
    v = d.run(gain_x, [mid], v, parts)

    below, above = d.beside("py", v, v)
    far_below, far_above = d.beside("py", v, v, 2)
    u, slabs = d.run(
        to_fine,
        [own, slab],
        v, below, above, far_below, far_above, u_ext, f_ext, r_ext, cx_ext, cy_ext, cz, lines_z0,
    )
    slabs = d.swap("px", slabs, 8)
    slabs = d.run(solve_x_fine, [slab], slabs, block)
    slabs = d.swap("px", slabs, 8)
    return d.run(finish, [(FX, 2, FZ)], u, slabs)


def solution(mesh):
    placed = (
        P("px", "py", None),
        P("px", "py", None),
        P("px"),
        P("py"),
        P(),
        P(),
        P(),
        P(),
        P(),
        P(("py", "px"), None),
    )

    def step(*args):
        return cycle(Device(), *args)

    return jax.shard_map(
        step, mesh=mesh, in_specs=placed, out_specs=P("px", "py", None), check_vma=False
    )
```
